32 devices in a mesh: dp: 8 (over z, x), tensor: 4 (over y, core).
Axes of the slice: x: 2, y: 2, z: 4, core: 2. Of those that a mesh axis runs over, the one named last changes fastest.
Arguments:
- inputs: bfloat16 [2, 4096, 768], P(None, 'dp'), may hold values from -6 to 6
- seg_parent: int32 [2, 8], replicated, may hold values from -1 to 7, as said below
- positions: int32 [2, 4096], P(None, 'dp'), may hold values from 0 to 2558, as said below
- w_query: bfloat16 [768, 768], P('dp', 'tensor'), may hold values from -0.21875 to 0.21875
- w_key: bfloat16 [768, 768], P('dp', 'tensor'), may hold values from -0.21875 to 0.21875
- w_value: bfloat16 [768, 768], P('dp', 'tensor'), may hold values from -0.21875 to 0.21875
- w_out: bfloat16 [768, 768], P('tensor', 'dp'), may hold values from -1.25 to 1.25
- w_gate: bfloat16 [768, 2048], P('dp', 'tensor'), may hold values from -0.21875 to 0.21875
- w_up: bfloat16 [768, 2048], P('dp', 'tensor'), may hold values from -0.21875 to 0.21875
- w_down: bfloat16 [2048, 768], P('tensor', 'dp'), may hold values from -0.125 to 0.125
- gain_attn: bfloat16 [768], P('dp'), may hold values from 0.25 to 1.75
- gain_mlp: bfloat16 [768], P('dp'), may hold values from 0.25 to 1.75
- out_grad: bfloat16 [2, 4096, 768], P(None, 'dp'), may hold values from -6 to 6
Outputs:
- layer_out: bfloat16 [2, 4096, 768], P(None, 'dp')
- input_grad: float32 [2, 4096, 768], P(None, 'dp')
- grad_query: float32 [768, 768], P('dp', 'tensor')
- grad_key: float32 [768, 768], P('dp', 'tensor')
- grad_value: float32 [768, 768], P('dp', 'tensor')
- grad_out: float32 [768, 768], P('tensor', 'dp')
- grad_gate: float32 [768, 2048], P('dp', 'tensor')
- grad_up: float32 [768, 2048], P('dp', 'tensor')
- grad_down: float32 [2048, 768], P('tensor', 'dp')
- grad_gain_attn: float32 [768], P('dp')
- grad_gain_mlp: float32 [768], P('dp')
The draws below stay inside these ranges and needn't reach their ends.
Inputs may be any that keep to these rules, and one draw needn't show every extreme that they name: `seg_parent`: segments are numbered by the rows that hold them. Each micro-batch holds 1 tree of 8 segments: a trunk of 2 segments in a row, 2 branch segments whose parent is the trunk's last segment, and two leaf segments after each branch. A path from any segment back to its root has at most 4 segments, and exactly 4 from every leaf; a segment is on the path of at most 8 segments, exactly that many for a root. The last segment of each micro-batch is a root. The tokens of a segment that stands j segments below its root take the positions c + j * 512 to c + j * 512 + 511 in order, where c is its tree's own offset from 0 to 511.
All inputs are finite; a program needn't handle non-finite values.
Results may differ from the reference program's by a relative error of at most 0.022.
Values may be sent and summed in bfloat16 or wider, within the bound.
No kernel may reach another device: no remote copies, remote signals or barrier semaphores. Data moves between devices by JAX's collectives and lax.ppermute only.
A program may use at most 384 MiB of HBM per device.

```python
from functools import partial
import jax
import jax.numpy as jnp
from jax import lax

D = 768
HEADS = 12
HEAD_DIM = 64
FF = 2048
SEG = 512
MICRO = 2
NSEG = 8
TREE_SEGS = 8
BRANCHES = 2
TRUNK = 2
PATH = 4
ROWS = 4096


def forest_tables(base_key):
    parents_all = []
    positions_all = []
    leaf_start = TRUNK + BRANCHES
    for batch_index in range(MICRO):
        order_key = jax.random.fold_in(base_key, batch_index)
        shuffled = jax.random.permutation(order_key, NSEG).astype(jnp.int32)
        slot_index = jnp.arange(NSEG, dtype=jnp.int32)
        root_place = jnp.sum(jnp.where(shuffled == 0, slot_index, 0)).astype(jnp.int32)
        last_value = shuffled[NSEG - 1]
        logical = jnp.where(slot_index == root_place, last_value, jnp.where(slot_index == NSEG - 1, 0, shuffled)).astype(jnp.int32)
        slot_of = jnp.argsort(logical, stable=True).astype(jnp.int32)
        tree_id = logical // TREE_SEGS
        role_id = logical % TREE_SEGS
        parent_role = jnp.where(role_id < TRUNK, role_id - 1, jnp.where(role_id < leaf_start, TRUNK - 1, TRUNK + (role_id - leaf_start) // 2))
        depth_of = jnp.where(role_id < TRUNK, role_id, jnp.where(role_id < leaf_start, TRUNK, TRUNK + 1))
        parent_slot = jnp.where(parent_role >= 0, slot_of[tree_id * TREE_SEGS + jnp.maximum(parent_role, 0)], -1)
        offsets_tree = jax.random.randint(jax.random.fold_in(order_key, 99), (NSEG // TREE_SEGS,), 0, SEG)
        if batch_index == 0:
            offsets_tree = offsets_tree.at[0].set(SEG - 1)
        if batch_index == 1:
            offsets_tree = offsets_tree.at[0].set(0)
        token_pos = (offsets_tree[tree_id] + depth_of * SEG)[:, None] + jnp.arange(SEG, dtype=jnp.int32)[None, :]
        parents_all.append(parent_slot.astype(jnp.int32))
        positions_all.append(token_pos.reshape(NSEG * SEG).astype(jnp.int32))
    return (jnp.stack(parents_all), jnp.stack(positions_all))


def draw_seg_parent(key, part):
    return forest_tables(jax.random.fold_in(key, 5))[0]


def draw_positions(key, part):
    return forest_tables(jax.random.fold_in(key, 5))[1]


def spiked(values, stream_key, source, target, parts, factor):
    def block_of(dim):
        return (jnp.arange(values.shape[dim]) // (values.shape[dim] // parts)).reshape((-1,) + (1,) * (values.ndim - 1 - dim))

    first = jax.random.permutation(stream_key, parts)[block_of(target)]
    far = (block_of(target) + parts // 2) % parts
    return jnp.where((block_of(source) == first) | (block_of(source) == far), factor * values, values)


def levels(own_key, dims, shards, smallest, largest):
    loudness = 1.0
    for axis_at, blocks in shards:
        steps = jax.random.uniform(jax.random.fold_in(jax.random.fold_in(own_key, 6), axis_at), (blocks,), jnp.float32, smallest / len(shards), largest / len(shards))
        loudness = loudness * jnp.repeat(jnp.exp(steps), dims[axis_at] // blocks).reshape((-1,) + (1,) * (len(dims) - 1 - axis_at))
    return loudness


def centred(key, extent, width, limit, pieces=(), held_as=jnp.bfloat16):
    array = width * jax.random.normal(key, extent, jnp.float32)
    if pieces:
        array = array * levels(key, extent, pieces, -0.22, 0.18)
    return jnp.clip(array, -limit, limit).astype(held_as)


def bell_draw_with(key, extent, width, most, split, heavy, kind=jnp.bfloat16):
    array = width * jax.random.normal(key, extent, jnp.float32)
    if split:
        array = array * levels(key, extent, split, -0.22, 0.18)
    return jnp.clip(spiked(array, jax.random.fold_in(key, 3), *heavy), -most, most).astype(kind)


def setup_inputs(seed: int = 0) -> dict:
    keys = jax.random.split(jax.random.key(seed), 14)
    return {
        "inputs": bell_draw_with(keys[0], (MICRO, ROWS, D), 1.0, 6.0, ((1, 8),), (1, 2, 8, 2.0)),
        "seg_parent": draw_seg_parent(jax.random.fold_in(keys[13], 71), 0),
        "positions": draw_positions(jax.random.fold_in(keys[13], 71), 0),
        "w_query": centred(keys[3], (D, D), D ** -0.5, 0.21875, ((0, 8), (1, 4))),
        "w_key": centred(keys[4], (D, D), D ** -0.5, 0.21875, ((0, 8), (1, 4))),
        "w_value": centred(keys[5], (D, D), D ** -0.5, 0.21875, ((0, 8), (1, 4))),
        "w_out": centred(keys[6], (D, D), (D // 32) ** -0.5, 1.25, ((0, 4), (1, 8))),
        "w_gate": centred(keys[7], (D, FF), D ** -0.5, 0.21875, ((0, 8), (1, 4))),
        "w_up": centred(keys[8], (D, FF), D ** -0.5, 0.21875, ((0, 8), (1, 4))),
        "w_down": centred(keys[9], (FF, D), FF ** -0.5, 0.125, ((0, 4), (1, 8))),
        "gain_attn": jnp.clip(1.0 + 0.15 * jax.random.normal(keys[10], (D,), jnp.float32), 0.25, 1.75).astype(jnp.bfloat16),
        "gain_mlp": jnp.clip(1.0 + 0.15 * jax.random.normal(keys[11], (D,), jnp.float32), 0.25, 1.75).astype(jnp.bfloat16),
        "out_grad": bell_draw_with(keys[12], (MICRO, ROWS, D), 1.0, 6.0, ((1, 8),), (1, 2, 8, 2.0)),
    }


EPSILON = 1e-06
BIG_NEG = -1e+30
HIGH = lax.Precision.HIGHEST

@jax.custom_vjp
def low(v):
    return lax.optimization_barrier(v.astype(jnp.bfloat16)).astype(jnp.float32)

@jax.custom_vjp
def low_back(v):
    return v

def low_keep(v):
    return (low(v), None)

def low_pass(kept, grad):
    return (grad,)

def back_keep(v):
    return (v, None)

def back_low(kept, grad):
    return (low(grad),)
low.defvjp(low_keep, low_pass)
low_back.defvjp(back_keep, back_low)

def dot_high(first_op, second_op):
    return jnp.dot(first_op, second_op, precision=HIGH, preferred_element_type=jnp.float32)

def rms_norm(values, gain_vec):
    inverse = lax.rsqrt(lax.optimization_barrier(jnp.mean(values * values, axis=-1, keepdims=True)) + EPSILON)
    return values * inverse * gain_vec

def rope_tables(token_pos):
    half_dim = HEAD_DIM // 2
    frequency = 10000.0 ** (-jnp.arange(half_dim, dtype=jnp.float32) * 2.0 / HEAD_DIM)
    angles = token_pos.astype(jnp.float32)[:, None] * frequency[None, :]
    return (jnp.cos(angles)[:, None, :], jnp.sin(angles)[:, None, :])

def rotate(tensor, cosine_table, sine_table):
    half_dim = tensor.shape[-1] // 2
    first_half = tensor[..., :half_dim]
    second_half = tensor[..., half_dim:]
    return jnp.concatenate([first_half * cosine_table - second_half * sine_table, first_half * sine_table + second_half * cosine_table], axis=-1)

def path_table(parent_row):
    current = jnp.arange(NSEG, dtype=jnp.int32)
    columns = [current]
    for depth_step in range(PATH - 1):
        current = jnp.where(current >= 0, parent_row[jnp.maximum(current, 0)], -1).astype(jnp.int32)
        columns.append(current)
    return jnp.stack(columns, axis=1)

def attend(queries, key_rows, value_rows, table):
    key_blocks = key_rows.reshape(NSEG, SEG, HEADS, HEAD_DIM)
    value_blocks = value_rows.reshape(NSEG, SEG, HEADS, HEAD_DIM)
    query_blocks = queries.reshape(NSEG, SEG, HEADS, HEAD_DIM)
    block_of = jnp.arange(PATH * SEG) // SEG
    offset_of = jnp.arange(PATH * SEG) % SEG
    causal = offset_of[None, :] <= jnp.arange(SEG)[:, None]
    scale = HEAD_DIM ** (-0.5)

    @jax.checkpoint
    def one_segment(packed):
        query_seg, chain_ids = packed
        valid_mask = chain_ids >= 0
        safe_ids = jnp.maximum(chain_ids, 0)
        chain_keys = key_blocks[safe_ids].reshape(PATH * SEG, HEADS, HEAD_DIM)
        chain_values = value_blocks[safe_ids].reshape(PATH * SEG, HEADS, HEAD_DIM)
        raw_scores = low_back(jnp.einsum('qhd,khd->hqk', query_seg, chain_keys, precision=HIGH))
        allowed = valid_mask[block_of][None, :] & ((block_of > 0)[None, :] | causal)
        scores = jnp.where(allowed[None], raw_scores * scale, BIG_NEG)
        prob_rows = low(jax.nn.softmax(scores, axis=-1))
        return jnp.einsum('hqk,khd->qhd', prob_rows, chain_values, precision=HIGH)
    outputs = lax.map(one_segment, (query_blocks, table))
    return outputs.reshape(NSEG * SEG, HEADS, HEAD_DIM)

def layer(parent_row, token_pos, tokens, w_query, w_key, w_value, w_out, w_gate, w_up, w_down, gain_attn, gain_mlp):
    row_count = tokens.shape[0]
    cosine_table, sine_table = rope_tables(token_pos)
    query_proj = low_back(dot_high(tokens, w_query)).reshape(row_count, HEADS, HEAD_DIM)
    queries = low(rotate(query_proj, cosine_table, sine_table))
    key_proj = low_back(dot_high(tokens, w_key)).reshape(row_count, HEADS, HEAD_DIM)
    key_rows = low(rotate(key_proj, cosine_table, sine_table))
    value_rows = low(low_back(dot_high(tokens, w_value))).reshape(row_count, HEADS, HEAD_DIM)
    attended = attend(queries, key_rows, value_rows, path_table(parent_row)).reshape(row_count, D)
    attended_low = low(low_back(attended))
    attn_out = low_back(dot_high(attended_low, w_out))
    hidden = rms_norm(tokens + attn_out, gain_attn)
    hidden_low = low(hidden)
    gate_proj = low_back(dot_high(hidden_low, w_gate))
    up_proj = low_back(dot_high(hidden_low, w_up))
    activation = low(jax.nn.silu(gate_proj) * up_proj)
    mlp_out = low_back(dot_high(activation, w_down))
    return rms_norm(hidden + mlp_out, gain_mlp)

def reference(inputs, seg_parent, positions, w_query, w_key, w_value, w_out, w_gate, w_up, w_down, gain_attn, gain_mlp, out_grad):
    params = tuple((weight_arg.astype(jnp.float32) for weight_arg in (w_query, w_key, w_value, w_out, w_gate, w_up, w_down, gain_attn, gain_mlp)))
    layer_outs = []
    input_grads = []
    totals = None
    for batch_index in range(MICRO):
        bound_layer = partial(layer, seg_parent[batch_index], positions[batch_index])
        result, pullback = jax.vjp(bound_layer, inputs[batch_index].astype(jnp.float32), *params)
        grads = pullback(out_grad[batch_index].astype(jnp.float32))
        layer_outs.append(result.astype(jnp.bfloat16))
        input_grads.append(grads[0])
        if totals is None:
            totals = grads[1:]
        else:
            totals = tuple((previous + current for previous, current in zip(totals, grads[1:])))
    return (jnp.stack(layer_outs), jnp.stack(input_grads), totals[0], totals[1], totals[2], totals[3], totals[4], totals[5], totals[6], totals[7], totals[8])
```

```python
import functools

import jax
import jax.numpy as jnp
from jax import lax
from jax.experimental import pallas as pl
from jax.experimental.pallas import tpu as pltpu
from jax.sharding import PartitionSpec as P

HEAD_DIM = 64
MICRO = 2
EPSILON = 1e-06
BIG_NEG = -1e30
FIRST_SLOT = 1
F32 = jnp.float32
BF16 = jnp.bfloat16


def dot(a, b, dims):
    return lax.dot_general(a, b, ((dims[0], dims[1]), ((), ())), preferred_element_type=F32)


def dot_nn(a, b):
    return dot(a, b, ((1,), (0,)))


def dot_nt(a, b):
    return dot(a, b, ((1,), (1,)))


def dot_tn(a, b):
    return dot(a, b, ((0,), (0,)))


def path_table(parent_row, seg_count, path_len):
    current = jnp.arange(seg_count, dtype=jnp.int32)
    columns = [current]
    for _ in range(path_len - 1):
        current = jnp.where(current >= 0, parent_row[jnp.maximum(current, 0)], -1)
        columns.append(current)
    return jnp.stack(columns, axis=1)


def causal_mask(tile, query_start):
    key_at = lax.broadcasted_iota(jnp.int32, tile, 0)
    query_at = lax.broadcasted_iota(jnp.int32, tile, 1) + query_start
    return key_at <= query_at


def forward_kernel(path_len, table, qkv, out_low, out_full, out_norm, top, total, acc):
    seg = pl.program_id(0)
    seg_len = qkv.shape[2]
    top[...] = jnp.full_like(top, BIG_NEG)
    total[...] = jnp.zeros_like(total)
    acc[...] = jnp.zeros_like(acc)
    query = qkv[seg, 0:HEAD_DIM, :]

    def block(source, own):
        key = qkv[source, HEAD_DIM : 2 * HEAD_DIM, :]
        value = qkv[source, 2 * HEAD_DIM : 3 * HEAD_DIM, :]
        scores = dot_tn(key, query)
        if own:
            scores = jnp.where(causal_mask((seg_len, seg_len), 0), scores, BIG_NEG)
        old = top[...]
        new = jnp.maximum(old, jnp.max(scores, axis=0, keepdims=True))
        shrink = jnp.exp(old - new)
        probs = jnp.exp(scores - new)
        total[...] = total[...] * shrink + jnp.sum(probs, axis=0, keepdims=True)
        acc[...] = acc[...] * shrink + dot_nn(value, probs.astype(BF16))
        top[...] = new

    block(seg, True)
    for step in range(1, path_len):
        source = table[seg * path_len + step]

        @pl.when(source >= 0)
        def _(source=source):
            block(source, False)

    result = acc[...] / total[...]
    out_low[0] = result.astype(BF16)
    out_full[0] = result
    out_norm[0] = top[...] + jnp.log(total[...])


def attention_forward(table, qkv, path_len):
    segs, rows, seg_len = qkv.shape
    whole = pl.BlockSpec((segs, rows, seg_len), lambda s, t: (0, 0, 0), pipeline_mode=pl.Buffered(1))
    tile = pl.BlockSpec((1, HEAD_DIM, seg_len), lambda s, t: (s, 0, 0))
    line = pl.BlockSpec((1, 1, seg_len), lambda s, t: (s, 0, 0))
    return pl.pallas_call(
        functools.partial(forward_kernel, path_len),
        out_shape=(
            jax.ShapeDtypeStruct((segs, HEAD_DIM, seg_len), BF16),
            jax.ShapeDtypeStruct((segs, HEAD_DIM, seg_len), F32),
            jax.ShapeDtypeStruct((segs, 1, seg_len), F32),
        ),
        grid_spec=pltpu.PrefetchScalarGridSpec(
            num_scalar_prefetch=1,
            grid=(segs,),
            in_specs=[whole],
            out_specs=[tile, tile, line],
            scratch_shapes=[
                pltpu.VMEM((1, seg_len), F32),
                pltpu.VMEM((1, seg_len), F32),
                pltpu.VMEM((HEAD_DIM, seg_len), F32),
            ],
        ),
        name="tree_attention_forward",
    )(table, qkv)


def backward_kernel(path_len, scale, table, qkv, grad_ref, full_ref, norm_ref, out, grad_key, grad_value, grad_query):
    seg = pl.program_id(0)
    segs, _, seg_len = qkv.shape

    @pl.when(seg == 0)
    def _():
        grad_key[...] = jnp.zeros_like(grad_key)
        grad_value[...] = jnp.zeros_like(grad_value)

    query = qkv[seg, 0:HEAD_DIM, :]
    grad = grad_ref[0]
    delta = jnp.sum(grad.astype(F32) * full_ref[0], axis=0, keepdims=True)
    norm = norm_ref[0]
    query_rows = query.T
    grad_rows = grad.T
    grad_query[...] = jnp.zeros_like(grad_query)

    def block(source, own):
        key = qkv[source, HEAD_DIM : 2 * HEAD_DIM, :]
        value = qkv[source, 2 * HEAD_DIM : 3 * HEAD_DIM, :]
        probs = jnp.exp(dot_tn(key, query) - norm)
        if own:
            probs = jnp.where(causal_mask((seg_len, seg_len), 0), probs, 0.0)
        score_grad = (probs * (dot_tn(value, grad) - delta)).astype(BF16)
        probs_low = probs.astype(BF16)
        grad_query[...] += dot_nn(key, score_grad)
        grad_key[source] += dot_nn(score_grad, query_rows)
        grad_value[source] += dot_nn(probs_low, grad_rows)

    block(seg, True)
    for step in range(1, path_len):
        source = table[seg * path_len + step]

        @pl.when(source >= 0)
        def _(source=source):
            block(source, False)

    out[seg, 0:HEAD_DIM, :] = (grad_query[...] * scale).astype(BF16)

    @pl.when(seg == segs - 1)
    def _():
        @pl.loop(0, segs)
        def _(at):
            out[at, HEAD_DIM : 2 * HEAD_DIM, :] = grad_key[at].T.astype(BF16)
            out[at, 2 * HEAD_DIM : 3 * HEAD_DIM, :] = grad_value[at].T.astype(BF16)


def attention_backward(table, qkv, grad, full, norm, path_len, scale):
    segs, rows, seg_len = qkv.shape
    whole = pl.BlockSpec((segs, rows, seg_len), lambda s, t: (0, 0, 0), pipeline_mode=pl.Buffered(1))
    tile = pl.BlockSpec((1, HEAD_DIM, seg_len), lambda s, t: (s, 0, 0))
    line = pl.BlockSpec((1, 1, seg_len), lambda s, t: (s, 0, 0))
    return pl.pallas_call(
        functools.partial(backward_kernel, path_len, scale),
        out_shape=jax.ShapeDtypeStruct((segs, rows, seg_len), BF16),
        grid_spec=pltpu.PrefetchScalarGridSpec(
            num_scalar_prefetch=1,
            grid=(segs,),
            in_specs=[whole, tile, tile, line],
            out_specs=pl.BlockSpec((segs, rows, seg_len), lambda s, t: (0, 0, 0)),
            scratch_shapes=[
                pltpu.VMEM((segs, seg_len, HEAD_DIM), F32),
                pltpu.VMEM((segs, seg_len, HEAD_DIM), F32),
                pltpu.VMEM((HEAD_DIM, seg_len), F32),
            ],
        ),
        name="tree_attention_backward",
    )(table, qkv, grad, full, norm)


def swap(value, bit):
    count = lax.axis_size("tensor")
    return lax.ppermute(value, "tensor", [(at, at ^ bit) for at in range(count)])


def exchange(blocks):
    return lax.all_to_all(blocks, "dp", 0, 0, tiled=True)


def rotary_tables(token_pos):
    half = HEAD_DIM // 2
    frequency = 10000.0 ** (-jnp.arange(half, dtype=F32) * 2.0 / HEAD_DIM)
    angles = frequency[:, None] * token_pos.astype(F32)[None, :]
    return jnp.cos(angles), jnp.sin(angles)


def rotate(tensor, cosine, sine):
    half = HEAD_DIM // 2
    first, second = tensor[..., :half, :], tensor[..., half:, :]
    return jnp.concatenate([first * cosine - second * sine, first * sine + second * cosine], axis=-2)


def rotate_back(tensor, cosine, sine):
    half = HEAD_DIM // 2
    first, second = tensor[..., :half, :], tensor[..., half:, :]
    return jnp.concatenate([first * cosine + second * sine, second * cosine - first * sine], axis=-2)


def rms_backward(grad_out, normed, inverse, gain):
    scaled = grad_out * gain
    return inverse * (scaled - normed * jnp.mean(scaled * normed, axis=-1, keepdims=True))


def body(
    inputs, seg_parent, positions, w_query, w_key, w_value, w_out, w_gate, w_up, w_down, gain_attn, gain_mlp, out_grad
):
    seg_count = lax.axis_size("dp")
    my_seg = lax.axis_index("dp")
    core = lax.axis_index("tensor") % 2
    tree_segs = min(16, seg_count)
    branch_count = tree_segs // 4
    path_len = tree_segs - 3 * branch_count + 2
    seg_len, width = inputs.shape[1:]
    scale = HEAD_DIM ** (-0.5)
    part_rows = w_query.shape[0]
    local_heads = w_query.shape[1] // HEAD_DIM
    hidden_units = w_gate.shape[1]
    head_width = local_heads * HEAD_DIM
    units = MICRO * local_heads
    last_slots = seg_count - FIRST_SLOT - units

    def by_head(weight):
        return weight.reshape(part_rows, local_heads, 1, HEAD_DIM)

    mine_qkv = jnp.concatenate([by_head(w_query), by_head(w_key), by_head(w_value)], axis=2)
    full_qkv = lax.all_gather(mine_qkv.reshape(part_rows, 3 * head_width), "dp", axis=0, tiled=True)
    packed = jnp.concatenate(
        [w_gate, w_up, w_down.T, w_out.T, gain_attn[:, None], gain_mlp[:, None]], axis=1
    )
    packed = lax.all_gather(packed, "dp", axis=0, tiled=True)
    full_gate = packed[:, :hidden_units]
    full_up = packed[:, hidden_units : 2 * hidden_units]
    full_down = packed[:, 2 * hidden_units : 3 * hidden_units]
    full_out = packed[:, 3 * hidden_units : 3 * hidden_units + head_width]
    gains = packed[:, 3 * hidden_units + head_width :].astype(F32).T
    gain_first, gain_second = gains[0:1], gains[1:2]

    tables = [rotary_tables(positions[b]) for b in range(MICRO)]
    blocks = []
    for b in range(MICRO):
        cosine, sine = tables[b]
        heads = dot(full_qkv, inputs[b], ((0,), (1,))).reshape(local_heads, 3, HEAD_DIM, seg_len)
        query = rotate(heads[:, 0], cosine, sine).astype(BF16) * jnp.asarray(scale, BF16)
        key = rotate(heads[:, 1], cosine, sine).astype(BF16)
        blocks.append(jnp.concatenate([query, key, heads[:, 2].astype(BF16)], axis=1))
    zeros = jnp.zeros((local_heads, 3 * HEAD_DIM, seg_len), BF16)

    def to_units(parts):
        shape = parts.shape[1:]
        return exchange(
            jnp.concatenate(
                [jnp.zeros((FIRST_SLOT, *shape), BF16), parts, jnp.zeros((last_slots, *shape), BF16)], axis=0
            )
        )

    def from_units(parts):
        return exchange(parts)[FIRST_SLOT : FIRST_SLOT + units]

    unit_qkv = to_units(jnp.concatenate(blocks, axis=0))
    unit_micro = (my_seg - FIRST_SLOT) // local_heads >= 1
    chain = jnp.where(
        unit_micro,
        path_table(seg_parent[1], seg_count, path_len),
        path_table(seg_parent[0], seg_count, path_len),
    ).reshape(-1)
    unit_low, unit_full, unit_norm = attention_forward(chain, unit_qkv, path_len)
    attended = from_units(unit_low).reshape(MICRO, head_width, seg_len)

    def pick(stack, at):
        return lax.dynamic_index_in_dim(stack, at, 0, keepdims=False)

    attended = jnp.stack([pick(attended, core), pick(attended, 1 - core)])
    tokens = pick(inputs, core).astype(F32)

    def reduce_mine(parts):
        both = parts[0] + swap(parts[1], 1)
        both = both.astype(F32)
        return both

    def tensor_sum(own, other):
        both = (own + swap(other.astype(BF16), 1).astype(F32)).astype(BF16)
        return both.astype(F32) + swap(both, 2).astype(F32)

    def with_other(own):
        return jnp.concatenate([own, swap(own, 1)], axis=0)

    attn_out = tensor_sum(dot(attended[0], full_out, ((0,), (1,))), dot(attended[1], full_out, ((0,), (1,))))
    resid_one = tokens + attn_out
    inverse_one = lax.rsqrt(jnp.mean(resid_one * resid_one, axis=-1, keepdims=True) + EPSILON)
    normed_one = resid_one * inverse_one
    hidden = normed_one * gain_first
    hidden_low = with_other(hidden.astype(BF16))
    gate = dot_nn(hidden_low, full_gate)
    up = dot_nn(hidden_low, full_up)
    sigmoid = jax.nn.sigmoid(gate)
    silu = gate * sigmoid
    activation = (silu * up).astype(BF16)
    mlp_part = dot_nt(activation, full_down)
    mlp = tensor_sum(mlp_part[:seg_len], mlp_part[seg_len:])
    resid_two = hidden + mlp
    inverse_two = lax.rsqrt(jnp.mean(resid_two * resid_two, axis=-1, keepdims=True) + EPSILON)
    normed_two = resid_two * inverse_two
    result = (normed_two * gain_second).astype(BF16)

    grad_result = pick(out_grad, core).astype(F32)
    gain_two_term = jnp.sum(grad_result * normed_two, axis=0)
    grad_resid_two = rms_backward(grad_result, normed_two, inverse_two, gain_second)
    grad_mlp_low = with_other(grad_resid_two.astype(BF16))
    grad_activation = dot_nn(grad_mlp_low, full_down)
    grad_gate_low = (grad_activation * up * sigmoid * (1.0 + gate * (1.0 - sigmoid))).astype(BF16)
    grad_up_low = (grad_activation * silu).astype(BF16)
    hidden_part = dot_nt(grad_gate_low, full_gate) + dot_nt(grad_up_low, full_up)
    grad_hidden = grad_resid_two + tensor_sum(hidden_part[:seg_len], hidden_part[seg_len:])
    gain_one_term = jnp.sum(grad_hidden * normed_one, axis=0)
    grad_resid_one = rms_backward(grad_hidden, normed_one, inverse_one, gain_first)
    grad_attn_low = with_other(grad_resid_one.astype(BF16))

    grad_own = dot(full_out, grad_attn_low[:seg_len], ((0,), (1,))).astype(BF16)
    grad_other = dot(full_out, grad_attn_low[seg_len:], ((0,), (1,))).astype(BF16)
    grad_pair = jnp.stack([grad_own, grad_other])
    grad_pair = jnp.concatenate([pick(grad_pair, core)[None], pick(grad_pair, 1 - core)[None]], axis=0)
    unit_grad = to_units(grad_pair.reshape(units, HEAD_DIM, seg_len))

    term_gate = dot_tn(hidden_low, grad_gate_low)
    term_up = dot_tn(hidden_low, grad_up_low)
    term_down = dot_tn(grad_mlp_low, activation)
    attended_rows = jnp.concatenate([attended[0], attended[1]], axis=1)
    term_out = dot(grad_attn_low, attended_rows, ((0,), (1,)))
    terms = jnp.concatenate(
        [
            term_gate.astype(BF16),
            term_up.astype(BF16),
            term_down.astype(BF16),
            term_out.astype(BF16),
            gain_one_term[:, None].astype(BF16),
            gain_two_term[:, None].astype(BF16),
        ],
        axis=1,
    )
    shard = lax.psum_scatter(terms, "dp", scatter_dimension=0, tiled=True).astype(F32)
    grad_gate = shard[:, :hidden_units]
    grad_up = shard[:, hidden_units : 2 * hidden_units]
    grad_down = shard[:, 2 * hidden_units : 3 * hidden_units].T
    grad_out = shard[:, 3 * hidden_units : 3 * hidden_units + head_width].T
    gain_terms = shard[:, 3 * hidden_units + head_width :].T
    gain_terms = gain_terms + swap(gain_terms, 1)

    unit_back = attention_backward(chain, unit_qkv, unit_grad, unit_full, unit_norm, path_len, scale)
    back = from_units(unit_back).astype(F32).reshape(MICRO, local_heads, 3, HEAD_DIM, seg_len)
    grads = []
    for b in range(MICRO):
        cosine, sine = tables[b]
        query = rotate_back(back[b, :, 0], cosine, sine)
        key = rotate_back(back[b, :, 1], cosine, sine)
        grads.append(
            jnp.concatenate([query, key, back[b, :, 2]], axis=1).reshape(3 * head_width, seg_len).astype(BF16)
        )
    stack = jnp.stack(grads)
    term_qkv = sum(dot(inputs[b], grads[b], ((0,), (1,))) for b in range(MICRO))
    term_qkv = term_qkv.reshape(seg_count, part_rows, 3 * head_width).astype(BF16)
    shard_qkv = jnp.sum(exchange(term_qkv).astype(F32), axis=0)
    shard_qkv = shard_qkv.reshape(part_rows, local_heads, 3, HEAD_DIM)

    input_mine = grad_resid_one + tensor_sum(
        dot(pick(stack, core), full_qkv, ((0,), (1,))), dot(pick(stack, 1 - core), full_qkv, ((0,), (1,)))
    )

    def both_micros(own):
        other = swap(own, 1)
        first = core == 0
        return jnp.stack([jnp.where(first, own, other), jnp.where(first, other, own)])

    return (
        both_micros(result),
        both_micros(input_mine),
        shard_qkv[:, :, 0].reshape(part_rows, head_width),
        shard_qkv[:, :, 1].reshape(part_rows, head_width),
        shard_qkv[:, :, 2].reshape(part_rows, head_width),
        grad_out,
        grad_gate,
        grad_up,
        grad_down,
        gain_terms[0],
        gain_terms[1],
    )


def solution(mesh):
    weight, turned = P("dp", "tensor"), P("tensor", "dp")
    rows, gain = P(None, "dp", None), P("dp")
    return jax.shard_map(
        body,
        mesh=mesh,
        in_specs=(
            rows, P(), P(None, "dp"), weight, weight, weight, turned, weight, weight, turned, gain, gain, rows,
        ),
        out_specs=(rows, rows, weight, weight, weight, turned, weight, weight, turned, gain, gain),
        check_vma=False,
    )
```

```python
import functools

import jax
import jax.numpy as jnp
from jax import lax
from jax.experimental import pallas as pl
from jax.experimental.pallas import tpu as pltpu
from jax.sharding import PartitionSpec as P

HEAD_DIM = 64
MICRO = 2
EPSILON = 1e-06
BIG_NEG = -1e30
FIRST_SLOT = 1
F32 = jnp.float32
BF16 = jnp.bfloat16


def dot(a, b, dims):
    return lax.dot_general(a, b, ((dims[0], dims[1]), ((), ())), preferred_element_type=F32)


def dot_nn(a, b):
    return dot(a, b, ((1,), (0,)))


def dot_nt(a, b):
    return dot(a, b, ((1,), (1,)))


def dot_tn(a, b):
    return dot(a, b, ((0,), (0,)))


def path_table(parent_row, seg_count, path_len):
    current = jnp.arange(seg_count, dtype=jnp.int32)
    columns = [current]
    for _ in range(path_len - 1):
        current = jnp.where(current >= 0, parent_row[jnp.maximum(current, 0)], -1)
        columns.append(current)
    return jnp.stack(columns, axis=1)


def causal_mask(tile, query_start):
    key_at = lax.broadcasted_iota(jnp.int32, tile, 0)
    query_at = lax.broadcasted_iota(jnp.int32, tile, 1) + query_start
    return key_at <= query_at


def forward_kernel(path_len, start, table, qkv, out_low, out_full, out_norm, top, total, acc):
    seg = pl.program_id(0)
    seg_len = qkv.shape[2]
    count = out_low.shape[2]
    top[...] = jnp.full_like(top, BIG_NEG)
    total[...] = jnp.zeros_like(total)
    acc[...] = jnp.zeros_like(acc)
    query = qkv[seg, 0:HEAD_DIM, start : start + count]

    def block(source, own):
        keys = start + count if own else seg_len
        key = qkv[source, HEAD_DIM : 2 * HEAD_DIM, 0:keys]
        value = qkv[source, 2 * HEAD_DIM : 3 * HEAD_DIM, 0:keys]
        scores = dot_tn(key, query)
        if own:
            scores = jnp.where(causal_mask((keys, count), start), scores, BIG_NEG)
        old = top[...]
        new = jnp.maximum(old, jnp.max(scores, axis=0, keepdims=True))
        shrink = jnp.exp(old - new)
        probs = jnp.exp(scores - new)
        total[...] = total[...] * shrink + jnp.sum(probs, axis=0, keepdims=True)
        acc[...] = acc[...] * shrink + dot_nn(value, probs.astype(BF16))
        top[...] = new

    block(seg, True)
    for step in range(1, path_len):
        source = table[seg * path_len + step]

        @pl.when(source >= 0)
        def _(source=source):
            block(source, False)

    result = acc[...] / total[...]
    out_low[0] = result.astype(BF16)
    out_full[0] = result
    out_norm[0] = top[...] + jnp.log(total[...])


def attention_forward(table, qkv, path_len, start, count):
    segs, rows, seg_len = qkv.shape
    places = segs * path_len
    whole = pl.BlockSpec((segs, rows, seg_len), lambda s, t: (0, 0, 0), pipeline_mode=pl.Buffered(1))
    placed = pl.BlockSpec((1, HEAD_DIM, count), lambda s, t: (t[places + s], 0, 0))
    tile = pl.BlockSpec((1, HEAD_DIM, count), lambda s, t: (s, 0, 0))
    line = pl.BlockSpec((1, 1, count), lambda s, t: (s, 0, 0))
    return pl.pallas_call(
        functools.partial(forward_kernel, path_len, start),
        out_shape=(
            jax.ShapeDtypeStruct((segs, HEAD_DIM, count), BF16),
            jax.ShapeDtypeStruct((segs, HEAD_DIM, count), F32),
            jax.ShapeDtypeStruct((segs, 1, count), F32),
        ),
        grid_spec=pltpu.PrefetchScalarGridSpec(
            num_scalar_prefetch=1,
            grid=(segs,),
            in_specs=[whole],
            out_specs=[placed, tile, line],
            scratch_shapes=[
                pltpu.VMEM((1, count), F32),
                pltpu.VMEM((1, count), F32),
                pltpu.VMEM((HEAD_DIM, count), F32),
            ],
        ),
        name="tree_attention_forward",
    )(table, qkv)


def backward_kernel(path_len, scale, table, qkv, *refs):
    chunks = (len(refs) - 4) // 3
    grad_refs, full_refs, norm_refs = refs[:chunks], refs[chunks : 2 * chunks], refs[2 * chunks : 3 * chunks]
    out, grad_key, grad_value, grad_query = refs[3 * chunks :]
    seg = pl.program_id(0)
    segs, _, seg_len = qkv.shape

    @pl.when(seg == 0)
    def _():
        grad_key[...] = jnp.zeros_like(grad_key)
        grad_value[...] = jnp.zeros_like(grad_value)

    query = qkv[seg, 0:HEAD_DIM, :]
    grad = jnp.concatenate([ref[0] for ref in grad_refs], axis=1)
    full = jnp.concatenate([ref[0] for ref in full_refs], axis=1)
    norm = jnp.concatenate([ref[0] for ref in norm_refs], axis=1)
    delta = jnp.sum(grad.astype(F32) * full, axis=0, keepdims=True)
    query_rows = query.T
    grad_rows = grad.T
    grad_query[...] = jnp.zeros_like(grad_query)

    def block(source, own):
        key = qkv[source, HEAD_DIM : 2 * HEAD_DIM, :]
        value = qkv[source, 2 * HEAD_DIM : 3 * HEAD_DIM, :]
        probs = jnp.exp(dot_tn(key, query) - norm)
        if own:
            probs = jnp.where(causal_mask((seg_len, seg_len), 0), probs, 0.0)
        score_grad = (probs * (dot_tn(value, grad) - delta)).astype(BF16)
        probs_low = probs.astype(BF16)
        grad_query[...] += dot_nn(key, score_grad)
        grad_key[source] += dot_nn(score_grad, query_rows)
        grad_value[source] += dot_nn(probs_low, grad_rows)

    block(seg, True)
    for step in range(1, path_len):
        source = table[seg * path_len + step]

        @pl.when(source >= 0)
        def _(source=source):
            block(source, False)

    out[seg, 0:HEAD_DIM, :] = (grad_query[...] * scale).astype(BF16)

    @pl.when(seg == segs - 1)
    def _():
        @pl.loop(0, segs)
        def _(at):
            out[at, HEAD_DIM : 2 * HEAD_DIM, :] = grad_key[at].T.astype(BF16)
            out[at, 2 * HEAD_DIM : 3 * HEAD_DIM, :] = grad_value[at].T.astype(BF16)


def attention_backward(table, qkv, grads, fulls, norms, path_len, scale):
    segs, rows, seg_len = qkv.shape
    places = segs * path_len
    whole = pl.BlockSpec((segs, rows, seg_len), lambda s, t: (0, 0, 0), pipeline_mode=pl.Buffered(1))
    placed = [pl.BlockSpec((1, HEAD_DIM, g.shape[2]), lambda s, t: (t[places + s], 0, 0)) for g in grads]
    tiles = [pl.BlockSpec((1, HEAD_DIM, g.shape[2]), lambda s, t: (s, 0, 0)) for g in grads]
    lines = [pl.BlockSpec((1, 1, g.shape[2]), lambda s, t: (s, 0, 0)) for g in grads]
    return pl.pallas_call(
        functools.partial(backward_kernel, path_len, scale),
        out_shape=jax.ShapeDtypeStruct((segs, rows, seg_len), BF16),
        grid_spec=pltpu.PrefetchScalarGridSpec(
            num_scalar_prefetch=1,
            grid=(segs,),
            in_specs=[whole, *placed, *tiles, *lines],
            out_specs=pl.BlockSpec((segs, rows, seg_len), lambda s, t: (0, 0, 0)),
            scratch_shapes=[
                pltpu.VMEM((segs, seg_len, HEAD_DIM), F32),
                pltpu.VMEM((segs, seg_len, HEAD_DIM), F32),
                pltpu.VMEM((HEAD_DIM, seg_len), F32),
            ],
        ),
        name="tree_attention_backward",
    )(table, qkv, *grads, *fulls, *norms)


def swap(value, bit):
    count = lax.axis_size("tensor")
    return lax.ppermute(value, "tensor", [(at, at ^ bit) for at in range(count)])


def send(value, bits, senders=None):
    senders = range(lax.axis_size("dp")) if senders is None else senders
    return lax.ppermute(value, "dp", [(at, at ^ bits) for at in senders])


def exchange(blocks):
    return lax.all_to_all(blocks, "dp", 0, 0, tiled=True)


def pick(stack, at):
    return lax.dynamic_index_in_dim(stack, at, 0, keepdims=False)


def small_group():
    return lax.axis_size("dp") in (4, 8)


def gather_parts(shard):
    if not small_group():
        return lax.all_gather(shard, "dp", axis=1, tiled=True)
    size, me = lax.axis_size("dp"), lax.axis_index("dp")
    groups, rows, columns = shard.shape
    near = [shard] + [send(shard, bits) for bits in range(2, size, 2)]
    far = send(jnp.stack(near), 1)
    full = jnp.zeros((groups, size * rows, columns), shard.dtype)
    for at in range(size // 2):
        full = lax.dynamic_update_slice(full, near[at], (0, (me ^ (2 * at)) * rows, 0))
        full = lax.dynamic_update_slice(full, far[at], (0, (me ^ (2 * at) ^ 1) * rows, 0))
    return full


def split_terms(terms):
    size, me = lax.axis_size("dp"), lax.axis_index("dp")
    groups, rows, columns = terms.shape
    sides = terms.reshape(groups, size // 2, 2, rows // size, columns)
    keep = lax.dynamic_index_in_dim(sides, me % 2, 2, keepdims=False)
    leave = lax.dynamic_index_in_dim(sides, 1 - me % 2, 2, keepdims=False)
    return keep, leave


def sum_parts(keep, leave):
    size, me = lax.axis_size("dp"), lax.axis_index("dp")
    half = (keep.astype(F32) + send(leave, 1).astype(F32)).astype(BF16)
    place = me // 2
    total = lax.dynamic_index_in_dim(half, place, 1, keepdims=False).astype(F32)
    for at in range(1, size // 2):
        part = lax.dynamic_index_in_dim(half, place ^ at, 1, keepdims=False)
        total = total + send(part, 2 * at).astype(F32)
    return total


def to_units_wide(parts):
    size, me = lax.axis_size("dp"), lax.axis_index("dp")
    units = parts.shape[0]
    if not small_group():
        return to_units(parts)
    last = FIRST_SLOT + units
    received = []
    for bits in range(size):
        part = pick(parts, jnp.clip((me ^ bits) - FIRST_SLOT, 0, units - 1))
        senders = [at for at in range(size) if FIRST_SLOT <= at ^ bits < last]
        received.append(send(part, bits, senders) if bits else part)
    return jnp.stack(received)


def from_units_wide(parts, units):
    size, me = lax.axis_size("dp"), lax.axis_index("dp")
    if not small_group():
        return list(from_units(parts, units))
    senders = range(FIRST_SLOT, FIRST_SLOT + units)
    received = [parts[0]] + [send(parts[bits], bits, senders) for bits in range(1, size)]
    received = jnp.stack(received)
    return [pick(received, (FIRST_SLOT + unit) ^ me) for unit in range(units)]


def to_units(parts):
    size, units, shape = lax.axis_size("dp"), parts.shape[0], parts.shape[1:]
    before = jnp.zeros((FIRST_SLOT, *shape), BF16)
    after = jnp.zeros((size - FIRST_SLOT - units, *shape), BF16)
    return exchange(jnp.concatenate([before, parts, after], axis=0))


def from_units(parts, units):
    return exchange(parts)[FIRST_SLOT : FIRST_SLOT + units]


def rotary_tables(token_pos):
    half = HEAD_DIM // 2
    frequency = 10000.0 ** (-jnp.arange(half, dtype=F32) * 2.0 / HEAD_DIM)
    angles = frequency[:, None] * token_pos.astype(F32)[None, :]
    return jnp.cos(angles), jnp.sin(angles)


def rotate(tensor, cosine, sine):
    half = HEAD_DIM // 2
    first, second = tensor[..., :half, :], tensor[..., half:, :]
    return jnp.concatenate([first * cosine - second * sine, first * sine + second * cosine], axis=-2)


def rotate_back(tensor, cosine, sine):
    half = HEAD_DIM // 2
    first, second = tensor[..., :half, :], tensor[..., half:, :]
    return jnp.concatenate([first * cosine + second * sine, second * cosine - first * sine], axis=-2)


def rms_backward(grad_out, normed, inverse, gain):
    scaled = grad_out * gain
    return inverse * (scaled - normed * jnp.mean(scaled * normed, axis=-1, keepdims=True))


def body(
    inputs, seg_parent, positions, w_query, w_key, w_value, w_out, w_gate, w_up, w_down, gain_attn, gain_mlp, out_grad
):
    seg_count = lax.axis_size("dp")
    my_seg = lax.axis_index("dp")
    core = lax.axis_index("tensor") % 2
    tree_segs = min(16, seg_count)
    branch_count = tree_segs // 4
    path_len = tree_segs - 3 * branch_count + 2
    seg_len, width = inputs.shape[1:]
    scale = HEAD_DIM ** (-0.5)
    part_rows = w_query.shape[0]
    local_heads = w_query.shape[1] // HEAD_DIM
    hidden_units = w_gate.shape[1]
    head_width = local_heads * HEAD_DIM
    units = MICRO * local_heads
    chunks = 2
    count = seg_len // chunks
    starts = [at * count for at in range(chunks)]

    def by_head(weight):
        return weight.reshape(part_rows, local_heads, 1, HEAD_DIM)

    mine_qkv = jnp.concatenate([by_head(w_query), by_head(w_key), by_head(w_value)], axis=2)
    full_qkv = gather_parts(mine_qkv.reshape(1, part_rows, 3 * head_width))[0]
    spare = jnp.zeros((part_rows, hidden_units - head_width - 2), BF16)
    last_group = jnp.concatenate([w_out.T, gain_attn[:, None], gain_mlp[:, None], spare], axis=1)
    full_gate, full_up, full_down, full_last = gather_parts(jnp.stack([w_gate, w_up, w_down.T, last_group]))
    full_out = full_last[:, :head_width]
    gains = full_last[:, head_width : head_width + 2].astype(F32).T
    gain_first, gain_second = gains[0:1], gains[1:2]

    tables = [rotary_tables(positions[b]) for b in range(MICRO)]
    blocks = []
    for b in range(MICRO):
        cosine, sine = tables[b]
        heads = dot(full_qkv, inputs[b], ((0,), (1,))).reshape(local_heads, 3, HEAD_DIM, seg_len)
        query = rotate(heads[:, 0], cosine, sine).astype(BF16) * jnp.asarray(scale, BF16)
        key = rotate(heads[:, 1], cosine, sine).astype(BF16)
        blocks.append(jnp.concatenate([query, key, heads[:, 2].astype(BF16)], axis=1))
    unit_qkv = to_units_wide(jnp.concatenate(blocks, axis=0))
    unit_micro = (my_seg - FIRST_SLOT) // local_heads >= 1
    chain = jnp.where(
        unit_micro,
        path_table(seg_parent[1], seg_count, path_len),
        path_table(seg_parent[0], seg_count, path_len),
    )
    place = jnp.arange(seg_count, dtype=jnp.int32)
    if small_group():
        place = place ^ my_seg
        chain = chain[place]
        chain = jnp.where(chain >= 0, chain ^ my_seg, -1)
    chain = jnp.concatenate([chain.reshape(-1), place])

    def tensor_sum(own, other):
        both = (own + swap(other.astype(BF16), 1).astype(F32)).astype(BF16)
        return both.astype(F32) + swap(both, 2).astype(F32)

    def with_other(own):
        return jnp.concatenate([own, swap(own, 1)], axis=0)

    unit_fulls, unit_norms, attended = [], [], []
    for start in starts:
        low, full, norm = attention_forward(chain, unit_qkv, path_len, start, count)
        unit_fulls.append(full)
        unit_norms.append(norm)
        attended.append(from_units(low, units).reshape(MICRO, head_width, count))

    tokens_all = pick(inputs, core)
    out_grad_all = pick(out_grad, core)
    hidden_lows, acts, mlp_lows, gate_lows, up_lows, attn_lows = [], [], [], [], [], []
    results, resid_ones, gain_ones, gain_twos, unit_grads, heads_by_rows = [], [], [], [], [], []
    for at, start in enumerate(starts):
        own_heads, other_heads = pick(attended[at], core), pick(attended[at], 1 - core)
        tokens = tokens_all[start : start + count].astype(F32)
        attn_out = tensor_sum(
            dot(own_heads, full_out, ((0,), (1,))), dot(other_heads, full_out, ((0,), (1,)))
        )
        heads_by_rows.append(jnp.concatenate([own_heads, other_heads], axis=1))
        resid_one = tokens + attn_out
        inverse_one = lax.rsqrt(jnp.mean(resid_one * resid_one, axis=-1, keepdims=True) + EPSILON)
        normed_one = resid_one * inverse_one
        hidden = normed_one * gain_first
        hidden_low = with_other(hidden.astype(BF16))
        gate = dot_nn(hidden_low, full_gate)
        up = dot_nn(hidden_low, full_up)
        sigmoid = jax.nn.sigmoid(gate)
        silu = gate * sigmoid
        activation = (silu * up).astype(BF16)
        mlp_part = dot_nt(activation, full_down)
        mlp = tensor_sum(mlp_part[:count], mlp_part[count:])
        resid_two = hidden + mlp
        inverse_two = lax.rsqrt(jnp.mean(resid_two * resid_two, axis=-1, keepdims=True) + EPSILON)
        normed_two = resid_two * inverse_two
        results.append((normed_two * gain_second).astype(BF16))

        grad_result = out_grad_all[start : start + count].astype(F32)
        gain_twos.append(jnp.sum(grad_result * normed_two, axis=0))
        grad_resid_two = rms_backward(grad_result, normed_two, inverse_two, gain_second)
        grad_mlp_low = with_other(grad_resid_two.astype(BF16))
        grad_activation = dot_nn(grad_mlp_low, full_down)
        grad_gate_low = (grad_activation * up * sigmoid * (1.0 + gate * (1.0 - sigmoid))).astype(BF16)
        grad_up_low = (grad_activation * silu).astype(BF16)
        hidden_part = dot_nt(grad_gate_low, full_gate) + dot_nt(grad_up_low, full_up)
        grad_hidden = grad_resid_two + tensor_sum(hidden_part[:count], hidden_part[count:])
        gain_ones.append(jnp.sum(grad_hidden * normed_one, axis=0))
        grad_resid_one = rms_backward(grad_hidden, normed_one, inverse_one, gain_first)
        grad_attn_low = with_other(grad_resid_one.astype(BF16))
        resid_ones.append(grad_resid_one)

        grad_own = dot(full_out, grad_attn_low[:count], ((0,), (1,))).astype(BF16)
        grad_other = dot(full_out, grad_attn_low[count:], ((0,), (1,))).astype(BF16)
        grad_pair = jnp.where(core == 0, jnp.stack([grad_own, grad_other]), jnp.stack([grad_other, grad_own]))
        unit_grads.append(to_units(grad_pair.reshape(units, HEAD_DIM, count)))
        hidden_lows.append(hidden_low)
        acts.append(activation)
        mlp_lows.append(grad_mlp_low)
        gate_lows.append(grad_gate_low)
        up_lows.append(grad_up_low)
        attn_lows.append(grad_attn_low)

    def over_rows(first, second, dims):
        return sum(dot(a, b, dims) for a, b in zip(first, second))

    heads_pad = [jnp.pad(rows, ((0, hidden_units - head_width), (0, 0))) for rows in heads_by_rows]
    term_last = over_rows(attn_lows, heads_pad, ((0,), (1,)))
    column = lax.broadcasted_iota(jnp.int32, term_last.shape, 1)
    term_last = jnp.where(column == head_width, sum(gain_ones)[:, None], term_last)
    term_last = jnp.where(column == head_width + 1, sum(gain_twos)[:, None], term_last)
    terms = jnp.stack(
        [
            over_rows(hidden_lows, gate_lows, ((0,), (0,))).astype(BF16),
            over_rows(hidden_lows, up_lows, ((0,), (0,))).astype(BF16),
            over_rows(mlp_lows, acts, ((0,), (0,))).astype(BF16),
            term_last.astype(BF16),
        ]
    )
    if small_group():
        keep, leave = split_terms(terms)
        keep, leave, unit_grads = lax.optimization_barrier((keep, leave, unit_grads))
        shard = sum_parts(keep, leave)
    else:
        shard = lax.psum_scatter(terms, "dp", scatter_dimension=1, tiled=True).astype(F32)
    grad_gate, grad_up, grad_down, grad_last = shard[0], shard[1], shard[2].T, shard[3]
    grad_out = grad_last[:, :head_width].T
    gain_terms = grad_last[:, head_width : head_width + 2].T
    gain_terms = gain_terms + swap(gain_terms, 1)

    unit_back = attention_backward(chain, unit_qkv, unit_grads, unit_fulls, unit_norms, path_len, scale)
    back = from_units_wide(unit_back, units)
    grads = []
    for b in range(MICRO):
        cosine, sine = tables[b]
        rows = []
        for head in range(local_heads):
            part = back[b * local_heads + head].astype(F32)
            rows.append(rotate_back(part[:HEAD_DIM], cosine, sine))
            rows.append(rotate_back(part[HEAD_DIM : 2 * HEAD_DIM], cosine, sine))
            rows.append(part[2 * HEAD_DIM :])
        grads.append(jnp.concatenate(rows, axis=0).astype(BF16))
    stack = jnp.stack(grads)
    term_qkv = sum(dot(inputs[b], grads[b], ((0,), (1,))) for b in range(MICRO)).astype(BF16)[None]
    if small_group():
        shard_qkv = sum_parts(*split_terms(term_qkv))
    else:
        shard_qkv = lax.psum_scatter(term_qkv, "dp", scatter_dimension=1, tiled=True).astype(F32)
    shard_qkv = shard_qkv.reshape(part_rows, local_heads, 3, HEAD_DIM)

    input_mine = jnp.concatenate(resid_ones, axis=0) + tensor_sum(
        dot(pick(stack, core), full_qkv, ((0,), (1,))), dot(pick(stack, 1 - core), full_qkv, ((0,), (1,)))
    )

    def both_micros(own):
        other = swap(own, 1)
        first = core == 0
        return jnp.stack([jnp.where(first, own, other), jnp.where(first, other, own)])

    return (
        both_micros(jnp.concatenate(results, axis=0)),
        both_micros(input_mine),
        shard_qkv[:, :, 0].reshape(part_rows, head_width),
        shard_qkv[:, :, 1].reshape(part_rows, head_width),
        shard_qkv[:, :, 2].reshape(part_rows, head_width),
        grad_out,
        grad_gate,
        grad_up,
        grad_down,
        gain_terms[0],
        gain_terms[1],
    )


def solution(mesh):
    weight, turned = P("dp", "tensor"), P("tensor", "dp")
    rows, gain = P(None, "dp", None), P("dp")
    return jax.shard_map(
        body,
        mesh=mesh,
        in_specs=(
            rows, P(), P(None, "dp"), weight, weight, weight, turned, weight, weight, turned, gain, gain, rows,
        ),
        out_specs=(rows, rows, weight, weight, weight, turned, weight, weight, turned, gain, gain),
        check_vma=False,
    )
```

```python
import functools

import jax
import jax.numpy as jnp
from jax import lax
from jax.experimental import pallas as pl
from jax.experimental.pallas import tpu as pltpu
from jax.sharding import PartitionSpec as P

HEAD_DIM = 64
MICRO = 2
EPSILON = 1e-06
BIG_NEG = -1e30
FIRST_SLOT = 1
F32 = jnp.float32
BF16 = jnp.bfloat16


def dot(a, b, dims):
    return lax.dot_general(a, b, ((dims[0], dims[1]), ((), ())), preferred_element_type=F32)


def dot_nn(a, b):
    return dot(a, b, ((1,), (0,)))


def dot_nt(a, b):
    return dot(a, b, ((1,), (1,)))


def dot_tn(a, b):
    return dot(a, b, ((0,), (0,)))


def path_table(parent_row, seg_count, path_len):
    current = jnp.arange(seg_count, dtype=jnp.int32)
    columns = [current]
    for _ in range(path_len - 1):
        current = jnp.where(current >= 0, parent_row[jnp.maximum(current, 0)], -1)
        columns.append(current)
    return jnp.stack(columns, axis=1)


def causal_mask(tile, query_start):
    key_at = lax.broadcasted_iota(jnp.int32, tile, 0)
    query_at = lax.broadcasted_iota(jnp.int32, tile, 1) + query_start
    return key_at <= query_at


def forward_kernel(path_len, table, qkv, out_low, out_full, out_norm, top, total, acc):
    seg = pl.program_id(0)
    seg_len = qkv.shape[2]
    top[...] = jnp.full_like(top, BIG_NEG)
    total[...] = jnp.zeros_like(total)
    acc[...] = jnp.zeros_like(acc)
    query = qkv[seg, 0:HEAD_DIM, :]

    def block(source, own):
        key = qkv[source, HEAD_DIM : 2 * HEAD_DIM, :]
        value = qkv[source, 2 * HEAD_DIM : 3 * HEAD_DIM, :]
        scores = dot_tn(key, query)
        if own:
            scores = jnp.where(causal_mask((seg_len, seg_len), 0), scores, BIG_NEG)
        old = top[...]
        new = jnp.maximum(old, jnp.max(scores, axis=0, keepdims=True))
        shrink = jnp.exp(old - new)
        probs = jnp.exp(scores - new)
        total[...] = total[...] * shrink + jnp.sum(probs, axis=0, keepdims=True)
        acc[...] = acc[...] * shrink + dot_nn(value, probs.astype(BF16))
        top[...] = new

    block(seg, True)
    for step in range(1, path_len):
        source = table[seg * path_len + step]

        @pl.when(source >= 0)
        def _(source=source):
            block(source, False)

    result = acc[...] / total[...]
    out_low[0] = result.astype(BF16)
    out_full[0] = result
    out_norm[0] = top[...] + jnp.log(total[...])


def attention_forward(table, qkv, path_len):
    segs, rows, seg_len = qkv.shape
    whole = pl.BlockSpec((segs, rows, seg_len), lambda s, t: (0, 0, 0), pipeline_mode=pl.Buffered(1))
    tile = pl.BlockSpec((1, HEAD_DIM, seg_len), lambda s, t: (s, 0, 0))
    line = pl.BlockSpec((1, 1, seg_len), lambda s, t: (s, 0, 0))
    return pl.pallas_call(
        functools.partial(forward_kernel, path_len),
        out_shape=(
            jax.ShapeDtypeStruct((segs, HEAD_DIM, seg_len), BF16),
            jax.ShapeDtypeStruct((segs, HEAD_DIM, seg_len), F32),
            jax.ShapeDtypeStruct((segs, 1, seg_len), F32),
        ),
        grid_spec=pltpu.PrefetchScalarGridSpec(
            num_scalar_prefetch=1,
            grid=(segs,),
            in_specs=[whole],
            out_specs=[tile, tile, line],
            scratch_shapes=[
                pltpu.VMEM((1, seg_len), F32),
                pltpu.VMEM((1, seg_len), F32),
                pltpu.VMEM((HEAD_DIM, seg_len), F32),
            ],
        ),
        name="tree_attention_forward",
    )(table, qkv)


def backward_kernel(path_len, scale, table, qkv, grad_ref, full_ref, norm_ref, out, grad_key, grad_value, grad_query):
    seg = pl.program_id(0)
    segs, _, seg_len = qkv.shape

    @pl.when(seg == 0)
    def _():
        grad_key[...] = jnp.zeros_like(grad_key)
        grad_value[...] = jnp.zeros_like(grad_value)

    query = qkv[seg, 0:HEAD_DIM, :]
    grad = grad_ref[0]
    delta = jnp.sum(grad.astype(F32) * full_ref[0], axis=0, keepdims=True)
    norm = norm_ref[0]
    query_rows = query.T
    grad_rows = grad.T
    grad_query[...] = jnp.zeros_like(grad_query)

    def block(source, own):
        key = qkv[source, HEAD_DIM : 2 * HEAD_DIM, :]
        value = qkv[source, 2 * HEAD_DIM : 3 * HEAD_DIM, :]
        probs = jnp.exp(dot_tn(key, query) - norm)
        if own:
            probs = jnp.where(causal_mask((seg_len, seg_len), 0), probs, 0.0)
        score_grad = (probs * (dot_tn(value, grad) - delta)).astype(BF16)
        probs_low = probs.astype(BF16)
        grad_query[...] += dot_nn(key, score_grad)
        grad_key[source] += dot_nn(score_grad, query_rows)
        grad_value[source] += dot_nn(probs_low, grad_rows)

    block(seg, True)
    for step in range(1, path_len):
        source = table[seg * path_len + step]

        @pl.when(source >= 0)
        def _(source=source):
            block(source, False)

    out[seg, 0:HEAD_DIM, :] = (grad_query[...] * scale).astype(BF16)

    @pl.when(seg == segs - 1)
    def _():
        @pl.loop(0, segs)
        def _(at):
            out[at, HEAD_DIM : 2 * HEAD_DIM, :] = grad_key[at].T.astype(BF16)
            out[at, 2 * HEAD_DIM : 3 * HEAD_DIM, :] = grad_value[at].T.astype(BF16)


def attention_backward(table, qkv, grad, full, norm, path_len, scale):
    segs, rows, seg_len = qkv.shape
    whole = pl.BlockSpec((segs, rows, seg_len), lambda s, t: (0, 0, 0), pipeline_mode=pl.Buffered(1))
    tile = pl.BlockSpec((1, HEAD_DIM, seg_len), lambda s, t: (s, 0, 0))
    line = pl.BlockSpec((1, 1, seg_len), lambda s, t: (s, 0, 0))
    return pl.pallas_call(
        functools.partial(backward_kernel, path_len, scale),
        out_shape=jax.ShapeDtypeStruct((segs, rows, seg_len), BF16),
        grid_spec=pltpu.PrefetchScalarGridSpec(
            num_scalar_prefetch=1,
            grid=(segs,),
            in_specs=[whole, tile, tile, line],
            out_specs=pl.BlockSpec((segs, rows, seg_len), lambda s, t: (0, 0, 0)),
            scratch_shapes=[
                pltpu.VMEM((segs, seg_len, HEAD_DIM), F32),
                pltpu.VMEM((segs, seg_len, HEAD_DIM), F32),
                pltpu.VMEM((HEAD_DIM, seg_len), F32),
            ],
        ),
        name="tree_attention_backward",
    )(table, qkv, grad, full, norm)


def swap(value, bit):
    count = lax.axis_size("tensor")
    return lax.ppermute(value, "tensor", [(at, at ^ bit) for at in range(count)])


def send(value, bits):
    return lax.ppermute(value, "dp", [(at, at ^ bits) for at in range(lax.axis_size("dp"))])


def exchange(blocks):
    return lax.all_to_all(blocks, "dp", 0, 0, tiled=True)


def exchange_far(blocks):
    size = lax.axis_size("dp")
    groups = [list(range(side, size, 2)) for side in range(2)]
    return lax.all_to_all(blocks, "dp", 0, 0, axis_index_groups=groups, tiled=True)


def rounded(value):
    return lax.reduce_precision(value, 8, 7)


def pick(stack, at):
    return lax.dynamic_index_in_dim(stack, at, 0, keepdims=False)


def small_group():
    return lax.axis_size("dp") in (4, 8)


def gather_near(shard):
    half = lax.axis_size("dp") // 2
    return exchange_far(jnp.broadcast_to(shard[None], (half, *shard.shape)))


def merge_sides(near, far):
    side = lax.axis_index("dp") % 2
    half, rows, columns = near.shape
    at = lax.broadcasted_iota(jnp.int32, (half, 2, rows, columns), 1)
    return jnp.where(at == side, near[:, None], far[:, None]).reshape(half * 2 * rows, columns)


def split_terms(terms):
    size, side = lax.axis_size("dp"), lax.axis_index("dp") % 2
    *groups, rows, columns = terms.shape
    sides = terms.reshape(*groups, size // 2, 2, rows // size, columns)
    axis = len(groups)
    parts = []
    for which in (side, 1 - side):
        part = lax.dynamic_index_in_dim(sides, which, axis + 1, keepdims=False)
        parts.append(jnp.moveaxis(part, axis, 0))
    return parts


def sum_over_dp(terms):
    if not small_group():
        return lax.psum_scatter(terms, "dp", scatter_dimension=terms.ndim - 2, tiled=True).astype(F32)
    keep, leave = split_terms(terms)
    half = (keep.astype(F32) + send(leave, 1).astype(F32)).astype(BF16)
    return jnp.sum(exchange_far(half).astype(F32), axis=0)


def to_units(parts):
    size, units, shape = lax.axis_size("dp"), parts.shape[0], parts.shape[1:]
    before = jnp.zeros((FIRST_SLOT, *shape), BF16)
    after = jnp.zeros((size - FIRST_SLOT - units, *shape), BF16)
    return exchange(jnp.concatenate([before, parts, after], axis=0))


def from_units(parts, units):
    return exchange(parts)[FIRST_SLOT : FIRST_SLOT + units]


def rotary_tables(token_pos):
    half = HEAD_DIM // 2
    frequency = 10000.0 ** (-jnp.arange(half, dtype=F32) * 2.0 / HEAD_DIM)
    angles = frequency[:, None] * token_pos.astype(F32)[None, :]
    return jnp.cos(angles), jnp.sin(angles)


def rotate(tensor, cosine, sine):
    half = HEAD_DIM // 2
    first, second = tensor[..., :half, :], tensor[..., half:, :]
    return jnp.concatenate([first * cosine - second * sine, first * sine + second * cosine], axis=-2)


def rotate_back(tensor, cosine, sine):
    half = HEAD_DIM // 2
    first, second = tensor[..., :half, :], tensor[..., half:, :]
    return jnp.concatenate([first * cosine + second * sine, second * cosine - first * sine], axis=-2)


def rms_backward(grad_out, normed, inverse, gain):
    scaled = grad_out * gain
    return inverse * (scaled - normed * jnp.mean(scaled * normed, axis=-1, keepdims=True))


def body(
    inputs, seg_parent, positions, w_query, w_key, w_value, w_out, w_gate, w_up, w_down, gain_attn, gain_mlp, out_grad
):
    seg_count = lax.axis_size("dp")
    my_seg = lax.axis_index("dp")
    core = lax.axis_index("tensor") % 2
    chip = lax.axis_index("tensor") // 2
    tree_segs = min(16, seg_count)
    branch_count = tree_segs // 4
    path_len = tree_segs - 3 * branch_count + 2
    seg_len, width = inputs.shape[1:]
    scale = HEAD_DIM ** (-0.5)
    part_rows = w_query.shape[0]
    local_heads = w_query.shape[1] // HEAD_DIM
    hidden_units = w_gate.shape[1]
    head_width = local_heads * HEAD_DIM
    units = MICRO * local_heads
    last_width = 256

    def by_head(weight):
        return weight.reshape(part_rows, local_heads, 1, HEAD_DIM)

    mine_qkv = jnp.concatenate([by_head(w_query), by_head(w_key), by_head(w_value)], axis=2)
    mine_qkv = mine_qkv.reshape(part_rows, 3 * head_width)
    spare = jnp.zeros((part_rows, last_width - head_width - 2), BF16)
    packed = jnp.concatenate(
        [w_gate, w_up, w_down.T, w_out.T, gain_attn[:, None], gain_mlp[:, None], spare], axis=1
    )
    if small_group():
        near_qkv = gather_near(mine_qkv)
        full_qkv = merge_sides(near_qkv, send(near_qkv, 1))
        near = gather_near(packed)
        far = send(near, 1)
        weights_own = merge_sides(near, far)
        weights_other = merge_sides(swap(near, 2), swap(far, 2))
    else:
        full_qkv = lax.all_gather(mine_qkv, "dp", axis=0, tiled=True)
        weights_own = lax.all_gather(packed, "dp", axis=0, tiled=True)
        weights_other = swap(weights_own, 2)

    tables = [rotary_tables(positions[b]) for b in range(MICRO)]
    blocks = []
    for b in range(MICRO):
        cosine, sine = tables[b]
        heads = dot(full_qkv, inputs[b], ((0,), (1,))).reshape(local_heads, 3, HEAD_DIM, seg_len)
        query = rotate(heads[:, 0], cosine, sine).astype(BF16) * jnp.asarray(scale, BF16)
        key = rotate(heads[:, 1], cosine, sine).astype(BF16)
        blocks.append(jnp.concatenate([query, key, heads[:, 2].astype(BF16)], axis=1))
    unit_qkv = to_units(jnp.concatenate(blocks, axis=0))
    unit_micro = (my_seg - FIRST_SLOT) // local_heads >= 1
    chain = jnp.where(
        unit_micro,
        path_table(seg_parent[1], seg_count, path_len),
        path_table(seg_parent[0], seg_count, path_len),
    ).reshape(-1)
    unit_low, unit_full, unit_norm = attention_forward(chain, unit_qkv, path_len)
    attended = from_units(unit_low, units).reshape(MICRO, head_width, seg_len)

    heads_own = pick(attended, chip)
    heads_other = swap(pick(attended, 1 - chip), 2)
    tokens = pick(inputs, chip).astype(F32)
    both_weights = (weights_own, weights_other)
    gates = [w[:, :hidden_units] for w in both_weights]
    ups = [w[:, hidden_units : 2 * hidden_units] for w in both_weights]
    downs = [w[:, 2 * hidden_units : 3 * hidden_units] for w in both_weights]
    lasts = [w[:, 3 * hidden_units :] for w in both_weights]
    outs = [w[:, :head_width] for w in lasts]
    gains = lasts[0][:, head_width : head_width + 2].astype(F32).T
    gain_first, gain_second = gains[0:1], gains[1:2]

    def core_sum(part):
        part = rounded(part)
        return part + swap(part.astype(BF16), 1).astype(F32)

    attn_out = core_sum(dot(heads_own, outs[0], ((0,), (1,))) + dot(heads_other, outs[1], ((0,), (1,))))
    resid_one = tokens + attn_out
    inverse_one = lax.rsqrt(jnp.mean(resid_one * resid_one, axis=-1, keepdims=True) + EPSILON)
    normed_one = resid_one * inverse_one
    hidden = normed_one * gain_first
    hidden_low = hidden.astype(BF16)
    gate = [dot_nn(hidden_low, w) for w in gates]
    up = [dot_nn(hidden_low, w) for w in ups]
    sigmoid = [jax.nn.sigmoid(g) for g in gate]
    silu = [g * s for g, s in zip(gate, sigmoid)]
    activation = [(s * u).astype(BF16) for s, u in zip(silu, up)]
    mlp = core_sum(dot_nt(activation[0], downs[0]) + dot_nt(activation[1], downs[1]))
    resid_two = hidden + mlp
    inverse_two = lax.rsqrt(jnp.mean(resid_two * resid_two, axis=-1, keepdims=True) + EPSILON)
    normed_two = resid_two * inverse_two
    result = (normed_two * gain_second).astype(BF16)

    grad_result = pick(out_grad, chip).astype(F32)
    gain_two_term = jnp.sum(grad_result * normed_two, axis=0)
    grad_resid_two = rms_backward(grad_result, normed_two, inverse_two, gain_second)
    grad_mlp_low = grad_resid_two.astype(BF16)
    grad_act = [dot_nn(grad_mlp_low, w) for w in downs]
    grad_gate_low = [
        (a * u * s * (1.0 + g * (1.0 - s))).astype(BF16) for a, u, s, g in zip(grad_act, up, sigmoid, gate)
    ]
    grad_up_low = [(a * s).astype(BF16) for a, s in zip(grad_act, silu)]
    hidden_part = (
        dot_nt(grad_gate_low[0], gates[0])
        + dot_nt(grad_up_low[0], ups[0])
        + dot_nt(grad_gate_low[1], gates[1])
        + dot_nt(grad_up_low[1], ups[1])
    )
    grad_hidden = grad_resid_two + core_sum(hidden_part)
    gain_one_term = jnp.sum(grad_hidden * normed_one, axis=0)
    grad_resid_one = rms_backward(grad_hidden, normed_one, inverse_one, gain_first)
    grad_attn_low = grad_resid_one.astype(BF16)

    grad_own = dot(outs[0], grad_attn_low, ((0,), (1,))).astype(BF16)
    grad_other = swap(dot(outs[1], grad_attn_low, ((0,), (1,))).astype(BF16), 2)
    first_chip = chip == 0
    grad_pair = jnp.stack(
        [jnp.where(first_chip, grad_own, grad_other), jnp.where(first_chip, grad_other, grad_own)]
    )
    unit_grad = to_units(grad_pair.reshape(units, HEAD_DIM, seg_len))

    own, other = [], []
    for at, terms in enumerate((own, other)):
        terms.append(dot_tn(hidden_low, grad_gate_low[at]))
        terms.append(dot_tn(hidden_low, grad_up_low[at]))
        terms.append(dot_tn(grad_mlp_low, activation[at]))
    heads_pad = [jnp.pad(rows, ((0, last_width - head_width), (0, 0))) for rows in (heads_own, heads_other)]
    term_last = []
    for rows in heads_pad:
        term = dot(grad_attn_low, rows, ((0,), (1,)))
        column = lax.broadcasted_iota(jnp.int32, term.shape, 1)
        term = jnp.where(column == head_width, gain_one_term[:, None], term)
        term_last.append(jnp.where(column == head_width + 1, gain_two_term[:, None], term))
    leave_mlp = jnp.stack([t.astype(BF16) for t in other])
    leave_last = term_last[1].astype(BF16)
    leave_mlp, leave_last, unit_grad = lax.optimization_barrier((leave_mlp, leave_last, unit_grad))
    terms_mlp = (jnp.stack(own) + swap(leave_mlp, 2).astype(F32)).astype(BF16)
    terms_last = (rounded(term_last[0]) + swap(leave_last, 2).astype(F32)).astype(BF16)
    shard = sum_over_dp(terms_mlp)
    shard_last = sum_over_dp(terms_last)
    gain_terms = shard_last[:, head_width : head_width + 2].T

    unit_back = attention_backward(chain, unit_qkv, unit_grad, unit_full, unit_norm, path_len, scale)
    back = from_units(unit_back, units).astype(F32).reshape(MICRO, local_heads, 3, HEAD_DIM, seg_len)
    grads = []
    for b in range(MICRO):
        cosine, sine = tables[b]
        query = rotate_back(back[b, :, 0], cosine, sine)
        key = rotate_back(back[b, :, 1], cosine, sine)
        grads.append(
            jnp.concatenate([query, key, back[b, :, 2]], axis=1).reshape(3 * head_width, seg_len).astype(BF16)
        )
    stack = jnp.stack(grads)
    term_qkv = sum(dot(inputs[b], grads[b], ((0,), (1,))) for b in range(MICRO)).astype(BF16)
    shard_qkv = sum_over_dp(term_qkv).reshape(part_rows, local_heads, 3, HEAD_DIM)

    part_own = dot(pick(stack, core), full_qkv, ((0,), (1,)))
    part_other = dot(pick(stack, 1 - core), full_qkv, ((0,), (1,)))
    part = part_own + swap(part_other.astype(BF16), 1).astype(F32) + jnp.where(core == chip, grad_resid_one, 0.0)
    part = rounded(part)
    input_mine = part + swap(part.astype(BF16), 2).astype(F32)

    def by_micro(own, other, first):
        return jnp.stack([jnp.where(first, own, other), jnp.where(first, other, own)])

    half = seg_len // 2
    result_half = swap(pick(result.reshape(2, half, width), core), 2)
    result_other = by_micro(result_half, swap(result_half, 1), core == 0).reshape(seg_len, width)
    return (
        by_micro(result, result_other, first_chip),
        by_micro(input_mine, swap(input_mine, 1), core == 0),
        shard_qkv[:, :, 0].reshape(part_rows, head_width),
        shard_qkv[:, :, 1].reshape(part_rows, head_width),
        shard_qkv[:, :, 2].reshape(part_rows, head_width),
        shard_last[:, :head_width].T,
        shard[0],
        shard[1],
        shard[2].T,
        gain_terms[0],
        gain_terms[1],
    )


def solution(mesh):
    weight, turned = P("dp", "tensor"), P("tensor", "dp")
    rows, gain = P(None, "dp", None), P("dp")
    return jax.shard_map(
        body,
        mesh=mesh,
        in_specs=(
            rows, P(), P(None, "dp"), weight, weight, weight, turned, weight, weight, turned, gain, gain, rows,
        ),
        out_specs=(rows, rows, weight, weight, weight, turned, weight, weight, turned, gain, gain),
        check_vma=False,
    )
```

```python
import functools

import jax
import jax.numpy as jnp
from jax import lax
from jax.experimental import pallas as pl
from jax.experimental.pallas import tpu as pltpu
from jax.sharding import PartitionSpec as P

HEAD_DIM = 64
MICRO = 2
EPSILON = 1e-06
BIG_NEG = -1e30
FIRST_SLOT = 1
F32 = jnp.float32
BF16 = jnp.bfloat16


def dot(a, b, dims):
    return lax.dot_general(a, b, ((dims[0], dims[1]), ((), ())), preferred_element_type=F32)


def dot_nn(a, b):
    return dot(a, b, ((1,), (0,)))


def dot_nt(a, b):
    return dot(a, b, ((1,), (1,)))


def dot_tn(a, b):
    return dot(a, b, ((0,), (0,)))


def path_table(parent_row, seg_count, path_len):
    current = jnp.arange(seg_count, dtype=jnp.int32)
    columns = [current]
    for _ in range(path_len - 1):
        current = jnp.where(current >= 0, parent_row[jnp.maximum(current, 0)], -1)
        columns.append(current)
    return jnp.stack(columns, axis=1)


def causal_mask(tile, query_start):
    key_at = lax.broadcasted_iota(jnp.int32, tile, 0)
    query_at = lax.broadcasted_iota(jnp.int32, tile, 1) + query_start
    return key_at <= query_at


def forward_kernel(path_len, table, qkv, out_low, out_full, out_norm, top, total, acc):
    seg = pl.program_id(0)
    seg_len = qkv.shape[2]
    top[...] = jnp.full_like(top, BIG_NEG)
    total[...] = jnp.zeros_like(total)
    acc[...] = jnp.zeros_like(acc)
    query = qkv[seg, 0:HEAD_DIM, :]

    def block(source, own):
        key = qkv[source, HEAD_DIM : 2 * HEAD_DIM, :]
        value = qkv[source, 2 * HEAD_DIM : 3 * HEAD_DIM, :]
        scores = dot_tn(key, query)
        if own:
            scores = jnp.where(causal_mask((seg_len, seg_len), 0), scores, BIG_NEG)
        old = top[...]
        new = jnp.maximum(old, jnp.max(scores, axis=0, keepdims=True))
        shrink = jnp.exp(old - new)
        probs = jnp.exp(scores - new)
        total[...] = total[...] * shrink + jnp.sum(probs, axis=0, keepdims=True)
        acc[...] = acc[...] * shrink + dot_nn(value, probs.astype(BF16))
        top[...] = new

    block(seg, True)
    for step in range(1, path_len):
        source = table[seg * path_len + step]

        @pl.when(source >= 0)
        def _(source=source):
            block(source, False)

    result = acc[...] / total[...]
    out_low[0] = result.astype(BF16)
    out_full[0] = result
    out_norm[0] = top[...] + jnp.log(total[...])


def attention_forward(table, qkv, path_len):
    segs, rows, seg_len = qkv.shape
    whole = pl.BlockSpec((segs, rows, seg_len), lambda s, t: (0, 0, 0), pipeline_mode=pl.Buffered(1))
    tile = pl.BlockSpec((1, HEAD_DIM, seg_len), lambda s, t: (s, 0, 0))
    line = pl.BlockSpec((1, 1, seg_len), lambda s, t: (s, 0, 0))
    return pl.pallas_call(
        functools.partial(forward_kernel, path_len),
        out_shape=(
            jax.ShapeDtypeStruct((segs, HEAD_DIM, seg_len), BF16),
            jax.ShapeDtypeStruct((segs, HEAD_DIM, seg_len), F32),
            jax.ShapeDtypeStruct((segs, 1, seg_len), F32),
        ),
        grid_spec=pltpu.PrefetchScalarGridSpec(
            num_scalar_prefetch=1,
            grid=(segs,),
            in_specs=[whole],
            out_specs=[tile, tile, line],
            scratch_shapes=[
                pltpu.VMEM((1, seg_len), F32),
                pltpu.VMEM((1, seg_len), F32),
                pltpu.VMEM((HEAD_DIM, seg_len), F32),
            ],
        ),
        name="tree_attention_forward",
    )(table, qkv)


def backward_kernel(path_len, scale, table, qkv, grad_ref, full_ref, norm_ref, out, grad_key, grad_value, grad_query):
    seg = pl.program_id(0)
    segs, _, seg_len = qkv.shape

    @pl.when(seg == 0)
    def _():
        grad_key[...] = jnp.zeros_like(grad_key)
        grad_value[...] = jnp.zeros_like(grad_value)

    query = qkv[seg, 0:HEAD_DIM, :]
    grad = grad_ref[0]
    delta = jnp.sum(grad.astype(F32) * full_ref[0], axis=0, keepdims=True)
    norm = norm_ref[0]
    query_rows = query.T
    grad_rows = grad.T
    grad_query[...] = jnp.zeros_like(grad_query)

    def block(source, own):
        key = qkv[source, HEAD_DIM : 2 * HEAD_DIM, :]
        value = qkv[source, 2 * HEAD_DIM : 3 * HEAD_DIM, :]
        probs = jnp.exp(dot_tn(key, query) - norm)
        if own:
            probs = jnp.where(causal_mask((seg_len, seg_len), 0), probs, 0.0)
        score_grad = (probs * (dot_tn(value, grad) - delta)).astype(BF16)
        probs_low = probs.astype(BF16)
        grad_query[...] += dot_nn(key, score_grad)
        grad_key[source] += dot_nn(score_grad, query_rows)
        grad_value[source] += dot_nn(probs_low, grad_rows)

    block(seg, True)
    for step in range(1, path_len):
        source = table[seg * path_len + step]

        @pl.when(source >= 0)
        def _(source=source):
            block(source, False)

    out[seg, 0:HEAD_DIM, :] = (grad_query[...] * scale).astype(BF16)

    @pl.when(seg == segs - 1)
    def _():
        @pl.loop(0, segs)
        def _(at):
            out[at, HEAD_DIM : 2 * HEAD_DIM, :] = grad_key[at].T.astype(BF16)
            out[at, 2 * HEAD_DIM : 3 * HEAD_DIM, :] = grad_value[at].T.astype(BF16)


def attention_backward(table, qkv, grad, full, norm, path_len, scale):
    segs, rows, seg_len = qkv.shape
    whole = pl.BlockSpec((segs, rows, seg_len), lambda s, t: (0, 0, 0), pipeline_mode=pl.Buffered(1))
    tile = pl.BlockSpec((1, HEAD_DIM, seg_len), lambda s, t: (s, 0, 0))
    line = pl.BlockSpec((1, 1, seg_len), lambda s, t: (s, 0, 0))
    return pl.pallas_call(
        functools.partial(backward_kernel, path_len, scale),
        out_shape=jax.ShapeDtypeStruct((segs, rows, seg_len), BF16),
        grid_spec=pltpu.PrefetchScalarGridSpec(
            num_scalar_prefetch=1,
            grid=(segs,),
            in_specs=[whole, tile, tile, line],
            out_specs=pl.BlockSpec((segs, rows, seg_len), lambda s, t: (0, 0, 0)),
            scratch_shapes=[
                pltpu.VMEM((segs, seg_len, HEAD_DIM), F32),
                pltpu.VMEM((segs, seg_len, HEAD_DIM), F32),
                pltpu.VMEM((HEAD_DIM, seg_len), F32),
            ],
        ),
        name="tree_attention_backward",
    )(table, qkv, grad, full, norm)


def swap(value, bit):
    count = lax.axis_size("tensor")
    return lax.ppermute(value, "tensor", [(at, at ^ bit) for at in range(count)])


def send(value, bits):
    return lax.ppermute(value, "dp", [(at, at ^ bits) for at in range(lax.axis_size("dp"))])


def exchange(blocks):
    return lax.all_to_all(blocks, "dp", 0, 0, tiled=True)


def exchange_far(blocks):
    size = lax.axis_size("dp")
    groups = [list(range(side, size, 2)) for side in range(2)]
    return lax.all_to_all(blocks, "dp", 0, 0, axis_index_groups=groups, tiled=True)


def rounded(value):
    return lax.reduce_precision(value, 8, 7)


def pick(stack, at):
    return lax.dynamic_index_in_dim(stack, at, 0, keepdims=False)


def small_group():
    return lax.axis_size("dp") in (4, 8)


def gather_far_sides(shard):
    return jnp.stack([shard] + [send(shard, bits) for bits in range(2, lax.axis_size("dp"), 2)])


def assemble_kernel(where, near, far, out):
    side = where[1]
    out[0, side] = near[0]
    out[0, 1 - side] = far[0]


def assemble(near, far):
    half, rows, columns = near.shape
    me = lax.axis_index("dp")
    where = jnp.stack([me // 2, me % 2]).astype(jnp.int32)
    block = pl.BlockSpec((1, rows, columns), lambda at, where: (at, 0, 0))
    full = pl.pallas_call(
        assemble_kernel,
        out_shape=jax.ShapeDtypeStruct((half, 2, rows, columns), near.dtype),
        grid_spec=pltpu.PrefetchScalarGridSpec(
            num_scalar_prefetch=1,
            grid=(half,),
            in_specs=[block, block],
            out_specs=pl.BlockSpec((1, 2, rows, columns), lambda at, where: (at ^ where[0], 0, 0, 0)),
        ),
        name="assemble",
    )(where, near, far)
    return full.reshape(half * 2 * rows, columns)


def after(values, *others):
    return lax.optimization_barrier((values, others))[0]


def gather_near(shard):
    half = lax.axis_size("dp") // 2
    return exchange_far(jnp.broadcast_to(shard[None], (half, *shard.shape)))


def merge_sides(near, far):
    side = lax.axis_index("dp") % 2
    half, rows, columns = near.shape
    at = lax.broadcasted_iota(jnp.int32, (half, 2, rows, columns), 1)
    return jnp.where(at == side, near[:, None], far[:, None]).reshape(half * 2 * rows, columns)


def split_terms(terms):
    size, side = lax.axis_size("dp"), lax.axis_index("dp") % 2
    *groups, rows, columns = terms.shape
    sides = terms.reshape(*groups, size // 2, 2, rows // size, columns)
    axis = len(groups)
    parts = []
    for which in (side, 1 - side):
        part = lax.dynamic_index_in_dim(sides, which, axis + 1, keepdims=False)
        parts.append(jnp.moveaxis(part, axis, 0))
    return parts


def sum_far_sides(half):
    place = lax.axis_index("dp") // 2
    total = pick(half, place).astype(F32)
    for at in range(1, half.shape[0]):
        total = total + send(pick(half, place ^ at), 2 * at).astype(F32)
    return total


def sum_sides(keep, leave):
    return (keep.astype(F32) + send(leave, 1).astype(F32)).astype(BF16)


def to_units(parts):
    size, units, shape = lax.axis_size("dp"), parts.shape[0], parts.shape[1:]
    before = jnp.zeros((FIRST_SLOT, *shape), BF16)
    after = jnp.zeros((size - FIRST_SLOT - units, *shape), BF16)
    return exchange(jnp.concatenate([before, parts, after], axis=0))


def from_units(parts, units):
    return exchange(parts)[FIRST_SLOT : FIRST_SLOT + units]


def rotary_tables(token_pos):
    half = HEAD_DIM // 2
    frequency = 10000.0 ** (-jnp.arange(half, dtype=F32) * 2.0 / HEAD_DIM)
    angles = frequency[:, None] * token_pos.astype(F32)[None, :]
    return jnp.cos(angles), jnp.sin(angles)


def rotate(tensor, cosine, sine):
    half = HEAD_DIM // 2
    first, second = tensor[..., :half, :], tensor[..., half:, :]
    return jnp.concatenate([first * cosine - second * sine, first * sine + second * cosine], axis=-2)


def rotate_back(tensor, cosine, sine):
    half = HEAD_DIM // 2
    first, second = tensor[..., :half, :], tensor[..., half:, :]
    return jnp.concatenate([first * cosine + second * sine, second * cosine - first * sine], axis=-2)


def rms_backward(grad_out, normed, inverse, gain):
    scaled = grad_out * gain
    return inverse * (scaled - normed * jnp.mean(scaled * normed, axis=-1, keepdims=True))


def body(
    inputs, seg_parent, positions, w_query, w_key, w_value, w_out, w_gate, w_up, w_down, gain_attn, gain_mlp, out_grad
):
    seg_count = lax.axis_size("dp")
    my_seg = lax.axis_index("dp")
    core = lax.axis_index("tensor") % 2
    chip = lax.axis_index("tensor") // 2
    tree_segs = min(16, seg_count)
    branch_count = tree_segs // 4
    path_len = tree_segs - 3 * branch_count + 2
    seg_len, width = inputs.shape[1:]
    scale = HEAD_DIM ** (-0.5)
    part_rows = w_query.shape[0]
    local_heads = w_query.shape[1] // HEAD_DIM
    hidden_units = w_gate.shape[1]
    head_width = local_heads * HEAD_DIM
    units = MICRO * local_heads
    last_width = 256

    def by_head(weight):
        return weight.reshape(part_rows, local_heads, 1, HEAD_DIM)

    mine_qkv = jnp.concatenate([by_head(w_query), by_head(w_key), by_head(w_value)], axis=2)
    mine_qkv = mine_qkv.reshape(part_rows, 3 * head_width)
    spare = jnp.zeros((part_rows, last_width - head_width - 2), BF16)
    packed = jnp.concatenate(
        [w_gate, w_up, w_down.T, w_out.T, gain_attn[:, None], gain_mlp[:, None], spare], axis=1
    )
    small = small_group()
    if small:
        near_qkv = gather_far_sides(mine_qkv)
        full_qkv = assemble(near_qkv, send(near_qkv, 1))
        near = gather_near(packed)
    else:
        full_qkv = lax.all_gather(mine_qkv, "dp", axis=0, tiled=True)

    tables = [rotary_tables(positions[b]) for b in range(MICRO)]
    blocks = []
    for b in range(MICRO):
        cosine, sine = tables[b]
        heads = dot(full_qkv, inputs[b], ((0,), (1,))).reshape(local_heads, 3, HEAD_DIM, seg_len)
        query = rotate(heads[:, 0], cosine, sine).astype(BF16) * jnp.asarray(scale, BF16)
        key = rotate(heads[:, 1], cosine, sine).astype(BF16)
        blocks.append(jnp.concatenate([query, key, heads[:, 2].astype(BF16)], axis=1))
    blocks = jnp.concatenate(blocks, axis=0)
    unit_qkv = to_units(blocks)
    if small:
        near = after(near, blocks)
        far = send(near, 1)
        near_other = swap(near, 2)
        far = after(far, unit_qkv)
        unit_qkv = after(unit_qkv, far)
        far_other = swap(far, 2)
        weights_own = merge_sides(near, far)
    unit_micro = (my_seg - FIRST_SLOT) // local_heads >= 1
    chain = jnp.where(
        unit_micro,
        path_table(seg_parent[1], seg_count, path_len),
        path_table(seg_parent[0], seg_count, path_len),
    ).reshape(-1)
    unit_low, unit_full, unit_norm = attention_forward(chain, unit_qkv, path_len)
    attended = from_units(unit_low, units).reshape(MICRO, head_width, seg_len)

    if small:
        weights_other = merge_sides(near_other, far_other)
    else:
        weights_own = lax.all_gather(packed, "dp", axis=0, tiled=True)
        weights_other = swap(weights_own, 2)
    heads_own = pick(attended, chip)
    heads_other = swap(pick(attended, 1 - chip), 2)
    tokens = pick(inputs, chip).astype(F32)
    both_weights = (weights_own, weights_other)
    gates = [w[:, :hidden_units] for w in both_weights]
    ups = [w[:, hidden_units : 2 * hidden_units] for w in both_weights]
    downs = [w[:, 2 * hidden_units : 3 * hidden_units] for w in both_weights]
    lasts = [w[:, 3 * hidden_units :] for w in both_weights]
    outs = [w[:, :head_width] for w in lasts]
    gains = lasts[0][:, head_width : head_width + 2].astype(F32).T
    gain_first, gain_second = gains[0:1], gains[1:2]

    def core_sum(part):
        part = rounded(part)
        return part + swap(part.astype(BF16), 1).astype(F32)

    attn_out = core_sum(dot(heads_own, outs[0], ((0,), (1,))) + dot(heads_other, outs[1], ((0,), (1,))))
    resid_one = tokens + attn_out
    inverse_one = lax.rsqrt(jnp.mean(resid_one * resid_one, axis=-1, keepdims=True) + EPSILON)
    normed_one = resid_one * inverse_one
    hidden = normed_one * gain_first
    hidden_low = hidden.astype(BF16)
    gate = [dot_nn(hidden_low, w) for w in gates]
    up = [dot_nn(hidden_low, w) for w in ups]
    sigmoid = [jax.nn.sigmoid(g) for g in gate]
    silu = [g * s for g, s in zip(gate, sigmoid)]
    activation = [(s * u).astype(BF16) for s, u in zip(silu, up)]
    mlp = core_sum(dot_nt(activation[0], downs[0]) + dot_nt(activation[1], downs[1]))
    resid_two = hidden + mlp
    inverse_two = lax.rsqrt(jnp.mean(resid_two * resid_two, axis=-1, keepdims=True) + EPSILON)
    normed_two = resid_two * inverse_two
    result = (normed_two * gain_second).astype(BF16)

    grad_result = pick(out_grad, chip).astype(F32)
    gain_two_term = jnp.sum(grad_result * normed_two, axis=0)
    grad_resid_two = rms_backward(grad_result, normed_two, inverse_two, gain_second)
    grad_mlp_low = grad_resid_two.astype(BF16)
    grad_act = [dot_nn(grad_mlp_low, w) for w in downs]
    grad_gate_low = [
        (a * u * s * (1.0 + g * (1.0 - s))).astype(BF16) for a, u, s, g in zip(grad_act, up, sigmoid, gate)
    ]
    grad_up_low = [(a * s).astype(BF16) for a, s in zip(grad_act, silu)]
    hidden_part = (
        dot_nt(grad_gate_low[0], gates[0])
        + dot_nt(grad_up_low[0], ups[0])
        + dot_nt(grad_gate_low[1], gates[1])
        + dot_nt(grad_up_low[1], ups[1])
    )
    grad_hidden = grad_resid_two + core_sum(hidden_part)
    gain_one_term = jnp.sum(grad_hidden * normed_one, axis=0)
    grad_resid_one = rms_backward(grad_hidden, normed_one, inverse_one, gain_first)
    grad_attn_low = grad_resid_one.astype(BF16)

    grad_own = dot(outs[0], grad_attn_low, ((0,), (1,))).astype(BF16)
    grad_other = swap(dot(outs[1], grad_attn_low, ((0,), (1,))).astype(BF16), 2)
    first_chip = chip == 0
    grad_pair = jnp.stack(
        [jnp.where(first_chip, grad_own, grad_other), jnp.where(first_chip, grad_other, grad_own)]
    )
    unit_grad = to_units(grad_pair.reshape(units, HEAD_DIM, seg_len))

    down = [dot_tn(grad_mlp_low, a) for a in activation]
    wide = [
        jnp.concatenate([dot_tn(hidden_low, g).astype(BF16), dot_tn(hidden_low, u).astype(BF16)], axis=1)
        for g, u in zip(grad_gate_low, grad_up_low)
    ]
    heads_pad = [jnp.pad(rows, ((0, last_width - head_width), (0, 0))) for rows in (heads_own, heads_other)]
    term_last = []
    for rows in heads_pad:
        term = dot(grad_attn_low, rows, ((0,), (1,)))
        column = lax.broadcasted_iota(jnp.int32, term.shape, 1)
        term = jnp.where(column == head_width, gain_one_term[:, None], term)
        term_last.append(jnp.where(column == head_width + 1, gain_two_term[:, None], term).astype(BF16))
    leave_terms = jnp.concatenate([wide[1], down[1].astype(BF16), term_last[1]], axis=1)
    keep_terms = jnp.concatenate([wide[0], down[0].astype(BF16), term_last[0]], axis=1)
    got_terms = swap(after(leave_terms, grad_other), 2)

    unit_grad = after(unit_grad, leave_terms)
    unit_back = attention_backward(chain, unit_qkv, unit_grad, unit_full, unit_norm, path_len, scale)
    back = from_units(unit_back, units)
    sum_terms = (keep_terms.astype(F32) + got_terms.astype(F32)).astype(BF16)
    if small:
        half_terms = sum_sides(*split_terms(after(sum_terms, unit_back)))
        half_terms, back = lax.optimization_barrier((half_terms, back))
        shard = sum_far_sides(half_terms)
    else:
        shard = lax.psum_scatter(sum_terms, "dp", scatter_dimension=0, tiled=True).astype(F32)
    shard_last = shard[:, 3 * hidden_units :]
    gain_terms = shard_last[:, head_width : head_width + 2].T
    back = back.astype(F32).reshape(MICRO, local_heads, 3, HEAD_DIM, seg_len)
    grads = []
    for b in range(MICRO):
        cosine, sine = tables[b]
        query = rotate_back(back[b, :, 0], cosine, sine)
        key = rotate_back(back[b, :, 1], cosine, sine)
        grads.append(
            jnp.concatenate([query, key, back[b, :, 2]], axis=1).reshape(3 * head_width, seg_len).astype(BF16)
        )
    stack = jnp.stack(grads)
    term_qkv = sum(dot(inputs[b], grads[b], ((0,), (1,))) for b in range(MICRO)).astype(BF16)
    if small:
        keep, leave = split_terms(term_qkv)
        shard_qkv = sum_far_sides(sum_sides(keep, leave))
    else:
        shard_qkv = lax.psum_scatter(term_qkv, "dp", scatter_dimension=0, tiled=True).astype(F32)
    shard_qkv = shard_qkv.reshape(part_rows, local_heads, 3, HEAD_DIM)

    part_own = dot(pick(stack, core), full_qkv, ((0,), (1,)))
    part_other = dot(pick(stack, 1 - core), full_qkv, ((0,), (1,)))
    part = part_own + swap(part_other.astype(BF16), 1).astype(F32) + jnp.where(core == chip, grad_resid_one, 0.0)
    part = rounded(part)
    input_mine = part + swap(part.astype(BF16), 2).astype(F32)

    def by_micro(own, other, first):
        return jnp.stack([jnp.where(first, own, other), jnp.where(first, other, own)])

    half = seg_len // 2
    result_half = swap(pick(result.reshape(2, half, width), core), 2)
    result_other = by_micro(result_half, swap(result_half, 1), core == 0).reshape(seg_len, width)
    return (
        by_micro(result, result_other, first_chip),
        by_micro(input_mine, swap(input_mine, 1), core == 0),
        shard_qkv[:, :, 0].reshape(part_rows, head_width),
        shard_qkv[:, :, 1].reshape(part_rows, head_width),
        shard_qkv[:, :, 2].reshape(part_rows, head_width),
        shard_last[:, :head_width].T,
        shard[:, :hidden_units],
        shard[:, hidden_units : 2 * hidden_units],
        shard[:, 2 * hidden_units : 3 * hidden_units].T,
        gain_terms[0],
        gain_terms[1],
    )


def solution(mesh):
    weight, turned = P("dp", "tensor"), P("tensor", "dp")
    rows, gain = P(None, "dp", None), P("dp")
    return jax.shard_map(
        body,
        mesh=mesh,
        in_specs=(
            rows, P(), P(None, "dp"), weight, weight, weight, turned, weight, weight, turned, gain, gain, rows,
        ),
        out_specs=(rows, rows, weight, weight, weight, turned, weight, weight, turned, gain, gain),
        check_vma=False,
    )
```

```python
import functools

import jax
import jax.numpy as jnp
from jax import lax
from jax.experimental import pallas as pl
from jax.experimental.pallas import tpu as pltpu
from jax.sharding import PartitionSpec as P

HEAD_DIM = 64
MICRO = 2
EPSILON = 1e-06
BIG_NEG = -1e30
FIRST_SLOT = 1
F32 = jnp.float32
BF16 = jnp.bfloat16


def dot(a, b, dims):
    return lax.dot_general(a, b, ((dims[0], dims[1]), ((), ())), preferred_element_type=F32)


def dot_nn(a, b):
    return dot(a, b, ((1,), (0,)))


def dot_nt(a, b):
    return dot(a, b, ((1,), (1,)))


def dot_tn(a, b):
    return dot(a, b, ((0,), (0,)))


def path_table(parent_row, seg_count, path_len):
    current = jnp.arange(seg_count, dtype=jnp.int32)
    columns = [current]
    for _ in range(path_len - 1):
        current = jnp.where(current >= 0, parent_row[jnp.maximum(current, 0)], -1)
        columns.append(current)
    return jnp.stack(columns, axis=1)


def causal_mask(tile):
    return lax.broadcasted_iota(jnp.int32, tile, 0) <= lax.broadcasted_iota(jnp.int32, tile, 1)


def for_path_length(table, seg, path_len, run):
    length = jnp.int32(1)
    for step in range(1, path_len):
        length = length + jnp.where(table[seg * path_len + step] >= 0, 1, 0)
    for steps in range(1, path_len + 1):

        @pl.when(length == steps)
        def _(steps=steps):
            run([seg] + [table[seg * path_len + step] for step in range(1, steps)])


def forward_kernel(path_len, sources, table, *refs):
    parts, (out_low, out_full, out_norm, *scratch) = refs[:sources], refs[sources:]
    qkv = scratch[0] if scratch else parts[0]
    seg = pl.program_id(0)
    seg_len = qkv.shape[2]
    if scratch:

        @pl.when(seg == 0)
        def _():
            for at, part in enumerate(parts):
                qkv[at] = part[0]

    def run(path):
        query = qkv[seg, 0:HEAD_DIM, :]
        scores = [dot_tn(qkv[source, HEAD_DIM : 2 * HEAD_DIM, :], query) for source in path]
        scores[0] = jnp.where(causal_mask((seg_len, seg_len)), scores[0], BIG_NEG)
        top = functools.reduce(jnp.maximum, [jnp.max(s, axis=0, keepdims=True) for s in scores])
        total, acc = 0.0, 0.0
        for source, score in zip(path, scores):
            probs = jnp.exp(score - top)
            total = total + jnp.sum(probs, axis=0, keepdims=True)
            acc = acc + dot_nn(qkv[source, 2 * HEAD_DIM : 3 * HEAD_DIM, :], probs.astype(BF16))
        result = acc * (1.0 / total)
        out_low[0] = result.astype(BF16)
        out_full[0] = result
        out_norm[0] = top + jnp.log(total)

    for_path_length(table, seg, path_len, run)


def part_specs(parts):
    return [pl.BlockSpec(p.shape, lambda s, t: (0, 0, 0), pipeline_mode=pl.Buffered(1)) for p in parts]


def attention_forward(table, parts, path_len):
    rows, seg_len = parts[0].shape[1:]
    segs = sum(p.shape[0] for p in parts)
    placed = pl.BlockSpec((1, HEAD_DIM, seg_len), lambda s, t: (s, 0, 0))
    tile = pl.BlockSpec((1, HEAD_DIM, seg_len), lambda s, t: (s, 0, 0))
    line = pl.BlockSpec((1, 1, seg_len), lambda s, t: (s, 0, 0))
    scratch = [pltpu.VMEM((segs, rows, seg_len), BF16)] if len(parts) > 1 else []
    return pl.pallas_call(
        functools.partial(forward_kernel, path_len, len(parts)),
        out_shape=(
            jax.ShapeDtypeStruct((segs, HEAD_DIM, seg_len), BF16),
            jax.ShapeDtypeStruct((segs, HEAD_DIM, seg_len), F32),
            jax.ShapeDtypeStruct((segs, 1, seg_len), F32),
        ),
        grid_spec=pltpu.PrefetchScalarGridSpec(
            num_scalar_prefetch=1,
            grid=(segs,),
            in_specs=part_specs(parts),
            out_specs=[placed, tile, line],
            scratch_shapes=scratch,
        ),
        name="tree_attention_forward",
    )(table, *parts)


def backward_kernel(path_len, scale, sources, table, *refs):
    parts, (grad_ref, full_ref, norm_ref) = refs[:sources], refs[sources : sources + 3]
    outs = refs[sources + 3 : 2 * sources + 3]
    grad_query, grad_key, grad_value, *scratch = refs[2 * sources + 3 :]
    qkv = scratch[0] if scratch else parts[0]
    seg = pl.program_id(0)
    segs, _, seg_len = qkv.shape

    @pl.when(seg == 0)
    def _():
        grad_key[...] = jnp.zeros_like(grad_key)
        grad_value[...] = jnp.zeros_like(grad_value)
        if scratch:
            for at, part in enumerate(parts):
                qkv[at] = part[0]

    def run(path):
        query = qkv[seg, 0:HEAD_DIM, :]
        grad = grad_ref[0]
        delta = jnp.sum(grad.astype(F32) * full_ref[0], axis=0, keepdims=True)
        norm = norm_ref[0]
        total = 0.0
        for step, source in enumerate(path):
            key = qkv[source, HEAD_DIM : 2 * HEAD_DIM, :]
            value = qkv[source, 2 * HEAD_DIM : 3 * HEAD_DIM, :]
            probs = jnp.exp(dot_tn(key, query) - norm)
            if step == 0:
                probs = jnp.where(causal_mask((seg_len, seg_len)), probs, 0.0)
            score_grad = (probs * (dot_tn(value, grad) - delta)).astype(BF16)
            total = total + dot_nn(key, score_grad)
            grad_key[source] += dot_nt(query, score_grad)
            grad_value[source] += dot_nt(grad, probs.astype(BF16))
        grad_query[seg] = (total * scale).astype(BF16)

    for_path_length(table, seg, path_len, run)

    @pl.when(seg == segs - 1)
    def _():
        at = 0
        for out in outs:
            rows = slice(at, at + out.shape[0])
            out[:, 0:HEAD_DIM, :] = grad_query[rows]
            out[:, HEAD_DIM : 2 * HEAD_DIM, :] = grad_key[rows].astype(BF16)
            out[:, 2 * HEAD_DIM : 3 * HEAD_DIM, :] = grad_value[rows].astype(BF16)
            at += out.shape[0]


def attention_backward(table, parts, grad, full, norm, path_len, scale):
    rows, seg_len = parts[0].shape[1:]
    segs = sum(p.shape[0] for p in parts)
    placed = pl.BlockSpec((1, HEAD_DIM, seg_len), lambda s, t: (s, 0, 0))
    tile = pl.BlockSpec((1, HEAD_DIM, seg_len), lambda s, t: (s, 0, 0))
    line = pl.BlockSpec((1, 1, seg_len), lambda s, t: (s, 0, 0))
    scratch = [
        pltpu.VMEM((segs, HEAD_DIM, seg_len), BF16),
        pltpu.VMEM((segs, HEAD_DIM, seg_len), F32),
        pltpu.VMEM((segs, HEAD_DIM, seg_len), F32),
    ]
    if len(parts) > 1:
        scratch.append(pltpu.VMEM((segs, rows, seg_len), BF16))
    return pl.pallas_call(
        functools.partial(backward_kernel, path_len, scale, len(parts)),
        out_shape=[jax.ShapeDtypeStruct(p.shape, BF16) for p in parts],
        grid_spec=pltpu.PrefetchScalarGridSpec(
            num_scalar_prefetch=1,
            grid=(segs,),
            in_specs=[*part_specs(parts), placed, tile, line],
            out_specs=part_specs(parts),
            scratch_shapes=scratch,
        ),
        name="tree_attention_backward",
    )(table, *parts, grad, full, norm)


def rotary_tables(token_pos):
    half = HEAD_DIM // 2
    frequency = 10000.0 ** (-jnp.arange(half, dtype=F32) * 2.0 / HEAD_DIM)
    angles = frequency[:, None] * token_pos.astype(F32)[None, :]
    return jnp.cos(angles), jnp.sin(angles)


def rotate(tensor, cosine, sine):
    half = HEAD_DIM // 2
    first, second = tensor[..., :half, :], tensor[..., half:, :]
    return jnp.concatenate([first * cosine - second * sine, first * sine + second * cosine], axis=-2)


def rotate_back(tensor, cosine, sine):
    half = HEAD_DIM // 2
    first, second = tensor[..., :half, :], tensor[..., half:, :]
    return jnp.concatenate([first * cosine + second * sine, second * cosine - first * sine], axis=-2)


def whole_call(kernel, where, operands, outs, scratch, name):
    def spec(shape):
        return pl.BlockSpec(shape, lambda at, where: (0,) * len(shape), pipeline_mode=pl.Buffered(1))

    return pl.pallas_call(
        kernel,
        out_shape=[jax.ShapeDtypeStruct(shape, kind) for shape, kind in outs],
        grid_spec=pltpu.PrefetchScalarGridSpec(
            num_scalar_prefetch=1,
            grid=(1,),
            in_specs=[spec(operand.shape) for operand in operands],
            out_specs=[spec(shape) for shape, _ in outs],
            scratch_shapes=scratch,
        ),
        name=name,
    )(where, *operands)


def store_sides(side, term, keep, leave):
    rows = keep.shape[1]
    for at in range(2 * keep.shape[0]):
        part = term[at * rows : (at + 1) * rows].astype(BF16)

        @pl.when(side == at % 2)
        def _(at=at, part=part):
            keep[at // 2] = part

        @pl.when(side != at % 2)
        def _(at=at, part=part):
            leave[at // 2] = part


def merge_kernel(where, own, got, keep, leave):
    store_sides(where[0] % 2, own[...].astype(F32) + got[...].astype(F32), keep, leave)


def merge_terms(where, own, got):
    rows, columns = own.shape
    size = lax.axis_size("dp")
    side = ((size // 2, rows // size, columns), BF16)
    return whole_call(merge_kernel, where, [own, got], [side, side], [], "merge_terms")


def tail_kernel(heads, where, blocks, tokens, weights, cosine, sine, resid, keep, leave, own, other, grads):
    core, chip = where[1], where[2]
    total = 0.0
    for batch in range(MICRO):
        for head in range(heads):
            block = blocks[FIRST_SLOT + batch * heads + head]
            start = 3 * HEAD_DIM * head
            query = rotate_back(block[0:HEAD_DIM].astype(F32), cosine[batch], sine[batch])
            key = rotate_back(block[HEAD_DIM : 2 * HEAD_DIM].astype(F32), cosine[batch], sine[batch])
            grads[batch, start : start + HEAD_DIM] = query.astype(BF16)
            grads[batch, start + HEAD_DIM : start + 2 * HEAD_DIM] = key.astype(BF16)
            grads[batch, start + 2 * HEAD_DIM : start + 3 * HEAD_DIM] = block[2 * HEAD_DIM :]
        total = total + dot_nt(tokens[batch].T, grads[batch])
    store_sides(where[0] % 2, total, keep, leave)
    own[...] = dot_nt(grads[core].T, weights[...]) + jnp.where(core == chip, 1.0, 0.0) * resid[...]
    other[...] = dot_nt(grads[1 - core].T, weights[...]).astype(BF16)


def swap(value, bit):
    count = lax.axis_size("tensor")
    return lax.ppermute(value, "tensor", [(at, at ^ bit) for at in range(count)])


def send(value, bits):
    return lax.ppermute(value, "dp", [(at, at ^ bits) for at in range(lax.axis_size("dp"))])


def exchange(blocks):
    return lax.all_to_all(blocks, "dp", 0, 0, tiled=True)


def exchange_far(blocks):
    size = lax.axis_size("dp")
    groups = [list(range(side, size, 2)) for side in range(2)]
    return lax.all_to_all(blocks, "dp", 0, 0, axis_index_groups=groups, tiled=True)


def rounded(value):
    return lax.reduce_precision(value, 8, 7)


def pick(stack, at):
    return lax.dynamic_index_in_dim(stack, at, 0, keepdims=False)


def small_group():
    return lax.axis_size("dp") in (4, 8)


def gather_far_sides(shard):
    return jnp.stack([shard] + [send(shard, bits) for bits in range(2, lax.axis_size("dp"), 2)])


def assemble_kernel(where, near, far, out):
    side = where[1]
    out[0, side] = near[0]
    out[0, 1 - side] = far[0]


def assemble(near, far):
    half, rows, columns = near.shape
    me = lax.axis_index("dp")
    where = jnp.stack([me // 2, me % 2]).astype(jnp.int32)
    block = pl.BlockSpec((1, rows, columns), lambda at, where: (at, 0, 0))
    full = pl.pallas_call(
        assemble_kernel,
        out_shape=jax.ShapeDtypeStruct((half, 2, rows, columns), near.dtype),
        grid_spec=pltpu.PrefetchScalarGridSpec(
            num_scalar_prefetch=1,
            grid=(half,),
            in_specs=[block, block],
            out_specs=pl.BlockSpec((1, 2, rows, columns), lambda at, where: (at ^ where[0], 0, 0, 0)),
        ),
        name="assemble",
    )(where, near, far)
    return full.reshape(half * 2 * rows, columns)


def after(values, *others):
    return lax.optimization_barrier((values, others))[0]


def gather_near(shard):
    half = lax.axis_size("dp") // 2
    return exchange_far(jnp.broadcast_to(shard[None], (half, *shard.shape)))


def merge_sides(near, far):
    side = lax.axis_index("dp") % 2
    half, rows, columns = near.shape
    at = lax.broadcasted_iota(jnp.int32, (half, 2, rows, columns), 1)
    return jnp.where(at == side, near[:, None], far[:, None]).reshape(half * 2 * rows, columns)


def split_terms(terms):
    size, side = lax.axis_size("dp"), lax.axis_index("dp") % 2
    *groups, rows, columns = terms.shape
    sides = terms.reshape(*groups, size // 2, 2, rows // size, columns)
    axis = len(groups)
    parts = []
    for which in (side, 1 - side):
        part = lax.dynamic_index_in_dim(sides, which, axis + 1, keepdims=False)
        parts.append(jnp.moveaxis(part, axis, 0))
    return parts


def sum_far_sides(half):
    place = lax.axis_index("dp") // 2
    total = pick(half, place).astype(F32)
    for at in range(1, half.shape[0]):
        total = total + send(pick(half, place ^ at), 2 * at).astype(F32)
    return total


def sum_sides(keep, leave):
    return (keep.astype(F32) + send(leave, 1).astype(F32)).astype(BF16)


def to_units(parts):
    size, units, shape = lax.axis_size("dp"), parts.shape[0], parts.shape[1:]
    before = jnp.zeros((FIRST_SLOT, *shape), BF16)
    after = jnp.zeros((size - FIRST_SLOT - units, *shape), BF16)
    return exchange(jnp.concatenate([before, parts, after], axis=0))


def from_units(parts, units):
    return exchange(parts)[FIRST_SLOT : FIRST_SLOT + units]


def rms_backward(grad_out, normed, inverse, gain):
    scaled = grad_out * gain
    return inverse * (scaled - normed * jnp.mean(scaled * normed, axis=-1, keepdims=True))


def body(
    inputs, seg_parent, positions, w_query, w_key, w_value, w_out, w_gate, w_up, w_down, gain_attn, gain_mlp, out_grad
):
    seg_count = lax.axis_size("dp")
    my_seg = lax.axis_index("dp")
    core = lax.axis_index("tensor") % 2
    chip = lax.axis_index("tensor") // 2
    where = jnp.stack([my_seg, core, chip]).astype(jnp.int32)
    tree_segs = min(16, seg_count)
    branch_count = tree_segs // 4
    path_len = tree_segs - 3 * branch_count + 2
    seg_len, width = inputs.shape[1:]
    scale = HEAD_DIM ** (-0.5)
    part_rows = w_query.shape[0]
    local_heads = w_query.shape[1] // HEAD_DIM
    hidden_units = w_gate.shape[1]
    head_width = local_heads * HEAD_DIM
    units = MICRO * local_heads
    last_width = 256

    def by_head(weight):
        return weight.reshape(part_rows, local_heads, 1, HEAD_DIM)

    mine_qkv = jnp.concatenate([by_head(w_query), by_head(w_key), by_head(w_value)], axis=2)
    mine_qkv = mine_qkv.reshape(part_rows, 3 * head_width)
    spare = jnp.zeros((part_rows, last_width - head_width - 2), BF16)
    packed = jnp.concatenate(
        [w_gate, w_up, w_down.T, w_out.T, gain_attn[:, None], gain_mlp[:, None], spare], axis=1
    )
    small = small_group()
    if small:
        near_qkv = gather_far_sides(mine_qkv)
        full_qkv = assemble(near_qkv, send(near_qkv, 1))
        near = gather_near(packed)
    else:
        full_qkv = lax.all_gather(mine_qkv, "dp", axis=0, tiled=True)

    tables = [rotary_tables(positions[b]) for b in range(MICRO)]
    cosines, sines = (jnp.stack([pair[at] for pair in tables]) for at in range(2))
    blocks = []
    for b in range(MICRO):
        cosine, sine = tables[b]
        heads = dot(full_qkv, inputs[b], ((0,), (1,))).reshape(local_heads, 3, HEAD_DIM, seg_len)
        query = rotate(heads[:, 0], cosine, sine).astype(BF16) * jnp.asarray(scale, BF16)
        key = rotate(heads[:, 1], cosine, sine).astype(BF16)
        blocks.append(jnp.concatenate([query, key, heads[:, 2].astype(BF16)], axis=1))
    blocks = jnp.concatenate(blocks, axis=0)
    unit_qkv = to_units(blocks)
    if small:
        near = after(near, blocks)
        far = send(near, 1)
        near_other = swap(near, 2)
        far = after(far, unit_qkv)
        unit_qkv = after(unit_qkv, far)
        far_other = swap(far, 2)
        weights_own = merge_sides(near, far)
    unit_micro = (my_seg - FIRST_SLOT) // local_heads >= 1
    chain = jnp.where(
        unit_micro,
        path_table(seg_parent[1], seg_count, path_len),
        path_table(seg_parent[0], seg_count, path_len),
    ).reshape(-1)
    unit_low, unit_full, unit_norm = attention_forward(chain, [unit_qkv], path_len)
    attended = from_units(unit_low, units).reshape(MICRO, head_width, seg_len)

    if small:
        weights_other = merge_sides(near_other, far_other)
    else:
        weights_own = lax.all_gather(packed, "dp", axis=0, tiled=True)
        weights_other = swap(weights_own, 2)
    heads_own = pick(attended, chip)
    heads_other = swap(pick(attended, 1 - chip), 2)
    tokens = pick(inputs, chip).astype(F32)
    both_weights = (weights_own, weights_other)
    gates = [w[:, :hidden_units] for w in both_weights]
    ups = [w[:, hidden_units : 2 * hidden_units] for w in both_weights]
    downs = [w[:, 2 * hidden_units : 3 * hidden_units] for w in both_weights]
    lasts = [w[:, 3 * hidden_units :] for w in both_weights]
    outs = [w[:, :head_width] for w in lasts]
    gains = lasts[0][:, head_width : head_width + 2].astype(F32).T
    gain_first, gain_second = gains[0:1], gains[1:2]

    def core_sum(part):
        part = rounded(part)
        return part + swap(part.astype(BF16), 1).astype(F32)

    attn_out = core_sum(dot(heads_own, outs[0], ((0,), (1,))) + dot(heads_other, outs[1], ((0,), (1,))))
    resid_one = tokens + attn_out
    inverse_one = lax.rsqrt(jnp.mean(resid_one * resid_one, axis=-1, keepdims=True) + EPSILON)
    normed_one = resid_one * inverse_one
    hidden = normed_one * gain_first
    hidden_low = hidden.astype(BF16)
    gate = [dot_nn(hidden_low, w) for w in gates]
    up = [dot_nn(hidden_low, w) for w in ups]
    sigmoid = [jax.nn.sigmoid(g) for g in gate]
    silu = [g * s for g, s in zip(gate, sigmoid)]
    activation = [(s * u).astype(BF16) for s, u in zip(silu, up)]
    mlp = core_sum(dot_nt(activation[0], downs[0]) + dot_nt(activation[1], downs[1]))
    resid_two = hidden + mlp
    inverse_two = lax.rsqrt(jnp.mean(resid_two * resid_two, axis=-1, keepdims=True) + EPSILON)
    normed_two = resid_two * inverse_two
    result = (normed_two * gain_second).astype(BF16)

    grad_result = pick(out_grad, chip).astype(F32)
    gain_two_term = jnp.sum(grad_result * normed_two, axis=0)
    grad_resid_two = rms_backward(grad_result, normed_two, inverse_two, gain_second)
    grad_mlp_low = grad_resid_two.astype(BF16)
    grad_act = [dot_nn(grad_mlp_low, w) for w in downs]
    grad_gate_low = [
        (a * u * s * (1.0 + g * (1.0 - s))).astype(BF16) for a, u, s, g in zip(grad_act, up, sigmoid, gate)
    ]
    grad_up_low = [(a * s).astype(BF16) for a, s in zip(grad_act, silu)]
    hidden_part = (
        dot_nt(grad_gate_low[0], gates[0])
        + dot_nt(grad_up_low[0], ups[0])
        + dot_nt(grad_gate_low[1], gates[1])
        + dot_nt(grad_up_low[1], ups[1])
    )
    grad_hidden = grad_resid_two + core_sum(hidden_part)
    gain_one_term = jnp.sum(grad_hidden * normed_one, axis=0)
    grad_resid_one = rms_backward(grad_hidden, normed_one, inverse_one, gain_first)
    grad_attn_low = grad_resid_one.astype(BF16)

    grad_own = dot(outs[0], grad_attn_low, ((0,), (1,))).astype(BF16)
    grad_other = swap(dot(outs[1], grad_attn_low, ((0,), (1,))).astype(BF16), 2)
    first_chip = chip == 0
    grad_pair = jnp.stack(
        [jnp.where(first_chip, grad_own, grad_other), jnp.where(first_chip, grad_other, grad_own)]
    )
    unit_grad = to_units(grad_pair.reshape(units, HEAD_DIM, seg_len))

    down = [dot_tn(grad_mlp_low, a) for a in activation]
    wide = [
        jnp.concatenate([dot_tn(hidden_low, g).astype(BF16), dot_tn(hidden_low, u).astype(BF16)], axis=1)
        for g, u in zip(grad_gate_low, grad_up_low)
    ]
    heads_pad = [jnp.pad(rows, ((0, last_width - head_width), (0, 0))) for rows in (heads_own, heads_other)]
    term_last = []
    for rows in heads_pad:
        term = dot(grad_attn_low, rows, ((0,), (1,)))
        column = lax.broadcasted_iota(jnp.int32, term.shape, 1)
        term = jnp.where(column == head_width, gain_one_term[:, None], term)
        term_last.append(jnp.where(column == head_width + 1, gain_two_term[:, None], term).astype(BF16))
    leave_terms = jnp.concatenate([wide[1], down[1].astype(BF16), term_last[1]], axis=1)
    keep_terms = jnp.concatenate([wide[0], down[0].astype(BF16), term_last[0]], axis=1)
    got_terms = swap(after(leave_terms, grad_other), 2)

    unit_grad = after(unit_grad, leave_terms)
    (unit_back,) = attention_backward(chain, [unit_qkv], unit_grad, unit_full, unit_norm, path_len, scale)
    back = exchange(unit_back)
    if small:
        half_terms = sum_sides(*merge_terms(where, keep_terms, after(got_terms, unit_back)))
    else:
        sum_terms = (keep_terms.astype(F32) + got_terms.astype(F32)).astype(BF16)
        shard = lax.psum_scatter(sum_terms, "dp", scatter_dimension=0, tiled=True).astype(F32)
    if small:
        side = ((seg_count // 2, part_rows, 3 * head_width), BF16)
        keep, leave, part, part_other = whole_call(
            functools.partial(tail_kernel, local_heads),
            where,
            [back, inputs, full_qkv, cosines, sines, grad_resid_one],
            [side, side, ((seg_len, width), F32), ((seg_len, width), BF16)],
            [pltpu.VMEM((MICRO, 3 * head_width, seg_len), BF16)],
            "tail",
        )
        half_terms, keep, leave = lax.optimization_barrier((half_terms, keep, leave))
        shard_qkv = sum_far_sides(sum_sides(keep, leave))
        shard = sum_far_sides(half_terms)
        part = part + swap(part_other, 1).astype(F32)
    else:
        back = back[FIRST_SLOT : FIRST_SLOT + units].astype(F32).reshape(MICRO, local_heads, 3, HEAD_DIM, seg_len)
        grads = []
        for b in range(MICRO):
            query = rotate_back(back[b, :, 0], cosines[b], sines[b])
            key = rotate_back(back[b, :, 1], cosines[b], sines[b])
            grads.append(
                jnp.concatenate([query, key, back[b, :, 2]], axis=1).reshape(3 * head_width, seg_len).astype(BF16)
            )
        stack = jnp.stack(grads)
        term_qkv = sum(dot(inputs[b], grads[b], ((0,), (1,))) for b in range(MICRO)).astype(BF16)
        shard_qkv = lax.psum_scatter(term_qkv, "dp", scatter_dimension=0, tiled=True).astype(F32)
        part_own = dot(pick(stack, core), full_qkv, ((0,), (1,)))
        part_other = dot(pick(stack, 1 - core), full_qkv, ((0,), (1,)))
        part = part_own + swap(part_other.astype(BF16), 1).astype(F32) + jnp.where(core == chip, grad_resid_one, 0.0)
    part = rounded(part)
    input_mine = part + swap(part.astype(BF16), 2).astype(F32)
    shard_last = shard[:, 3 * hidden_units :]
    gain_terms = shard_last[:, head_width : head_width + 2].T
    shard_qkv = shard_qkv.reshape(part_rows, local_heads, 3, HEAD_DIM)

    def by_micro(own, other, first):
        return jnp.stack([jnp.where(first, own, other), jnp.where(first, other, own)])

    half = seg_len // 2
    result_half = swap(pick(result.reshape(2, half, width), core), 2)
    result_other = by_micro(result_half, swap(result_half, 1), core == 0).reshape(seg_len, width)
    return (
        by_micro(result, result_other, first_chip),
        by_micro(input_mine, swap(input_mine, 1), core == 0),
        shard_qkv[:, :, 0].reshape(part_rows, head_width),
        shard_qkv[:, :, 1].reshape(part_rows, head_width),
        shard_qkv[:, :, 2].reshape(part_rows, head_width),
        shard_last[:, :head_width].T,
        shard[:, :hidden_units],
        shard[:, hidden_units : 2 * hidden_units],
        shard[:, 2 * hidden_units : 3 * hidden_units].T,
        gain_terms[0],
        gain_terms[1],
    )


def solution(mesh):
    weight, turned = P("dp", "tensor"), P("tensor", "dp")
    rows, gain = P(None, "dp", None), P("dp")
    return jax.shard_map(
        body,
        mesh=mesh,
        in_specs=(
            rows, P(), P(None, "dp"), weight, weight, weight, turned, weight, weight, turned, gain, gain, rows,
        ),
        out_specs=(rows, rows, weight, weight, weight, turned, weight, weight, turned, gain, gain),
        check_vma=False,
    )
```

```python
import functools

import jax
import jax.numpy as jnp
from jax import lax
from jax.experimental import pallas as pl
from jax.experimental.pallas import tpu as pltpu
from jax.sharding import PartitionSpec as P

HEAD_DIM = 64
MICRO = 2
EPSILON = 1e-06
BIG_NEG = -1e30
FIRST_SLOT = 1
F32 = jnp.float32
BF16 = jnp.bfloat16


def dot(a, b, dims):
    return lax.dot_general(a, b, ((dims[0], dims[1]), ((), ())), preferred_element_type=F32)


def dot_nn(a, b):
    return dot(a, b, ((1,), (0,)))


def dot_nt(a, b):
    return dot(a, b, ((1,), (1,)))


def dot_tn(a, b):
    return dot(a, b, ((0,), (0,)))


def causal_mask(tile):
    return lax.broadcasted_iota(jnp.int32, tile, 0) <= lax.broadcasted_iota(jnp.int32, tile, 1)


def for_path_length(table, seg, path_len, run):
    path, length = [seg], jnp.int32(1)
    for _ in range(1, path_len):
        parent = table[1 + table[0] + jnp.maximum(path[-1], 0)]
        path.append(jnp.where(path[-1] >= 0, parent, -1))
        length = length + jnp.where(path[-1] >= 0, 1, 0)
    for steps in range(1, path_len + 1):

        @pl.when(length == steps)
        def _(steps=steps):
            run(path[:steps])


def forward_kernel(path_len, sources, table, *refs):
    parts, (out_low, out_full, out_norm, *scratch) = refs[:sources], refs[sources:]
    qkv = scratch[0] if scratch else parts[0]
    seg = pl.program_id(0)
    seg_len = qkv.shape[2]
    if scratch:

        @pl.when(seg == 0)
        def _():
            for at, part in enumerate(parts):
                qkv[at] = part[0]

    def run(path):
        query = qkv[seg, 0:HEAD_DIM, :]
        scores = [dot_tn(qkv[source, HEAD_DIM : 2 * HEAD_DIM, :], query) for source in path]
        scores[0] = jnp.where(causal_mask((seg_len, seg_len)), scores[0], BIG_NEG)
        top = functools.reduce(jnp.maximum, [jnp.max(s, axis=0, keepdims=True) for s in scores])
        total, acc = 0.0, 0.0
        for source, score in zip(path, scores):
            probs = jnp.exp(score - top)
            total = total + jnp.sum(probs, axis=0, keepdims=True)
            acc = acc + dot_nn(qkv[source, 2 * HEAD_DIM : 3 * HEAD_DIM, :], probs.astype(BF16))
        result = acc * (1.0 / total)
        out_low[0] = result.astype(BF16)
        out_full[0] = result
        out_norm[0] = top + jnp.log(total)

    for_path_length(table, seg, path_len, run)


def part_specs(parts):
    return [pl.BlockSpec(p.shape, lambda s, t: (0, 0, 0), pipeline_mode=pl.Buffered(1)) for p in parts]


def attention_forward(table, parts, path_len):
    rows, seg_len = parts[0].shape[1:]
    segs = sum(p.shape[0] for p in parts)
    placed = pl.BlockSpec((1, HEAD_DIM, seg_len), lambda s, t: (s, 0, 0))
    tile = pl.BlockSpec((1, HEAD_DIM, seg_len), lambda s, t: (s, 0, 0))
    line = pl.BlockSpec((1, 1, seg_len), lambda s, t: (s, 0, 0))
    scratch = [pltpu.VMEM((segs, rows, seg_len), BF16)] if len(parts) > 1 else []
    return pl.pallas_call(
        functools.partial(forward_kernel, path_len, len(parts)),
        out_shape=(
            jax.ShapeDtypeStruct((segs, HEAD_DIM, seg_len), BF16),
            jax.ShapeDtypeStruct((segs, HEAD_DIM, seg_len), F32),
            jax.ShapeDtypeStruct((segs, 1, seg_len), F32),
        ),
        grid_spec=pltpu.PrefetchScalarGridSpec(
            num_scalar_prefetch=1,
            grid=(segs,),
            in_specs=part_specs(parts),
            out_specs=[placed, tile, line],
            scratch_shapes=scratch,
        ),
        name="tree_attention_forward",
    )(table, *parts)


def backward_kernel(path_len, scale, sources, table, *refs):
    parts, (grad_ref, full_ref, norm_ref) = refs[:sources], refs[sources : sources + 3]
    outs = refs[sources + 3 : 2 * sources + 3]
    grad_query, grad_key, grad_value, *scratch = refs[2 * sources + 3 :]
    qkv = scratch[0] if scratch else parts[0]
    seg = pl.program_id(0)
    segs, _, seg_len = qkv.shape

    @pl.when(seg == 0)
    def _():
        grad_key[...] = jnp.zeros_like(grad_key)
        grad_value[...] = jnp.zeros_like(grad_value)
        if scratch:
            for at, part in enumerate(parts):
                qkv[at] = part[0]

    def run(path):
        query = qkv[seg, 0:HEAD_DIM, :]
        grad = grad_ref[0]
        delta = jnp.sum(grad.astype(F32) * full_ref[0], axis=0, keepdims=True)
        norm = norm_ref[0]
        total = 0.0
        for step, source in enumerate(path):
            key = qkv[source, HEAD_DIM : 2 * HEAD_DIM, :]
            value = qkv[source, 2 * HEAD_DIM : 3 * HEAD_DIM, :]
            probs = jnp.exp(dot_tn(key, query) - norm)
            if step == 0:
                probs = jnp.where(causal_mask((seg_len, seg_len)), probs, 0.0)
            score_grad = (probs * (dot_tn(value, grad) - delta)).astype(BF16)
            total = total + dot_nn(key, score_grad)
            grad_key[source] += dot_nt(query, score_grad)
            grad_value[source] += dot_nt(grad, probs.astype(BF16))
        grad_query[seg] = (total * scale).astype(BF16)

    for_path_length(table, seg, path_len, run)

    @pl.when(seg == segs - 1)
    def _():
        at = 0
        for out in outs:
            rows = slice(at, at + out.shape[0])
            out[:, 0:HEAD_DIM, :] = grad_query[rows]
            out[:, HEAD_DIM : 2 * HEAD_DIM, :] = grad_key[rows].astype(BF16)
            out[:, 2 * HEAD_DIM : 3 * HEAD_DIM, :] = grad_value[rows].astype(BF16)
            at += out.shape[0]


def attention_backward(table, parts, grad, full, norm, path_len, scale):
    rows, seg_len = parts[0].shape[1:]
    segs = sum(p.shape[0] for p in parts)
    placed = pl.BlockSpec((1, HEAD_DIM, seg_len), lambda s, t: (s, 0, 0))
    tile = pl.BlockSpec((1, HEAD_DIM, seg_len), lambda s, t: (s, 0, 0))
    line = pl.BlockSpec((1, 1, seg_len), lambda s, t: (s, 0, 0))
    scratch = [
        pltpu.VMEM((segs, HEAD_DIM, seg_len), BF16),
        pltpu.VMEM((segs, HEAD_DIM, seg_len), F32),
        pltpu.VMEM((segs, HEAD_DIM, seg_len), F32),
    ]
    if len(parts) > 1:
        scratch.append(pltpu.VMEM((segs, rows, seg_len), BF16))
    return pl.pallas_call(
        functools.partial(backward_kernel, path_len, scale, len(parts)),
        out_shape=[jax.ShapeDtypeStruct(p.shape, BF16) for p in parts],
        grid_spec=pltpu.PrefetchScalarGridSpec(
            num_scalar_prefetch=1,
            grid=(segs,),
            in_specs=[*part_specs(parts), placed, tile, line],
            out_specs=part_specs(parts),
            scratch_shapes=scratch,
        ),
        name="tree_attention_backward",
    )(table, *parts, grad, full, norm)


def rotary_tables(token_pos):
    half = HEAD_DIM // 2
    frequency = 10000.0 ** (-jnp.arange(half, dtype=F32) * 2.0 / HEAD_DIM)
    angles = frequency[:, None] * token_pos.astype(F32)[None, :]
    return jnp.cos(angles), jnp.sin(angles)


def rotate(tensor, cosine, sine):
    half = HEAD_DIM // 2
    first, second = tensor[..., :half, :], tensor[..., half:, :]
    return jnp.concatenate([first * cosine - second * sine, first * sine + second * cosine], axis=-2)


def rotate_back(tensor, cosine, sine):
    half = HEAD_DIM // 2
    first, second = tensor[..., :half, :], tensor[..., half:, :]
    return jnp.concatenate([first * cosine + second * sine, second * cosine - first * sine], axis=-2)


def whole_call(kernel, where, operands, outs, scratch, name):
    def spec(shape):
        return pl.BlockSpec(shape, lambda at, where: (0,) * len(shape), pipeline_mode=pl.Buffered(1))

    return pl.pallas_call(
        kernel,
        out_shape=[jax.ShapeDtypeStruct(shape, kind) for shape, kind in outs],
        grid_spec=pltpu.PrefetchScalarGridSpec(
            num_scalar_prefetch=1,
            grid=(1,),
            in_specs=[spec(operand.shape) for operand in operands],
            out_specs=[spec(shape) for shape, _ in outs],
            scratch_shapes=scratch,
        ),
        name=name,
    )(where, *operands)


def pack_kernel(where, query, key, value, gate, up, down, out, gain_one, gain_two, mine, spread):
    parts = []
    for at in range(0, query.shape[1], HEAD_DIM):
        parts += [ref[:, at : at + HEAD_DIM] for ref in (query, key, value)]
    mine[...] = jnp.concatenate(parts, axis=1)
    width, heads = gate.shape[1], out.shape[0]
    spare = jnp.zeros((out.shape[1], spread.shape[2] - 3 * width - heads - 2), BF16)
    gains = [ref[...].astype(F32).T.astype(BF16) for ref in (gain_one, gain_two)]
    last = jnp.concatenate([out[...].T, *gains, spare], axis=1)
    turned = down[...].T
    for at in range(spread.shape[0]):
        spread[at, :, 0:width] = gate[...]
        spread[at, :, width : 2 * width] = up[...]
        spread[at, :, 2 * width : 3 * width] = turned
        spread[at, :, 3 * width :] = last


def store_sides(side, term, keep, leave):
    rows = keep.shape[1]
    for at in range(2 * keep.shape[0]):
        part = term[at * rows : (at + 1) * rows].astype(BF16)

        @pl.when(side == at % 2)
        def _(at=at, part=part):
            keep[at // 2] = part

        @pl.when(side != at % 2)
        def _(at=at, part=part):
            leave[at // 2] = part


def merge_kernel(where, own, got, keep, leave):
    store_sides(where[0] % 2, own[...].astype(F32) + got[...].astype(F32), keep, leave)


def merge_terms(where, own, got):
    rows, columns = own.shape
    size = lax.axis_size("dp")
    side = ((size // 2, rows // size, columns), BF16)
    return whole_call(merge_kernel, where, [own, got], [side, side], [], "merge_terms")


def tail_kernel(heads, where, blocks, tokens, weights, cosine, sine, resid, keep, leave, own, other, grads):
    core, chip = where[1], where[2]
    total = 0.0
    for batch in range(MICRO):
        for head in range(heads):
            block = blocks[FIRST_SLOT + batch * heads + head]
            start = 3 * HEAD_DIM * head
            query = rotate_back(block[0:HEAD_DIM].astype(F32), cosine[batch], sine[batch])
            key = rotate_back(block[HEAD_DIM : 2 * HEAD_DIM].astype(F32), cosine[batch], sine[batch])
            grads[batch, start : start + HEAD_DIM] = query.astype(BF16)
            grads[batch, start + HEAD_DIM : start + 2 * HEAD_DIM] = key.astype(BF16)
            grads[batch, start + 2 * HEAD_DIM : start + 3 * HEAD_DIM] = block[2 * HEAD_DIM :]
        total = total + dot_nt(tokens[batch].T, grads[batch])
    store_sides(where[0] % 2, total, keep, leave)
    own[...] = dot_nt(grads[core].T, weights[...]) + jnp.where(core == chip, 1.0, 0.0) * resid[...]
    other[...] = dot_nt(grads[1 - core].T, weights[...]).astype(BF16)


def swap(value, bit):
    count = lax.axis_size("tensor")
    return lax.ppermute(value, "tensor", [(at, at ^ bit) for at in range(count)])


def send(value, bits):
    return lax.ppermute(value, "dp", [(at, at ^ bits) for at in range(lax.axis_size("dp"))])


def exchange(blocks):
    return lax.all_to_all(blocks, "dp", 0, 0, tiled=True)


def exchange_far(blocks):
    size = lax.axis_size("dp")
    groups = [list(range(side, size, 2)) for side in range(2)]
    return lax.all_to_all(blocks, "dp", 0, 0, axis_index_groups=groups, tiled=True)


def rounded(value):
    return lax.reduce_precision(value, 8, 7)


def pick(stack, at):
    return lax.dynamic_index_in_dim(stack, at, 0, keepdims=False)


def small_group():
    return lax.axis_size("dp") in (4, 8)


def gather_far_sides(shard):
    return jnp.stack([shard] + [send(shard, bits) for bits in range(2, lax.axis_size("dp"), 2)])


def assemble_kernel(where, near, far, out):
    side = where[1]
    out[0, side] = near[0]
    out[0, 1 - side] = far[0]


def assemble(near, far):
    half, rows, columns = near.shape
    me = lax.axis_index("dp")
    where = jnp.stack([me // 2, me % 2]).astype(jnp.int32)
    block = pl.BlockSpec((1, rows, columns), lambda at, where: (at, 0, 0))
    full = pl.pallas_call(
        assemble_kernel,
        out_shape=jax.ShapeDtypeStruct((half, 2, rows, columns), near.dtype),
        grid_spec=pltpu.PrefetchScalarGridSpec(
            num_scalar_prefetch=1,
            grid=(half,),
            in_specs=[block, block],
            out_specs=pl.BlockSpec((1, 2, rows, columns), lambda at, where: (at ^ where[0], 0, 0, 0)),
        ),
        name="assemble",
    )(where, near, far)
    return full.reshape(half * 2 * rows, columns)


def after(values, *others):
    return lax.optimization_barrier((values, others))[0]


def gather_near(shard):
    half = lax.axis_size("dp") // 2
    return exchange_far(jnp.broadcast_to(shard[None], (half, *shard.shape)))


def merge_sides(near, far):
    side = lax.axis_index("dp") % 2
    half, rows, columns = near.shape
    at = lax.broadcasted_iota(jnp.int32, (half, 2, rows, columns), 1)
    return jnp.where(at == side, near[:, None], far[:, None]).reshape(half * 2 * rows, columns)


def split_terms(terms):
    size, side = lax.axis_size("dp"), lax.axis_index("dp") % 2
    *groups, rows, columns = terms.shape
    sides = terms.reshape(*groups, size // 2, 2, rows // size, columns)
    axis = len(groups)
    parts = []
    for which in (side, 1 - side):
        part = lax.dynamic_index_in_dim(sides, which, axis + 1, keepdims=False)
        parts.append(jnp.moveaxis(part, axis, 0))
    return parts


def sum_far_sides(half):
    place = lax.axis_index("dp") // 2
    total = pick(half, place).astype(F32)
    for at in range(1, half.shape[0]):
        total = total + send(pick(half, place ^ at), 2 * at).astype(F32)
    return total


def sum_sides(keep, leave):
    return (keep.astype(F32) + send(leave, 1).astype(F32)).astype(BF16)


def to_units(parts):
    size, units, shape = lax.axis_size("dp"), parts.shape[0], parts.shape[1:]
    before = jnp.zeros((FIRST_SLOT, *shape), BF16)
    after = jnp.zeros((size - FIRST_SLOT - units, *shape), BF16)
    return exchange(jnp.concatenate([before, parts, after], axis=0))


def from_units(parts, units):
    return exchange(parts)[FIRST_SLOT : FIRST_SLOT + units]


def rms_backward(grad_out, normed, inverse, gain):
    scaled = grad_out * gain
    return inverse * (scaled - normed * jnp.mean(scaled * normed, axis=-1, keepdims=True))


def body(
    inputs, seg_parent, positions, w_query, w_key, w_value, w_out, w_gate, w_up, w_down, gain_attn, gain_mlp, out_grad
):
    seg_count = lax.axis_size("dp")
    my_seg = lax.axis_index("dp")
    core = lax.axis_index("tensor") % 2
    chip = lax.axis_index("tensor") // 2
    where = jnp.stack([my_seg, core, chip]).astype(jnp.int32)
    tree_segs = min(16, seg_count)
    branch_count = tree_segs // 4
    path_len = tree_segs - 3 * branch_count + 2
    seg_len, width = inputs.shape[1:]
    scale = HEAD_DIM ** (-0.5)
    part_rows = w_query.shape[0]
    local_heads = w_query.shape[1] // HEAD_DIM
    hidden_units = w_gate.shape[1]
    head_width = local_heads * HEAD_DIM
    units = MICRO * local_heads
    last_width = 256

    small = small_group()
    columns = 3 * hidden_units + last_width
    spread_count = seg_count // 2 if small else 1
    mine_qkv, spread = whole_call(
        pack_kernel,
        where,
        [w_query, w_key, w_value, w_gate, w_up, w_down, w_out, gain_attn[None], gain_mlp[None]],
        [((part_rows, 3 * head_width), BF16), ((spread_count, part_rows, columns), BF16)],
        [],
        "pack",
    )
    if small:
        near_qkv = gather_far_sides(mine_qkv)
        far_qkv = send(near_qkv, 1)
        near = exchange_far(spread)
        full_qkv = assemble(near_qkv, far_qkv)
    else:
        full_qkv = lax.all_gather(mine_qkv, "dp", axis=0, tiled=True)
        packed = spread[0]

    tables = [rotary_tables(positions[b]) for b in range(MICRO)]
    cosines, sines = (jnp.stack([pair[at] for pair in tables]) for at in range(2))
    blocks = []
    for b in range(MICRO):
        cosine, sine = tables[b]
        heads = dot(full_qkv, inputs[b], ((0,), (1,))).reshape(local_heads, 3, HEAD_DIM, seg_len)
        query = rotate(heads[:, 0], cosine, sine).astype(BF16) * jnp.asarray(scale, BF16)
        key = rotate(heads[:, 1], cosine, sine).astype(BF16)
        blocks.append(jnp.concatenate([query, key, heads[:, 2].astype(BF16)], axis=1))
    blocks = jnp.concatenate(blocks, axis=0)
    unit_qkv = to_units(blocks)
    if small:
        near = after(near, blocks)
        cut = 2 * hidden_units
        far_one = send(near[:, :, cut:], 1)
        far_two = send(after(near[:, :, :cut], far_one), 1)
        near_other = swap(near, 2)
        unit_qkv, far_one, near_other = lax.optimization_barrier((unit_qkv, far_one, near_other))
        far_one_other = swap(far_one, 2)
    unit_micro = (my_seg - FIRST_SLOT) // local_heads >= 1
    chain = jnp.concatenate([jnp.where(unit_micro, seg_count, 0).reshape(1), seg_parent.reshape(-1)])
    chain = chain.astype(jnp.int32)
    unit_low, unit_full, unit_norm = attention_forward(chain, [unit_qkv], path_len)
    if small:
        unit_low, far_two, far_one_other = lax.optimization_barrier((unit_low, far_two, far_one_other))
        far_two_other = swap(far_two, 2)
        far = jnp.concatenate([far_two, far_one], axis=2)
        weights_own = merge_sides(near, far)
    attended = from_units(unit_low, units).reshape(MICRO, head_width, seg_len)

    if small:
        weights_other = merge_sides(near_other, jnp.concatenate([far_two_other, far_one_other], axis=2))
    else:
        weights_own = lax.all_gather(packed, "dp", axis=0, tiled=True)
        weights_other = swap(weights_own, 2)
    heads_own = pick(attended, chip)
    heads_other = swap(pick(attended, 1 - chip), 2)
    tokens = pick(inputs, chip).astype(F32)
    both_weights = (weights_own, weights_other)
    gates = [w[:, :hidden_units] for w in both_weights]
    ups = [w[:, hidden_units : 2 * hidden_units] for w in both_weights]
    downs = [w[:, 2 * hidden_units : 3 * hidden_units] for w in both_weights]
    lasts = [w[:, 3 * hidden_units :] for w in both_weights]
    outs = [w[:, :head_width] for w in lasts]
    gains = lasts[0][:, head_width : head_width + 2].astype(F32).T
    gain_first, gain_second = gains[0:1], gains[1:2]

    def core_sum(part):
        part = rounded(part)
        return part + swap(part.astype(BF16), 1).astype(F32)

    attn_out = core_sum(dot(heads_own, outs[0], ((0,), (1,))) + dot(heads_other, outs[1], ((0,), (1,))))
    resid_one = tokens + attn_out
    inverse_one = lax.rsqrt(jnp.mean(resid_one * resid_one, axis=-1, keepdims=True) + EPSILON)
    normed_one = resid_one * inverse_one
    hidden = normed_one * gain_first
    hidden_low = hidden.astype(BF16)
    gate = [dot_nn(hidden_low, w) for w in gates]
    up = [dot_nn(hidden_low, w) for w in ups]
    sigmoid = [jax.nn.sigmoid(g) for g in gate]
    silu = [g * s for g, s in zip(gate, sigmoid)]
    activation = [(s * u).astype(BF16) for s, u in zip(silu, up)]
    mlp = core_sum(dot_nt(activation[0], downs[0]) + dot_nt(activation[1], downs[1]))
    resid_two = hidden + mlp
    inverse_two = lax.rsqrt(jnp.mean(resid_two * resid_two, axis=-1, keepdims=True) + EPSILON)
    normed_two = resid_two * inverse_two
    result = (normed_two * gain_second).astype(BF16)

    grad_result = pick(out_grad, chip).astype(F32)
    gain_two_term = jnp.sum(grad_result * normed_two, axis=0)
    grad_resid_two = rms_backward(grad_result, normed_two, inverse_two, gain_second)
    grad_mlp_low = grad_resid_two.astype(BF16)
    grad_act = [dot_nn(grad_mlp_low, w) for w in downs]
    grad_gate_low = [
        (a * u * s * (1.0 + g * (1.0 - s))).astype(BF16) for a, u, s, g in zip(grad_act, up, sigmoid, gate)
    ]
    grad_up_low = [(a * s).astype(BF16) for a, s in zip(grad_act, silu)]
    hidden_part = (
        dot_nt(grad_gate_low[0], gates[0])
        + dot_nt(grad_up_low[0], ups[0])
        + dot_nt(grad_gate_low[1], gates[1])
        + dot_nt(grad_up_low[1], ups[1])
    )
    grad_hidden = grad_resid_two + core_sum(hidden_part)
    gain_one_term = jnp.sum(grad_hidden * normed_one, axis=0)
    grad_resid_one = rms_backward(grad_hidden, normed_one, inverse_one, gain_first)
    grad_attn_low = grad_resid_one.astype(BF16)

    grad_own = dot(outs[0], grad_attn_low, ((0,), (1,))).astype(BF16)
    grad_other = swap(dot(outs[1], grad_attn_low, ((0,), (1,))).astype(BF16), 2)
    first_chip = chip == 0
    grad_pair = jnp.stack(
        [jnp.where(first_chip, grad_own, grad_other), jnp.where(first_chip, grad_other, grad_own)]
    )
    unit_grad = to_units(grad_pair.reshape(units, HEAD_DIM, seg_len))

    down = [dot_tn(grad_mlp_low, a) for a in activation]
    wide = [
        jnp.concatenate([dot_tn(hidden_low, g).astype(BF16), dot_tn(hidden_low, u).astype(BF16)], axis=1)
        for g, u in zip(grad_gate_low, grad_up_low)
    ]
    heads_pad = [jnp.pad(rows, ((0, last_width - head_width), (0, 0))) for rows in (heads_own, heads_other)]
    term_last = []
    for rows in heads_pad:
        term = dot(grad_attn_low, rows, ((0,), (1,)))
        column = lax.broadcasted_iota(jnp.int32, term.shape, 1)
        term = jnp.where(column == head_width, gain_one_term[:, None], term)
        term_last.append(jnp.where(column == head_width + 1, gain_two_term[:, None], term).astype(BF16))
    leave_terms = jnp.concatenate([wide[1], down[1].astype(BF16), term_last[1]], axis=1)
    keep_terms = jnp.concatenate([wide[0], down[0].astype(BF16), term_last[0]], axis=1)
    got_terms = swap(after(leave_terms, grad_other), 2)

    unit_grad = after(unit_grad, leave_terms)
    (unit_back,) = attention_backward(chain, [unit_qkv], unit_grad, unit_full, unit_norm, path_len, scale)
    back = exchange(unit_back)
    if small:
        half_terms = sum_sides(*merge_terms(where, keep_terms, after(got_terms, unit_back)))
    else:
        sum_terms = (keep_terms.astype(F32) + got_terms.astype(F32)).astype(BF16)
        shard = lax.psum_scatter(sum_terms, "dp", scatter_dimension=0, tiled=True).astype(F32)
    if small:
        side = ((seg_count // 2, part_rows, 3 * head_width), BF16)
        keep, leave, part, part_other = whole_call(
            functools.partial(tail_kernel, local_heads),
            where,
            [back, inputs, full_qkv, cosines, sines, grad_resid_one],
            [side, side, ((seg_len, width), F32), ((seg_len, width), BF16)],
            [pltpu.VMEM((MICRO, 3 * head_width, seg_len), BF16)],
            "tail",
        )
        half_terms, keep, leave = lax.optimization_barrier((half_terms, keep, leave))
        shard_qkv = sum_far_sides(sum_sides(keep, leave))
        shard = sum_far_sides(half_terms)
        part = part + swap(part_other, 1).astype(F32)
    else:
        back = back[FIRST_SLOT : FIRST_SLOT + units].astype(F32).reshape(MICRO, local_heads, 3, HEAD_DIM, seg_len)
        grads = []
        for b in range(MICRO):
            query = rotate_back(back[b, :, 0], cosines[b], sines[b])
            key = rotate_back(back[b, :, 1], cosines[b], sines[b])
            grads.append(
                jnp.concatenate([query, key, back[b, :, 2]], axis=1).reshape(3 * head_width, seg_len).astype(BF16)
            )
        stack = jnp.stack(grads)
        term_qkv = sum(dot(inputs[b], grads[b], ((0,), (1,))) for b in range(MICRO)).astype(BF16)
        shard_qkv = lax.psum_scatter(term_qkv, "dp", scatter_dimension=0, tiled=True).astype(F32)
        part_own = dot(pick(stack, core), full_qkv, ((0,), (1,)))
        part_other = dot(pick(stack, 1 - core), full_qkv, ((0,), (1,)))
        part = part_own + swap(part_other.astype(BF16), 1).astype(F32) + jnp.where(core == chip, grad_resid_one, 0.0)
    part = rounded(part)
    input_mine = part + swap(part.astype(BF16), 2).astype(F32)
    shard_last = shard[:, 3 * hidden_units :]
    gain_terms = shard_last[:, head_width : head_width + 2].T
    shard_qkv = shard_qkv.reshape(part_rows, local_heads, 3, HEAD_DIM)

    def by_micro(own, other, first):
        return jnp.stack([jnp.where(first, own, other), jnp.where(first, other, own)])

    half = seg_len // 2
    result_half = swap(pick(result.reshape(2, half, width), core), 2)
    result_other = by_micro(result_half, swap(result_half, 1), core == 0).reshape(seg_len, width)
    return (
        by_micro(result, result_other, first_chip),
        by_micro(input_mine, swap(input_mine, 1), core == 0),
        shard_qkv[:, :, 0].reshape(part_rows, head_width),
        shard_qkv[:, :, 1].reshape(part_rows, head_width),
        shard_qkv[:, :, 2].reshape(part_rows, head_width),
        shard_last[:, :head_width].T,
        shard[:, :hidden_units],
        shard[:, hidden_units : 2 * hidden_units],
        shard[:, 2 * hidden_units : 3 * hidden_units].T,
        gain_terms[0],
        gain_terms[1],
    )


def solution(mesh):
    weight, turned = P("dp", "tensor"), P("tensor", "dp")
    rows, gain = P(None, "dp", None), P("dp")
    return jax.shard_map(
        body,
        mesh=mesh,
        in_specs=(
            rows, P(), P(None, "dp"), weight, weight, weight, turned, weight, weight, turned, gain, gain, rows,
        ),
        out_specs=(rows, rows, weight, weight, weight, turned, weight, weight, turned, gain, gain),
        check_vma=False,
    )
```

```python
import functools

import jax
import jax.numpy as jnp
from jax import lax
from jax.experimental import pallas as pl
from jax.experimental.pallas import tpu as pltpu
from jax.sharding import PartitionSpec as P

HEAD_DIM = 64
MICRO = 2
EPSILON = 1e-06
BIG_NEG = -1e30
FIRST_SLOT = 1
F32 = jnp.float32
BF16 = jnp.bfloat16


def dot(a, b, dims):
    return lax.dot_general(a, b, ((dims[0], dims[1]), ((), ())), preferred_element_type=F32)


def dot_nn(a, b):
    return dot(a, b, ((1,), (0,)))


def dot_nt(a, b):
    return dot(a, b, ((1,), (1,)))


def dot_tn(a, b):
    return dot(a, b, ((0,), (0,)))


def causal_mask(tile):
    return lax.broadcasted_iota(jnp.int32, tile, 0) <= lax.broadcasted_iota(jnp.int32, tile, 1)


def path_of(table, seg, path_len):
    path, length = [seg], jnp.int32(1)
    for _ in range(1, path_len):
        parent = table[1 + table[0] + jnp.maximum(path[-1], 0)]
        path.append(jnp.where(path[-1] >= 0, parent, -1))
        length = length + jnp.where(path[-1] >= 0, 1, 0)
    return path, length


def forward_kernel(path_len, sources, table, *refs):
    parts, (out_low, out_full, out_norm, *scratch) = refs[:sources], refs[sources:]
    qkv = scratch[0] if scratch else parts[0]
    seg = pl.program_id(0)
    seg_len = qkv.shape[2]
    if scratch:

        @pl.when(seg == 0)
        def _():
            for at, part in enumerate(parts):
                qkv[at] = part[0]

    def run(path):
        query = qkv[seg, 0:HEAD_DIM, :]
        scores = [dot_tn(qkv[source, HEAD_DIM : 2 * HEAD_DIM, :], query) for source in path]
        scores[0] = jnp.where(causal_mask((seg_len, seg_len)), scores[0], BIG_NEG)
        top = functools.reduce(jnp.maximum, [jnp.max(s, axis=0, keepdims=True) for s in scores])
        total, acc = 0.0, 0.0
        for source, score in zip(path, scores):
            probs = jnp.exp(score - top)
            total = total + jnp.sum(probs, axis=0, keepdims=True)
            acc = acc + dot_nn(qkv[source, 2 * HEAD_DIM : 3 * HEAD_DIM, :], probs.astype(BF16))
        result = acc * (1.0 / total)
        out_low[0] = result.astype(BF16)
        out_full[0] = result
        out_norm[0] = top + jnp.log(total)

    path, length = path_of(table, seg, path_len)
    for steps in range(1, path_len + 1):
        pl.when(length == steps)(functools.partial(run, path[:steps]))


def part_specs(parts):
    return [pl.BlockSpec(p.shape, lambda s, t: (0, 0, 0), pipeline_mode=pl.Buffered(1)) for p in parts]


def attention_forward(table, parts, path_len):
    rows, seg_len = parts[0].shape[1:]
    segs = sum(p.shape[0] for p in parts)
    placed = pl.BlockSpec((1, HEAD_DIM, seg_len), lambda s, t: (s, 0, 0))
    tile = pl.BlockSpec((1, HEAD_DIM, seg_len), lambda s, t: (s, 0, 0))
    line = pl.BlockSpec((1, 1, seg_len), lambda s, t: (s, 0, 0))
    scratch = [pltpu.VMEM((segs, rows, seg_len), BF16)] if len(parts) > 1 else []
    return pl.pallas_call(
        functools.partial(forward_kernel, path_len, len(parts)),
        out_shape=(
            jax.ShapeDtypeStruct((segs, HEAD_DIM, seg_len), BF16),
            jax.ShapeDtypeStruct((segs, HEAD_DIM, seg_len), F32),
            jax.ShapeDtypeStruct((segs, 1, seg_len), F32),
        ),
        grid_spec=pltpu.PrefetchScalarGridSpec(
            num_scalar_prefetch=1,
            grid=(segs,),
            in_specs=part_specs(parts),
            out_specs=[placed, tile, line],
            scratch_shapes=scratch,
        ),
        name="tree_attention_forward",
    )(table, *parts)


def backward_kernel(path_len, scale, sources, table, *refs):
    parts, (grad_ref, full_ref, norm_ref) = refs[:sources], refs[sources : sources + 3]
    outs = refs[sources + 3 : 2 * sources + 3]
    grad_query, grad_key, grad_value, partial, *scratch = refs[2 * sources + 3 :]
    qkv = scratch[0] if scratch else parts[0]
    seg = pl.program_id(0)
    segs, _, seg_len = qkv.shape

    @pl.when(seg == 0)
    def _():
        @pl.loop(0, segs)
        def _(at):
            grad_key[at] = jnp.zeros(grad_key.shape[1:], F32)
            grad_value[at] = jnp.zeros(grad_value.shape[1:], F32)

        if scratch:
            for at, part in enumerate(parts):
                qkv[at] = part[0]

    def run(path, first):
        query = qkv[seg, 0:HEAD_DIM, :]
        grad = grad_ref[0]
        delta = jnp.sum(grad.astype(F32) * full_ref[0], axis=0, keepdims=True)
        norm = norm_ref[0]
        total = 0.0 if first == 0 else partial[...]
        for step, source in enumerate(path):
            key = qkv[source, HEAD_DIM : 2 * HEAD_DIM, :]
            value = qkv[source, 2 * HEAD_DIM : 3 * HEAD_DIM, :]
            probs = jnp.exp(dot_tn(key, query) - norm)
            if first + step == 0:
                probs = jnp.where(causal_mask((seg_len, seg_len)), probs, 0.0)
            score_grad = (probs * (dot_tn(value, grad) - delta)).astype(BF16)
            total = total + dot_nn(key, score_grad)
            grad_key[source] += dot_nt(query, score_grad)
            grad_value[source] += dot_nt(grad, probs.astype(BF16))
        partial[...] = total

    path, length = path_of(table, seg, path_len)
    pl.when(length == 1)(functools.partial(run, path[:1], 0))
    pl.when(length >= 2)(functools.partial(run, path[:2], 0))
    for first in range(2, path_len):
        pl.when(length > first)(functools.partial(run, path[first : first + 1], first))
    grad_query[seg] = (partial[...] * scale).astype(BF16)

    @pl.when(seg == segs - 1)
    def _():
        first = 0
        for out in outs:

            @pl.loop(0, out.shape[0])
            def _(at, out=out, first=first):
                out[at, 0:HEAD_DIM, :] = grad_query[first + at]
                out[at, HEAD_DIM : 2 * HEAD_DIM, :] = grad_key[first + at].astype(BF16)
                out[at, 2 * HEAD_DIM : 3 * HEAD_DIM, :] = grad_value[first + at].astype(BF16)

            first += out.shape[0]


def attention_backward(table, parts, grad, full, norm, path_len, scale):
    rows, seg_len = parts[0].shape[1:]
    segs = sum(p.shape[0] for p in parts)
    placed = pl.BlockSpec((1, HEAD_DIM, seg_len), lambda s, t: (s, 0, 0))
    tile = pl.BlockSpec((1, HEAD_DIM, seg_len), lambda s, t: (s, 0, 0))
    line = pl.BlockSpec((1, 1, seg_len), lambda s, t: (s, 0, 0))
    scratch = [
        pltpu.VMEM((segs, HEAD_DIM, seg_len), BF16),
        pltpu.VMEM((segs, HEAD_DIM, seg_len), F32),
        pltpu.VMEM((segs, HEAD_DIM, seg_len), F32),
        pltpu.VMEM((HEAD_DIM, seg_len), F32),
    ]
    if len(parts) > 1:
        scratch.append(pltpu.VMEM((segs, rows, seg_len), BF16))
    return pl.pallas_call(
        functools.partial(backward_kernel, path_len, scale, len(parts)),
        out_shape=[jax.ShapeDtypeStruct(p.shape, BF16) for p in parts],
        grid_spec=pltpu.PrefetchScalarGridSpec(
            num_scalar_prefetch=1,
            grid=(segs,),
            in_specs=[*part_specs(parts), placed, tile, line],
            out_specs=part_specs(parts),
            scratch_shapes=scratch,
        ),
        name="tree_attention_backward",
    )(table, *parts, grad, full, norm)


def rotary_tables(token_pos):
    half = HEAD_DIM // 2
    frequency = 10000.0 ** (-jnp.arange(half, dtype=F32) * 2.0 / HEAD_DIM)
    angles = frequency[:, None] * token_pos.astype(F32)[None, :]
    return jnp.cos(angles), jnp.sin(angles)


def rotate(tensor, cosine, sine):
    half = HEAD_DIM // 2
    first, second = tensor[..., :half, :], tensor[..., half:, :]
    return jnp.concatenate([first * cosine - second * sine, first * sine + second * cosine], axis=-2)


def rotate_back(tensor, cosine, sine):
    half = HEAD_DIM // 2
    first, second = tensor[..., :half, :], tensor[..., half:, :]
    return jnp.concatenate([first * cosine + second * sine, second * cosine - first * sine], axis=-2)


def whole_call(kernel, where, operands, outs, scratch, name):
    def spec(shape):
        return pl.BlockSpec(shape, lambda at, where: (0,) * len(shape), pipeline_mode=pl.Buffered(1))

    return pl.pallas_call(
        kernel,
        out_shape=[jax.ShapeDtypeStruct(shape, kind) for shape, kind in outs],
        grid_spec=pltpu.PrefetchScalarGridSpec(
            num_scalar_prefetch=1,
            grid=(1,),
            in_specs=[spec(operand.shape) for operand in operands],
            out_specs=[spec(shape) for shape, _ in outs],
            scratch_shapes=scratch,
        ),
        name=name,
    )(where, *operands)


def pack_kernel(where, query, key, value, gate, up, down, out, gain_one, gain_two, mine, spread):
    mine[...] = jnp.concatenate([query[...], key[...], value[...]], axis=1)
    width, heads = gate.shape[1], out.shape[0]
    spare = jnp.zeros((out.shape[1], spread.shape[2] - 3 * width - heads - 2), BF16)
    gains = [ref[...].astype(F32).T.astype(BF16) for ref in (gain_one, gain_two)]
    last = jnp.concatenate([out[...].T, *gains, spare], axis=1)
    turned = down[...].T

    @pl.loop(0, spread.shape[0])
    def _(at):
        spread[at, :, 0:width] = gate[...]
        spread[at, :, width : 2 * width] = up[...]
        spread[at, :, 2 * width : 3 * width] = turned
        spread[at, :, 3 * width :] = last


def merge_kernel(where, own, got, *outs):
    half = own.shape[0] // 2
    side = where[0] % 2
    rows = [pl.ds(pl.multiple_of(half * which, half), half) for which in (side, 1 - side)]
    start = 0
    for keep, leave in zip(outs[0::2], outs[1::2]):
        columns = slice(start, start + keep.shape[2])
        for out, at in zip((keep, leave), rows):
            out[0] = (own[at, columns].astype(F32) + got[at, columns].astype(F32)).astype(BF16)
        start += keep.shape[2]


def merge_terms(where, own, got, groups):
    rows, columns = own.shape
    half = lax.axis_size("dp") // 2
    tile = rows // half
    block = pl.BlockSpec((tile, columns), lambda at, where: (at, 0))
    shapes = [(half, tile // 2, width) for width in groups for _ in range(2)]
    return pl.pallas_call(
        merge_kernel,
        out_shape=[jax.ShapeDtypeStruct(shape, BF16) for shape in shapes],
        grid_spec=pltpu.PrefetchScalarGridSpec(
            num_scalar_prefetch=1,
            grid=(half,),
            in_specs=[block, block],
            out_specs=[pl.BlockSpec((1, *shape[1:]), lambda at, where: (at, 0, 0)) for shape in shapes],
        ),
        name="merge_terms",
    )(where, own, got)


def tail_kernel(heads, where, blocks, tokens, weights, cosine, sine, resid, keep, leave, own, other, grads, terms):
    core, chip = where[1], where[2]
    terms[...] = jnp.zeros_like(terms)

    @pl.loop(0, MICRO)
    def _(batch):
        for head in range(heads):
            block = blocks[FIRST_SLOT + batch * heads + head]
            query = rotate_back(block[0:HEAD_DIM].astype(F32), cosine[batch], sine[batch])
            key = rotate_back(block[HEAD_DIM : 2 * HEAD_DIM].astype(F32), cosine[batch], sine[batch])
            for kind, part in enumerate((query.astype(BF16), key.astype(BF16), block[2 * HEAD_DIM :])):
                start = (kind * heads + head) * HEAD_DIM
                grads[batch, start : start + HEAD_DIM] = part
        terms[...] += dot_nt(tokens[batch].T, grads[batch])

    half, rows, _ = keep.shape
    side = where[0] % 2
    for at in range(half):
        for out, which in ((keep, side), (leave, 1 - side)):
            out[at] = terms[pl.ds(pl.multiple_of((2 * at + which) * rows, rows), rows), :].astype(BF16)
    own[...] = dot_nt(grads[core].T, weights[...]) + jnp.where(core == chip, 1.0, 0.0) * resid[...]
    other[...] = dot_nt(grads[1 - core].T, weights[...]).astype(BF16)


def swap(value, bit):
    count = lax.axis_size("tensor")
    return lax.ppermute(value, "tensor", [(at, at ^ bit) for at in range(count)])


def send(value, bits):
    return lax.ppermute(value, "dp", [(at, at ^ bits) for at in range(lax.axis_size("dp"))])


def exchange(blocks):
    return lax.all_to_all(blocks, "dp", 0, 0, tiled=True)


def exchange_far(blocks):
    size = lax.axis_size("dp")
    groups = [list(range(side, size, 2)) for side in range(2)]
    return lax.all_to_all(blocks, "dp", 0, 0, axis_index_groups=groups, tiled=True)


def rounded(value):
    return lax.reduce_precision(value, 8, 7)


def pick(stack, at):
    return lax.dynamic_index_in_dim(stack, at, 0, keepdims=False)


def small_group():
    return lax.axis_size("dp") in (4, 8)


def gather_far_sides(shard):
    return jnp.stack([shard] + [send(shard, bits) for bits in range(2, lax.axis_size("dp"), 2)])


def assemble_kernel(where, near, far, out):
    side = where[1]
    out[0, side] = near[0]
    out[0, 1 - side] = far[0]


def assemble(near, far):
    half, rows, columns = near.shape
    me = lax.axis_index("dp")
    where = jnp.stack([me // 2, me % 2]).astype(jnp.int32)
    block = pl.BlockSpec((1, rows, columns), lambda at, where: (at, 0, 0))
    full = pl.pallas_call(
        assemble_kernel,
        out_shape=jax.ShapeDtypeStruct((half, 2, rows, columns), near.dtype),
        grid_spec=pltpu.PrefetchScalarGridSpec(
            num_scalar_prefetch=1,
            grid=(half,),
            in_specs=[block, block],
            out_specs=pl.BlockSpec((1, 2, rows, columns), lambda at, where: (at ^ where[0], 0, 0, 0)),
        ),
        name="assemble",
    )(where, near, far)
    return full.reshape(half * 2 * rows, columns)


def after(values, *others):
    return lax.optimization_barrier((values, others))[0]


def gather_near(shard):
    half = lax.axis_size("dp") // 2
    return exchange_far(jnp.broadcast_to(shard[None], (half, *shard.shape)))


def merge_sides(near, far):
    side = lax.axis_index("dp") % 2
    half, rows, columns = near.shape
    at = lax.broadcasted_iota(jnp.int32, (half, 2, rows, columns), 1)
    return jnp.where(at == side, near[:, None], far[:, None]).reshape(half * 2 * rows, columns)


def split_terms(terms):
    size, side = lax.axis_size("dp"), lax.axis_index("dp") % 2
    *groups, rows, columns = terms.shape
    sides = terms.reshape(*groups, size // 2, 2, rows // size, columns)
    axis = len(groups)
    parts = []
    for which in (side, 1 - side):
        part = lax.dynamic_index_in_dim(sides, which, axis + 1, keepdims=False)
        parts.append(jnp.moveaxis(part, axis, 0))
    return parts


def sum_far_sides(half):
    place = lax.axis_index("dp") // 2
    total = pick(half, place).astype(F32)
    for at in range(1, half.shape[0]):
        total = total + send(pick(half, place ^ at), 2 * at).astype(F32)
    return total


def sum_sides(keep, leave):
    return (keep.astype(F32) + send(leave, 1).astype(F32)).astype(BF16)


def to_units(parts):
    size, units, shape = lax.axis_size("dp"), parts.shape[0], parts.shape[1:]
    before = jnp.zeros((FIRST_SLOT, *shape), BF16)
    after = jnp.zeros((size - FIRST_SLOT - units, *shape), BF16)
    return exchange(jnp.concatenate([before, parts, after], axis=0))


def from_units(parts, units):
    return exchange(parts)[FIRST_SLOT : FIRST_SLOT + units]


def rms_backward(grad_out, normed, inverse, gain):
    scaled = grad_out * gain
    return inverse * (scaled - normed * jnp.mean(scaled * normed, axis=-1, keepdims=True))


def body(
    inputs, seg_parent, positions, w_query, w_key, w_value, w_out, w_gate, w_up, w_down, gain_attn, gain_mlp, out_grad
):
    seg_count = lax.axis_size("dp")
    my_seg = lax.axis_index("dp")
    core = lax.axis_index("tensor") % 2
    chip = lax.axis_index("tensor") // 2
    where = jnp.stack([my_seg, core, chip]).astype(jnp.int32)
    tree_segs = min(16, seg_count)
    branch_count = tree_segs // 4
    path_len = tree_segs - 3 * branch_count + 2
    seg_len, width = inputs.shape[1:]
    scale = HEAD_DIM ** (-0.5)
    part_rows = w_query.shape[0]
    local_heads = w_query.shape[1] // HEAD_DIM
    hidden_units = w_gate.shape[1]
    head_width = local_heads * HEAD_DIM
    units = MICRO * local_heads
    last_width = 256

    small = small_group()
    columns = 3 * hidden_units + last_width
    spread_count = seg_count // 2 if small else 1
    mine_qkv, spread = whole_call(
        pack_kernel,
        where,
        [w_query, w_key, w_value, w_gate, w_up, w_down, w_out, gain_attn[None], gain_mlp[None]],
        [((part_rows, 3 * head_width), BF16), ((spread_count, part_rows, columns), BF16)],
        [],
        "pack",
    )
    if small:
        near_qkv = gather_far_sides(mine_qkv)
        far_qkv = send(near_qkv, 1)
        near = exchange_far(spread)
        full_qkv = assemble(near_qkv, far_qkv)
    else:
        full_qkv = lax.all_gather(mine_qkv, "dp", axis=0, tiled=True)
        packed = spread[0]

    tables = [rotary_tables(positions[b]) for b in range(MICRO)]
    cosines, sines = (jnp.stack([pair[at] for pair in tables]) for at in range(2))
    blocks = []
    for b in range(MICRO):
        cosine, sine = tables[b]
        heads = dot(full_qkv, inputs[b], ((0,), (1,))).reshape(3, local_heads, HEAD_DIM, seg_len)
        query = rotate(heads[0], cosine, sine).astype(BF16) * jnp.asarray(scale, BF16)
        key = rotate(heads[1], cosine, sine).astype(BF16)
        blocks.append(jnp.concatenate([query, key, heads[2].astype(BF16)], axis=1))
    blocks = jnp.concatenate(blocks, axis=0)
    unit_qkv = to_units(blocks)
    if small:
        near = after(near, blocks)
        cut = 2 * hidden_units
        far_one = send(near[:, :, cut:], 1)
        far_two = send(after(near[:, :, :cut], far_one), 1)
        near_other = swap(near, 2)
        unit_qkv, far_one, near_other = lax.optimization_barrier((unit_qkv, far_one, near_other))
        far_one_other = swap(far_one, 2)
    unit_micro = (my_seg - FIRST_SLOT) // local_heads >= 1
    chain = jnp.concatenate([jnp.where(unit_micro, seg_count, 0).reshape(1), seg_parent.reshape(-1)])
    chain = chain.astype(jnp.int32)
    unit_low, unit_full, unit_norm = attention_forward(chain, [unit_qkv], path_len)
    if small:
        unit_low, far_two, far_one_other = lax.optimization_barrier((unit_low, far_two, far_one_other))
        far_two_other = swap(far_two, 2)
        far = jnp.concatenate([far_two, far_one], axis=2)
        weights_own = merge_sides(near, far)
    attended = from_units(unit_low, units).reshape(MICRO, head_width, seg_len)

    if small:
        weights_other = merge_sides(near_other, jnp.concatenate([far_two_other, far_one_other], axis=2))
    else:
        weights_own = lax.all_gather(packed, "dp", axis=0, tiled=True)
        weights_other = swap(weights_own, 2)
    heads_own = pick(attended, chip)
    heads_other = swap(pick(attended, 1 - chip), 2)
    tokens = pick(inputs, chip).astype(F32)
    both_weights = (weights_own, weights_other)
    gates = [w[:, :hidden_units] for w in both_weights]
    ups = [w[:, hidden_units : 2 * hidden_units] for w in both_weights]
    downs = [w[:, 2 * hidden_units : 3 * hidden_units] for w in both_weights]
    lasts = [w[:, 3 * hidden_units :] for w in both_weights]
    outs = [w[:, :head_width] for w in lasts]
    gains = lasts[0][:, head_width : head_width + 2].astype(F32).T
    gain_first, gain_second = gains[0:1], gains[1:2]

    def core_sum(part):
        part = rounded(part)
        return part + swap(part.astype(BF16), 1).astype(F32)

    attn_out = core_sum(dot(heads_own, outs[0], ((0,), (1,))) + dot(heads_other, outs[1], ((0,), (1,))))
    resid_one = tokens + attn_out
    inverse_one = lax.rsqrt(jnp.mean(resid_one * resid_one, axis=-1, keepdims=True) + EPSILON)
    normed_one = resid_one * inverse_one
    hidden = normed_one * gain_first
    hidden_low = hidden.astype(BF16)
    gate = [dot_nn(hidden_low, w) for w in gates]
    up = [dot_nn(hidden_low, w) for w in ups]
    sigmoid = [jax.nn.sigmoid(g) for g in gate]
    silu = [g * s for g, s in zip(gate, sigmoid)]
    activation = [(s * u).astype(BF16) for s, u in zip(silu, up)]
    mlp = core_sum(dot_nt(activation[0], downs[0]) + dot_nt(activation[1], downs[1]))
    resid_two = hidden + mlp
    inverse_two = lax.rsqrt(jnp.mean(resid_two * resid_two, axis=-1, keepdims=True) + EPSILON)
    normed_two = resid_two * inverse_two
    result = (normed_two * gain_second).astype(BF16)

    grad_result = pick(out_grad, chip).astype(F32)
    gain_two_term = jnp.sum(grad_result * normed_two, axis=0)
    grad_resid_two = rms_backward(grad_result, normed_two, inverse_two, gain_second)
    grad_mlp_low = grad_resid_two.astype(BF16)
    grad_act = [dot_nn(grad_mlp_low, w) for w in downs]
    grad_gate_low = [
        (a * u * s * (1.0 + g * (1.0 - s))).astype(BF16) for a, u, s, g in zip(grad_act, up, sigmoid, gate)
    ]
    grad_up_low = [(a * s).astype(BF16) for a, s in zip(grad_act, silu)]
    hidden_part = (
        dot_nt(grad_gate_low[0], gates[0])
        + dot_nt(grad_up_low[0], ups[0])
        + dot_nt(grad_gate_low[1], gates[1])
        + dot_nt(grad_up_low[1], ups[1])
    )
    grad_hidden = grad_resid_two + core_sum(hidden_part)
    gain_one_term = jnp.sum(grad_hidden * normed_one, axis=0)
    grad_resid_one = rms_backward(grad_hidden, normed_one, inverse_one, gain_first)
    grad_attn_low = grad_resid_one.astype(BF16)

    grad_own = dot(outs[0], grad_attn_low, ((0,), (1,))).astype(BF16)
    grad_other = swap(dot(outs[1], grad_attn_low, ((0,), (1,))).astype(BF16), 2)
    first_chip = chip == 0
    grad_pair = jnp.stack(
        [jnp.where(first_chip, grad_own, grad_other), jnp.where(first_chip, grad_other, grad_own)]
    )
    unit_grad = to_units(grad_pair.reshape(units, HEAD_DIM, seg_len))

    down = [dot_tn(grad_mlp_low, a) for a in activation]
    wide = [
        jnp.concatenate([dot_tn(hidden_low, g).astype(BF16), dot_tn(hidden_low, u).astype(BF16)], axis=1)
        for g, u in zip(grad_gate_low, grad_up_low)
    ]
    heads_pad = [jnp.pad(rows, ((0, last_width - head_width), (0, 0))) for rows in (heads_own, heads_other)]
    term_last = []
    for rows in heads_pad:
        term = dot(grad_attn_low, rows, ((0,), (1,)))
        column = lax.broadcasted_iota(jnp.int32, term.shape, 1)
        term = jnp.where(column == head_width, gain_one_term[:, None], term)
        term_last.append(jnp.where(column == head_width + 1, gain_two_term[:, None], term).astype(BF16))
    leave_terms = jnp.concatenate([wide[1], down[1].astype(BF16), term_last[1]], axis=1)
    keep_terms = jnp.concatenate([wide[0], down[0].astype(BF16), term_last[0]], axis=1)
    got_terms = swap(leave_terms, 2)

    unit_grad = after(unit_grad, leave_terms)
    (unit_back,) = attention_backward(chain, [unit_qkv], unit_grad, unit_full, unit_norm, path_len, scale)
    back = exchange(unit_back)
    if small:
        half_terms = sum_sides(*merge_terms(where, keep_terms, after(got_terms, unit_back), [columns]))
    else:
        sum_terms = (keep_terms.astype(F32) + got_terms.astype(F32)).astype(BF16)
        shard = lax.psum_scatter(sum_terms, "dp", scatter_dimension=0, tiled=True).astype(F32)
    if small:
        side = ((seg_count // 2, part_rows, 3 * head_width), BF16)
        keep, leave, part, part_other = whole_call(
            functools.partial(tail_kernel, local_heads),
            where,
            [back, inputs, full_qkv, cosines, sines, grad_resid_one],
            [side, side, ((seg_len, width), F32), ((seg_len, width), BF16)],
            [pltpu.VMEM((MICRO, 3 * head_width, seg_len), BF16), pltpu.VMEM((width, 3 * head_width), F32)],
            "tail",
        )
        half_terms, keep, leave = lax.optimization_barrier((half_terms, keep, leave))
        shard = sum_far_sides(half_terms)
        shard_qkv = sum_far_sides(sum_sides(keep, leave))
        part = part + swap(part_other, 1).astype(F32)
    else:
        back = back[FIRST_SLOT : FIRST_SLOT + units].astype(F32).reshape(MICRO, local_heads, 3, HEAD_DIM, seg_len)
        grads = []
        for b in range(MICRO):
            query = rotate_back(back[b, :, 0], cosines[b], sines[b])
            key = rotate_back(back[b, :, 1], cosines[b], sines[b])
            grads.append(
                jnp.concatenate([query, key, back[b, :, 2]], axis=0).reshape(3 * head_width, seg_len).astype(BF16)
            )
        stack = jnp.stack(grads)
        term_qkv = sum(dot(inputs[b], grads[b], ((0,), (1,))) for b in range(MICRO)).astype(BF16)
        shard_qkv = lax.psum_scatter(term_qkv, "dp", scatter_dimension=0, tiled=True).astype(F32)
        part_own = dot(pick(stack, core), full_qkv, ((0,), (1,)))
        part_other = dot(pick(stack, 1 - core), full_qkv, ((0,), (1,)))
        part = part_own + swap(part_other.astype(BF16), 1).astype(F32) + jnp.where(core == chip, grad_resid_one, 0.0)
    part = rounded(part)
    input_mine = part + swap(part.astype(BF16), 2).astype(F32)
    shard_last = shard[:, 3 * hidden_units :]
    gain_terms = shard_last[:, head_width : head_width + 2].T

    def by_micro(own, other, first):
        return jnp.stack([jnp.where(first, own, other), jnp.where(first, other, own)])

    half = seg_len // 2
    result_half = swap(pick(result.reshape(2, half, width), core), 2)
    result_other = by_micro(result_half, swap(result_half, 1), core == 0).reshape(seg_len, width)
    return (
        by_micro(result, result_other, first_chip),
        by_micro(input_mine, swap(input_mine, 1), core == 0),
        shard_qkv[:, : head_width],
        shard_qkv[:, head_width : 2 * head_width],
        shard_qkv[:, 2 * head_width :],
        shard_last[:, :head_width].T,
        shard[:, :hidden_units],
        shard[:, hidden_units : 2 * hidden_units],
        shard[:, 2 * hidden_units : 3 * hidden_units].T,
        gain_terms[0],
        gain_terms[1],
    )


def solution(mesh):
    weight, turned = P("dp", "tensor"), P("tensor", "dp")
    rows, gain = P(None, "dp", None), P("dp")
    return jax.shard_map(
        body,
        mesh=mesh,
        in_specs=(
            rows, P(), P(None, "dp"), weight, weight, weight, turned, weight, weight, turned, gain, gain, rows,
        ),
        out_specs=(rows, rows, weight, weight, weight, turned, weight, weight, turned, gain, gain),
        check_vma=False,
    )
```

```python
import functools

import jax
import jax.numpy as jnp
from jax import lax
from jax.experimental import pallas as pl
from jax.experimental.pallas import tpu as pltpu
from jax.sharding import PartitionSpec as P

HEAD_DIM = 64
MICRO = 2
EPSILON = 1e-06
BIG_NEG = -1e30
FIRST_SLOT = 1
F32 = jnp.float32
BF16 = jnp.bfloat16


def dot(a, b, dims):
    return lax.dot_general(a, b, ((dims[0], dims[1]), ((), ())), preferred_element_type=F32)


def dot_nn(a, b):
    return dot(a, b, ((1,), (0,)))


def dot_nt(a, b):
    return dot(a, b, ((1,), (1,)))


def dot_tn(a, b):
    return dot(a, b, ((0,), (0,)))


def causal_mask(tile):
    return lax.broadcasted_iota(jnp.int32, tile, 0) <= lax.broadcasted_iota(jnp.int32, tile, 1)


def path_of(table, seg, path_len):
    path, length = [seg], jnp.int32(1)
    for _ in range(1, path_len):
        parent = table[1 + table[0] + jnp.maximum(path[-1], 0)]
        path.append(jnp.where(path[-1] >= 0, parent, -1))
        length = length + jnp.where(path[-1] >= 0, 1, 0)
    return path, length


def forward_kernel(path_len, sources, table, *refs):
    parts, (out_low, out_full, out_norm, *scratch) = refs[:sources], refs[sources:]
    qkv = scratch[0] if scratch else parts[0]
    seg = pl.program_id(0)
    seg_len = qkv.shape[2]
    if scratch:

        @pl.when(seg == 0)
        def _():
            for at, part in enumerate(parts):
                qkv[at] = part[0]

    def run(path):
        query = qkv[seg, 0:HEAD_DIM, :]
        scores = [dot_tn(qkv[source, HEAD_DIM : 2 * HEAD_DIM, :], query) for source in path]
        scores[0] = jnp.where(causal_mask((seg_len, seg_len)), scores[0], BIG_NEG)
        top = functools.reduce(jnp.maximum, [jnp.max(s, axis=0, keepdims=True) for s in scores])
        total, acc = 0.0, 0.0
        for source, score in zip(path, scores):
            probs = jnp.exp(score - top)
            total = total + jnp.sum(probs, axis=0, keepdims=True)
            acc = acc + dot_nn(qkv[source, 2 * HEAD_DIM : 3 * HEAD_DIM, :], probs.astype(BF16))
        result = acc * (1.0 / total)
        out_low[0] = result.astype(BF16)
        out_full[0] = result
        out_norm[0] = top + jnp.log(total)

    path, length = path_of(table, seg, path_len)
    for steps in range(1, path_len + 1):
        pl.when(length == steps)(functools.partial(run, path[:steps]))


def part_specs(parts):
    return [pl.BlockSpec(p.shape, lambda s, t: (0, 0, 0), pipeline_mode=pl.Buffered(1)) for p in parts]


def attention_forward(table, parts, path_len):
    rows, seg_len = parts[0].shape[1:]
    segs = sum(p.shape[0] for p in parts)
    placed = pl.BlockSpec((1, HEAD_DIM, seg_len), lambda s, t: (s, 0, 0))
    tile = pl.BlockSpec((1, HEAD_DIM, seg_len), lambda s, t: (s, 0, 0))
    line = pl.BlockSpec((1, 1, seg_len), lambda s, t: (s, 0, 0))
    scratch = [pltpu.VMEM((segs, rows, seg_len), BF16)] if len(parts) > 1 else []
    return pl.pallas_call(
        functools.partial(forward_kernel, path_len, len(parts)),
        out_shape=(
            jax.ShapeDtypeStruct((segs, HEAD_DIM, seg_len), BF16),
            jax.ShapeDtypeStruct((segs, HEAD_DIM, seg_len), F32),
            jax.ShapeDtypeStruct((segs, 1, seg_len), F32),
        ),
        grid_spec=pltpu.PrefetchScalarGridSpec(
            num_scalar_prefetch=1,
            grid=(segs,),
            in_specs=part_specs(parts),
            out_specs=[placed, tile, line],
            scratch_shapes=scratch,
        ),
        cost_estimate=pl.CostEstimate(flops=17_000_000_000, bytes_accessed=1 << 22, transcendentals=0),
        name="tree_attention_forward",
    )(table, *parts)


def backward_kernel(path_len, scale, sources, table, *refs):
    parts, (grad_ref, full_ref, norm_ref) = refs[:sources], refs[sources : sources + 3]
    outs = refs[sources + 3 : 2 * sources + 3]
    grad_query, grad_key, grad_value, partial, *scratch = refs[2 * sources + 3 :]
    qkv = scratch[0] if scratch else parts[0]
    seg = pl.program_id(0)
    segs, _, seg_len = qkv.shape

    @pl.when(seg == 0)
    def _():
        @pl.loop(0, segs)
        def _(at):
            grad_key[at] = jnp.zeros(grad_key.shape[1:], F32)
            grad_value[at] = jnp.zeros(grad_value.shape[1:], F32)

        if scratch:
            for at, part in enumerate(parts):
                qkv[at] = part[0]

    def run(path, first):
        query = qkv[seg, 0:HEAD_DIM, :]
        grad = grad_ref[0]
        delta = jnp.sum(grad.astype(F32) * full_ref[0], axis=0, keepdims=True)
        norm = norm_ref[0]
        total = 0.0 if first == 0 else partial[...]
        for step, source in enumerate(path):
            key = qkv[source, HEAD_DIM : 2 * HEAD_DIM, :]
            value = qkv[source, 2 * HEAD_DIM : 3 * HEAD_DIM, :]
            probs = jnp.exp(dot_tn(key, query) - norm)
            if first + step == 0:
                probs = jnp.where(causal_mask((seg_len, seg_len)), probs, 0.0)
            score_grad = (probs * (dot_tn(value, grad) - delta)).astype(BF16)
            total = total + dot_nn(key, score_grad)
            grad_key[source] += dot_nt(query, score_grad)
            grad_value[source] += dot_nt(grad, probs.astype(BF16))
        partial[...] = total

    path, length = path_of(table, seg, path_len)
    pl.when(length == 1)(functools.partial(run, path[:1], 0))
    pl.when(length >= 2)(functools.partial(run, path[:2], 0))
    for first in range(2, path_len):
        pl.when(length > first)(functools.partial(run, path[first : first + 1], first))
    grad_query[seg] = (partial[...] * scale).astype(BF16)

    @pl.when(seg == segs - 1)
    def _():
        first = 0
        for out in outs:

            @pl.loop(0, out.shape[0])
            def _(at, out=out, first=first):
                out[at, 0:HEAD_DIM, :] = grad_query[first + at]
                out[at, HEAD_DIM : 2 * HEAD_DIM, :] = grad_key[first + at].astype(BF16)
                out[at, 2 * HEAD_DIM : 3 * HEAD_DIM, :] = grad_value[first + at].astype(BF16)

            first += out.shape[0]


def attention_backward(table, parts, grad, full, norm, path_len, scale):
    rows, seg_len = parts[0].shape[1:]
    segs = sum(p.shape[0] for p in parts)
    placed = pl.BlockSpec((1, HEAD_DIM, seg_len), lambda s, t: (s, 0, 0))
    tile = pl.BlockSpec((1, HEAD_DIM, seg_len), lambda s, t: (s, 0, 0))
    line = pl.BlockSpec((1, 1, seg_len), lambda s, t: (s, 0, 0))
    scratch = [
        pltpu.VMEM((segs, HEAD_DIM, seg_len), BF16),
        pltpu.VMEM((segs, HEAD_DIM, seg_len), F32),
        pltpu.VMEM((segs, HEAD_DIM, seg_len), F32),
        pltpu.VMEM((HEAD_DIM, seg_len), F32),
    ]
    if len(parts) > 1:
        scratch.append(pltpu.VMEM((segs, rows, seg_len), BF16))
    return pl.pallas_call(
        functools.partial(backward_kernel, path_len, scale, len(parts)),
        out_shape=[jax.ShapeDtypeStruct(p.shape, BF16) for p in parts],
        grid_spec=pltpu.PrefetchScalarGridSpec(
            num_scalar_prefetch=1,
            grid=(segs,),
            in_specs=[*part_specs(parts), placed, tile, line],
            out_specs=part_specs(parts),
            scratch_shapes=scratch,
        ),
        compiler_params=pltpu.CompilerParams(vmem_limit_bytes=28 << 20 if segs <= 8 else None),
        name="tree_attention_backward",
    )(table, *parts, grad, full, norm)


def rotary_tables(token_pos):
    half = HEAD_DIM // 2
    frequency = 10000.0 ** (-jnp.arange(half, dtype=F32) * 2.0 / HEAD_DIM)
    angles = frequency[:, None] * token_pos.astype(F32)[None, :]
    return jnp.cos(angles), jnp.sin(angles)


def rotate(tensor, cosine, sine):
    half = HEAD_DIM // 2
    first, second = tensor[..., :half, :], tensor[..., half:, :]
    return jnp.concatenate([first * cosine - second * sine, first * sine + second * cosine], axis=-2)


def rotate_back(tensor, cosine, sine):
    half = HEAD_DIM // 2
    first, second = tensor[..., :half, :], tensor[..., half:, :]
    return jnp.concatenate([first * cosine + second * sine, second * cosine - first * sine], axis=-2)


def whole_call(kernel, where, operands, outs, scratch, name):
    def spec(shape):
        return pl.BlockSpec(shape, lambda at, where: (0,) * len(shape), pipeline_mode=pl.Buffered(1))

    return pl.pallas_call(
        kernel,
        out_shape=[jax.ShapeDtypeStruct(shape, kind) for shape, kind in outs],
        grid_spec=pltpu.PrefetchScalarGridSpec(
            num_scalar_prefetch=1,
            grid=(1,),
            in_specs=[spec(operand.shape) for operand in operands],
            out_specs=[spec(shape) for shape, _ in outs],
            scratch_shapes=scratch,
        ),
        name=name,
    )(where, *operands)


def pack_kernel(where, query, key, value, gate, up, down, out, gain_one, gain_two, mine, spread):
    mine[...] = jnp.concatenate([query[...], key[...], value[...]], axis=1)
    width, heads = gate.shape[1], out.shape[0]
    spare = jnp.zeros((out.shape[1], spread.shape[2] - 3 * width - heads - 2), BF16)
    gains = [ref[...].astype(F32).T.astype(BF16) for ref in (gain_one, gain_two)]
    last = jnp.concatenate([out[...].T, *gains, spare], axis=1)
    turned = down[...].T

    @pl.loop(0, spread.shape[0])
    def _(at):
        spread[at, :, 0:width] = gate[...]
        spread[at, :, width : 2 * width] = up[...]
        spread[at, :, 2 * width : 3 * width] = turned
        spread[at, :, 3 * width :] = last


def merge_kernel(where, own, got, *outs):
    half = own.shape[0] // 2
    side = where[0] % 2
    rows = [pl.ds(pl.multiple_of(half * which, half), half) for which in (side, 1 - side)]
    start = 0
    for keep, leave in zip(outs[0::2], outs[1::2]):
        columns = slice(start, start + keep.shape[2])
        for out, at in zip((keep, leave), rows):
            out[0] = (own[at, columns].astype(F32) + got[at, columns].astype(F32)).astype(BF16)
        start += keep.shape[2]


def merge_terms(where, own, got, groups):
    rows, columns = own.shape
    half = lax.axis_size("dp") // 2
    tile = rows // half
    block = pl.BlockSpec((tile, columns), lambda at, where: (at, 0))
    shapes = [(half, tile // 2, width) for width in groups for _ in range(2)]
    return pl.pallas_call(
        merge_kernel,
        out_shape=[jax.ShapeDtypeStruct(shape, BF16) for shape in shapes],
        grid_spec=pltpu.PrefetchScalarGridSpec(
            num_scalar_prefetch=1,
            grid=(half,),
            in_specs=[block, block],
            out_specs=[pl.BlockSpec((1, *shape[1:]), lambda at, where: (at, 0, 0)) for shape in shapes],
        ),
        compiler_params=pltpu.CompilerParams(vmem_limit_bytes=16 << 20),
        name="merge_terms",
    )(where, own, got)


def tail_kernel(heads, where, blocks, tokens, weights, cosine, sine, resid, keep, leave, own, other, grads, terms):
    core, chip = where[1], where[2]
    terms[...] = jnp.zeros_like(terms)

    @pl.loop(0, MICRO)
    def _(batch):
        for head in range(heads):
            block = blocks[FIRST_SLOT + batch * heads + head]
            query = rotate_back(block[0:HEAD_DIM].astype(F32), cosine[batch], sine[batch])
            key = rotate_back(block[HEAD_DIM : 2 * HEAD_DIM].astype(F32), cosine[batch], sine[batch])
            for kind, part in enumerate((query.astype(BF16), key.astype(BF16), block[2 * HEAD_DIM :])):
                start = (kind * heads + head) * HEAD_DIM
                grads[batch, start : start + HEAD_DIM] = part
        terms[...] += dot_nt(tokens[batch].T, grads[batch])

    half, rows, _ = keep.shape
    side = where[0] % 2
    for at in range(half):
        for out, which in ((keep, side), (leave, 1 - side)):
            out[at] = terms[pl.ds(pl.multiple_of((2 * at + which) * rows, rows), rows), :].astype(BF16)
    own[...] = dot_nt(grads[core].T, weights[...]) + jnp.where(core == chip, 1.0, 0.0) * resid[...]
    other[...] = dot_nt(grads[1 - core].T, weights[...]).astype(BF16)


def swap(value, bit):
    count = lax.axis_size("tensor")
    return lax.ppermute(value, "tensor", [(at, at ^ bit) for at in range(count)])


def send(value, bits):
    return lax.ppermute(value, "dp", [(at, at ^ bits) for at in range(lax.axis_size("dp"))])


def exchange(blocks):
    return lax.all_to_all(blocks, "dp", 0, 0, tiled=True)


def exchange_far(blocks):
    size = lax.axis_size("dp")
    groups = [list(range(side, size, 2)) for side in range(2)]
    return lax.all_to_all(blocks, "dp", 0, 0, axis_index_groups=groups, tiled=True)


def rounded(value):
    return lax.reduce_precision(value, 8, 7)


def pick(stack, at):
    return lax.dynamic_index_in_dim(stack, at, 0, keepdims=False)


def small_group():
    return lax.axis_size("dp") in (4, 8)


def gather_far_sides(shard):
    return jnp.stack([shard] + [send(shard, bits) for bits in range(2, lax.axis_size("dp"), 2)])


def assemble_kernel(where, near, far, out):
    place, side = where[0] // 2, where[0] % 2
    for at in range(near.shape[0]):
        out[place ^ at, side] = near[at]
        out[place ^ at, 1 - side] = far[at]


def assemble(near, far):
    half, rows, columns = near.shape
    where = lax.axis_index("dp").astype(jnp.int32).reshape(1)
    (full,) = whole_call(
        assemble_kernel, where, [near, far], [((half, 2, rows, columns), near.dtype)], [], "assemble"
    )
    return full.reshape(half * 2 * rows, columns)


def after(values, *others):
    return lax.optimization_barrier((values, others))[0]


def gather_near(shard):
    half = lax.axis_size("dp") // 2
    return exchange_far(jnp.broadcast_to(shard[None], (half, *shard.shape)))


def merge_sides(near, far):
    side = lax.axis_index("dp") % 2
    half, rows, columns = near.shape
    at = lax.broadcasted_iota(jnp.int32, (half, 2, rows, columns), 1)
    return jnp.where(at == side, near[:, None], far[:, None]).reshape(half * 2 * rows, columns)


def split_terms(terms):
    size, side = lax.axis_size("dp"), lax.axis_index("dp") % 2
    *groups, rows, columns = terms.shape
    sides = terms.reshape(*groups, size // 2, 2, rows // size, columns)
    axis = len(groups)
    parts = []
    for which in (side, 1 - side):
        part = lax.dynamic_index_in_dim(sides, which, axis + 1, keepdims=False)
        parts.append(jnp.moveaxis(part, axis, 0))
    return parts


def sum_far_sides(half):
    place = lax.axis_index("dp") // 2
    total = pick(half, place).astype(F32)
    for at in range(1, half.shape[0]):
        total = total + send(pick(half, place ^ at), 2 * at).astype(F32)
    return total


def sum_sides(keep, leave):
    return (keep.astype(F32) + send(leave, 1).astype(F32)).astype(BF16)


def to_units(parts):
    size, units, shape = lax.axis_size("dp"), parts.shape[0], parts.shape[1:]
    before = jnp.zeros((FIRST_SLOT, *shape), BF16)
    after = jnp.zeros((size - FIRST_SLOT - units, *shape), BF16)
    return exchange(jnp.concatenate([before, parts, after], axis=0))


def from_units(parts, units):
    return exchange(parts)[FIRST_SLOT : FIRST_SLOT + units]


def rms_backward(grad_out, normed, inverse, gain):
    scaled = grad_out * gain
    return inverse * (scaled - normed * jnp.mean(scaled * normed, axis=-1, keepdims=True))


def body(
    inputs, seg_parent, positions, w_query, w_key, w_value, w_out, w_gate, w_up, w_down, gain_attn, gain_mlp, out_grad
):
    seg_count = lax.axis_size("dp")
    my_seg = lax.axis_index("dp")
    core = lax.axis_index("tensor") % 2
    chip = lax.axis_index("tensor") // 2
    where = jnp.stack([my_seg, core, chip]).astype(jnp.int32)
    tree_segs = min(16, seg_count)
    branch_count = tree_segs // 4
    path_len = tree_segs - 3 * branch_count + 2
    seg_len, width = inputs.shape[1:]
    scale = HEAD_DIM ** (-0.5)
    part_rows = w_query.shape[0]
    local_heads = w_query.shape[1] // HEAD_DIM
    hidden_units = w_gate.shape[1]
    head_width = local_heads * HEAD_DIM
    units = MICRO * local_heads
    last_width = 256

    small = small_group()
    columns = 3 * hidden_units + last_width
    spread_count = seg_count // 2 if small else 1
    mine_qkv, spread = whole_call(
        pack_kernel,
        where,
        [w_query, w_key, w_value, w_gate, w_up, w_down, w_out, gain_attn[None], gain_mlp[None]],
        [((part_rows, 3 * head_width), BF16), ((spread_count, part_rows, columns), BF16)],
        [],
        "pack",
    )
    if small:
        near_qkv = gather_far_sides(mine_qkv)
        far_qkv = send(near_qkv, 1)
        near = exchange_far(spread)
        full_qkv = assemble(near_qkv, far_qkv)
    else:
        full_qkv = lax.all_gather(mine_qkv, "dp", axis=0, tiled=True)
        packed = spread[0]

    tables = [rotary_tables(positions[b]) for b in range(MICRO)]
    cosines, sines = (jnp.stack([pair[at] for pair in tables]) for at in range(2))
    blocks = []
    for b in range(MICRO):
        cosine, sine = tables[b]
        heads = dot(full_qkv, inputs[b], ((0,), (1,))).reshape(3, local_heads, HEAD_DIM, seg_len)
        query = rotate(heads[0], cosine, sine).astype(BF16) * jnp.asarray(scale, BF16)
        key = rotate(heads[1], cosine, sine).astype(BF16)
        blocks.append(jnp.concatenate([query, key, heads[2].astype(BF16)], axis=1))
    blocks = jnp.concatenate(blocks, axis=0)
    unit_qkv = to_units(blocks)
    if small:
        near = after(near, blocks)
        cut = 2 * hidden_units
        far_one = send(near[:, :, cut:], 1)
        far_two = send(after(near[:, :, :cut], far_one), 1)
        near_other = swap(near, 2)
        unit_qkv, far_one, near_other = lax.optimization_barrier((unit_qkv, far_one, near_other))
        far_one_other = swap(far_one, 2)
    unit_micro = (my_seg - FIRST_SLOT) // local_heads >= 1
    chain = jnp.concatenate([jnp.where(unit_micro, seg_count, 0).reshape(1), seg_parent.reshape(-1)])
    chain = chain.astype(jnp.int32)
    unit_low, unit_full, unit_norm = attention_forward(chain, [unit_qkv], path_len)
    if small:
        unit_low, far_two, far_one_other = lax.optimization_barrier((unit_low, far_two, far_one_other))
        far_two_other = swap(far_two, 2)
        far = jnp.concatenate([far_two, far_one], axis=2)
        weights_own = merge_sides(near, far)
    attended = from_units(unit_low, units).reshape(MICRO, head_width, seg_len)

    if small:
        weights_other = merge_sides(near_other, jnp.concatenate([far_two_other, far_one_other], axis=2))
    else:
        weights_own = lax.all_gather(packed, "dp", axis=0, tiled=True)
        weights_other = swap(weights_own, 2)
    heads_own = pick(attended, chip)
    heads_other = swap(pick(attended, 1 - chip), 2)
    tokens = pick(inputs, chip).astype(F32)
    both_weights = (weights_own, weights_other)
    gates = [w[:, :hidden_units] for w in both_weights]
    ups = [w[:, hidden_units : 2 * hidden_units] for w in both_weights]
    downs = [w[:, 2 * hidden_units : 3 * hidden_units] for w in both_weights]
    lasts = [w[:, 3 * hidden_units :] for w in both_weights]
    outs = [w[:, :head_width] for w in lasts]
    gains = lasts[0][:, head_width : head_width + 2].astype(F32).T
    gain_first, gain_second = gains[0:1], gains[1:2]

    def core_sum(part):
        part = rounded(part)
        return part + swap(part.astype(BF16), 1).astype(F32)

    attn_out = core_sum(dot(heads_own, outs[0], ((0,), (1,))) + dot(heads_other, outs[1], ((0,), (1,))))
    resid_one = tokens + attn_out
    inverse_one = lax.rsqrt(jnp.mean(resid_one * resid_one, axis=-1, keepdims=True) + EPSILON)
    normed_one = resid_one * inverse_one
    hidden = normed_one * gain_first
    hidden_low = hidden.astype(BF16)
    gate = [dot_nn(hidden_low, w) for w in gates]
    up = [dot_nn(hidden_low, w) for w in ups]
    sigmoid = [jax.nn.sigmoid(g) for g in gate]
    silu = [g * s for g, s in zip(gate, sigmoid)]
    activation = [(s * u).astype(BF16) for s, u in zip(silu, up)]
    mlp = core_sum(dot_nt(activation[0], downs[0]) + dot_nt(activation[1], downs[1]))
    resid_two = hidden + mlp
    inverse_two = lax.rsqrt(jnp.mean(resid_two * resid_two, axis=-1, keepdims=True) + EPSILON)
    normed_two = resid_two * inverse_two
    result = (normed_two * gain_second).astype(BF16)

    grad_result = pick(out_grad, chip).astype(F32)
    gain_two_term = jnp.sum(grad_result * normed_two, axis=0)
    grad_resid_two = rms_backward(grad_result, normed_two, inverse_two, gain_second)
    grad_mlp_low = grad_resid_two.astype(BF16)
    grad_act = [dot_nn(grad_mlp_low, w) for w in downs]
    grad_gate_low = [
        (a * u * s * (1.0 + g * (1.0 - s))).astype(BF16) for a, u, s, g in zip(grad_act, up, sigmoid, gate)
    ]
    grad_up_low = [(a * s).astype(BF16) for a, s in zip(grad_act, silu)]
    hidden_part = (
        dot_nt(grad_gate_low[0], gates[0])
        + dot_nt(grad_up_low[0], ups[0])
        + dot_nt(grad_gate_low[1], gates[1])
        + dot_nt(grad_up_low[1], ups[1])
    )
    grad_hidden = grad_resid_two + core_sum(hidden_part)
    gain_one_term = jnp.sum(grad_hidden * normed_one, axis=0)
    grad_resid_one = rms_backward(grad_hidden, normed_one, inverse_one, gain_first)
    grad_attn_low = grad_resid_one.astype(BF16)

    grad_own = dot(outs[0], grad_attn_low, ((0,), (1,))).astype(BF16)
    grad_other = swap(dot(outs[1], grad_attn_low, ((0,), (1,))).astype(BF16), 2)
    first_chip = chip == 0
    grad_pair = jnp.stack(
        [jnp.where(first_chip, grad_own, grad_other), jnp.where(first_chip, grad_other, grad_own)]
    )
    unit_grad = to_units(grad_pair.reshape(units, HEAD_DIM, seg_len))

    down = [dot_tn(grad_mlp_low, a) for a in activation]
    wide = [
        jnp.concatenate([dot_tn(hidden_low, g).astype(BF16), dot_tn(hidden_low, u).astype(BF16)], axis=1)
        for g, u in zip(grad_gate_low, grad_up_low)
    ]
    heads_pad = [jnp.pad(rows, ((0, last_width - head_width), (0, 0))) for rows in (heads_own, heads_other)]
    term_last = []
    for rows in heads_pad:
        term = dot(grad_attn_low, rows, ((0,), (1,)))
        column = lax.broadcasted_iota(jnp.int32, term.shape, 1)
        term = jnp.where(column == head_width, gain_one_term[:, None], term)
        term_last.append(jnp.where(column == head_width + 1, gain_two_term[:, None], term).astype(BF16))
    leave_terms = jnp.concatenate([wide[1], down[1].astype(BF16), term_last[1]], axis=1)
    keep_terms = jnp.concatenate([wide[0], down[0].astype(BF16), term_last[0]], axis=1)
    got_terms = swap(leave_terms, 2)

    unit_grad = after(unit_grad, leave_terms, result)
    (unit_back,) = attention_backward(chain, [unit_qkv], unit_grad, unit_full, unit_norm, path_len, scale)
    back = exchange(unit_back)
    if small:
        half_terms = sum_sides(*merge_terms(where, keep_terms, after(got_terms, unit_back), [columns]))
    else:
        sum_terms = (keep_terms.astype(F32) + got_terms.astype(F32)).astype(BF16)
        shard = lax.psum_scatter(sum_terms, "dp", scatter_dimension=0, tiled=True).astype(F32)
    if small:
        side = ((seg_count // 2, part_rows, 3 * head_width), BF16)
        keep, leave, part, part_other = whole_call(
            functools.partial(tail_kernel, local_heads),
            where,
            [back, inputs, full_qkv, cosines, sines, grad_resid_one],
            [side, side, ((seg_len, width), F32), ((seg_len, width), BF16)],
            [pltpu.VMEM((MICRO, 3 * head_width, seg_len), BF16), pltpu.VMEM((width, 3 * head_width), F32)],
            "tail",
        )
        half_terms, keep, leave = lax.optimization_barrier((half_terms, keep, leave))
        shard = sum_far_sides(half_terms)
        shard_qkv = sum_far_sides(sum_sides(keep, leave))
        part = part + swap(part_other, 1).astype(F32)
    else:
        back = back[FIRST_SLOT : FIRST_SLOT + units].astype(F32).reshape(MICRO, local_heads, 3, HEAD_DIM, seg_len)
        grads = []
        for b in range(MICRO):
            query = rotate_back(back[b, :, 0], cosines[b], sines[b])
            key = rotate_back(back[b, :, 1], cosines[b], sines[b])
            grads.append(
                jnp.concatenate([query, key, back[b, :, 2]], axis=0).reshape(3 * head_width, seg_len).astype(BF16)
            )
        stack = jnp.stack(grads)
        term_qkv = sum(dot(inputs[b], grads[b], ((0,), (1,))) for b in range(MICRO)).astype(BF16)
        shard_qkv = lax.psum_scatter(term_qkv, "dp", scatter_dimension=0, tiled=True).astype(F32)
        part_own = dot(pick(stack, core), full_qkv, ((0,), (1,)))
        part_other = dot(pick(stack, 1 - core), full_qkv, ((0,), (1,)))
        part = part_own + swap(part_other.astype(BF16), 1).astype(F32) + jnp.where(core == chip, grad_resid_one, 0.0)
    part = rounded(part)
    input_mine = part + swap(part.astype(BF16), 2).astype(F32)
    shard_last = shard[:, 3 * hidden_units :]
    gain_terms = shard_last[:, head_width : head_width + 2].T

    def by_micro(own, other, first):
        return jnp.stack([jnp.where(first, own, other), jnp.where(first, other, own)])

    half = seg_len // 2
    result_half = swap(pick(result.reshape(2, half, width), core), 2)
    result_other = by_micro(result_half, swap(result_half, 1), core == 0).reshape(seg_len, width)
    return (
        by_micro(result, result_other, first_chip),
        by_micro(input_mine, swap(input_mine, 1), core == 0),
        shard_qkv[:, : head_width],
        shard_qkv[:, head_width : 2 * head_width],
        shard_qkv[:, 2 * head_width :],
        shard_last[:, :head_width].T,
        shard[:, :hidden_units],
        shard[:, hidden_units : 2 * hidden_units],
        shard[:, 2 * hidden_units : 3 * hidden_units].T,
        gain_terms[0],
        gain_terms[1],
    )


def solution(mesh):
    weight, turned = P("dp", "tensor"), P("tensor", "dp")
    rows, gain = P(None, "dp", None), P("dp")
    return jax.shard_map(
        body,
        mesh=mesh,
        in_specs=(
            rows, P(), P(None, "dp"), weight, weight, weight, turned, weight, weight, turned, gain, gain, rows,
        ),
        out_specs=(rows, rows, weight, weight, weight, turned, weight, weight, turned, gain, gain),
        check_vma=False,
    )
```

```python
import functools

import jax
import jax.numpy as jnp
from jax import lax
from jax.experimental import pallas as pl
from jax.experimental.pallas import tpu as pltpu
from jax.sharding import PartitionSpec as P

HEAD_DIM = 64
MICRO = 2
EPSILON = 1e-06
BIG_NEG = -1e30
FIRST_SLOT = 1
F32 = jnp.float32
BF16 = jnp.bfloat16


def dot(a, b, dims):
    return lax.dot_general(a, b, ((dims[0], dims[1]), ((), ())), preferred_element_type=F32)


def dot_nn(a, b):
    return dot(a, b, ((1,), (0,)))


def dot_nt(a, b):
    return dot(a, b, ((1,), (1,)))


def dot_tn(a, b):
    return dot(a, b, ((0,), (0,)))


def causal_mask(tile):
    return lax.broadcasted_iota(jnp.int32, tile, 0) <= lax.broadcasted_iota(jnp.int32, tile, 1)


def path_of(table, seg, path_len):
    path, length = [seg], jnp.int32(1)
    for _ in range(1, path_len):
        parent = table[1 + table[0] + jnp.maximum(path[-1], 0)]
        path.append(jnp.where(path[-1] >= 0, parent, -1))
        length = length + jnp.where(path[-1] >= 0, 1, 0)
    return path, length


def forward_kernel(path_len, sources, table, *refs):
    parts, (out_low, out_full, out_norm, *scratch) = refs[:sources], refs[sources:]
    qkv = scratch[0] if scratch else parts[0]
    seg = pl.program_id(0)
    seg_len = qkv.shape[2]
    if scratch:

        @pl.when(seg == 0)
        def _():
            for at, part in enumerate(parts):
                qkv[at] = part[0]

    def run(path):
        query = qkv[seg, 0:HEAD_DIM, :]
        scores = [dot_tn(qkv[source, HEAD_DIM : 2 * HEAD_DIM, :], query) for source in path]
        scores[0] = jnp.where(causal_mask((seg_len, seg_len)), scores[0], BIG_NEG)
        top = functools.reduce(jnp.maximum, [jnp.max(s, axis=0, keepdims=True) for s in scores])
        total, acc = 0.0, 0.0
        for source, score in zip(path, scores):
            probs = jnp.exp(score - top)
            total = total + jnp.sum(probs, axis=0, keepdims=True)
            acc = acc + dot_nn(qkv[source, 2 * HEAD_DIM : 3 * HEAD_DIM, :], probs.astype(BF16))
        result = acc * (1.0 / total)
        out_low[0] = result.astype(BF16)
        out_full[0] = result
        out_norm[0] = top + jnp.log(total)

    path, length = path_of(table, seg, path_len)
    for steps in range(1, path_len + 1):
        pl.when(length == steps)(functools.partial(run, path[:steps]))


def part_specs(parts):
    return [pl.BlockSpec(p.shape, lambda s, t: (0, 0, 0), pipeline_mode=pl.Buffered(1)) for p in parts]


def attention_forward(table, parts, path_len):
    rows, seg_len = parts[0].shape[1:]
    segs = sum(p.shape[0] for p in parts)
    placed = pl.BlockSpec((1, HEAD_DIM, seg_len), lambda s, t: (s, 0, 0))
    tile = pl.BlockSpec((1, HEAD_DIM, seg_len), lambda s, t: (s, 0, 0))
    line = pl.BlockSpec((1, 1, seg_len), lambda s, t: (s, 0, 0))
    scratch = [pltpu.VMEM((segs, rows, seg_len), BF16)] if len(parts) > 1 else []
    return pl.pallas_call(
        functools.partial(forward_kernel, path_len, len(parts)),
        out_shape=(
            jax.ShapeDtypeStruct((segs, HEAD_DIM, seg_len), BF16),
            jax.ShapeDtypeStruct((segs, HEAD_DIM, seg_len), F32),
            jax.ShapeDtypeStruct((segs, 1, seg_len), F32),
        ),
        grid_spec=pltpu.PrefetchScalarGridSpec(
            num_scalar_prefetch=1,
            grid=(segs,),
            in_specs=part_specs(parts),
            out_specs=[placed, tile, line],
            scratch_shapes=scratch,
        ),
        cost_estimate=pl.CostEstimate(flops=17_000_000_000, bytes_accessed=1 << 22, transcendentals=0),
        name="tree_attention_forward",
    )(table, *parts)


def backward_kernel(path_len, scale, sources, table, *refs):
    parts, (grad_ref, full_ref, norm_ref) = refs[:sources], refs[sources : sources + 3]
    outs = refs[sources + 3 : 2 * sources + 3]
    grad_query, grad_key, grad_value, partial, *scratch = refs[2 * sources + 3 :]
    qkv = scratch[0] if scratch else parts[0]
    seg = pl.program_id(0)
    segs, _, seg_len = qkv.shape

    @pl.when(seg == 0)
    def _():
        @pl.loop(0, segs)
        def _(at):
            grad_key[at] = jnp.zeros(grad_key.shape[1:], F32)
            grad_value[at] = jnp.zeros(grad_value.shape[1:], F32)

        if scratch:
            for at, part in enumerate(parts):
                qkv[at] = part[0]

    def run(path, first):
        query = qkv[seg, 0:HEAD_DIM, :]
        grad = grad_ref[0]
        delta = jnp.sum(grad.astype(F32) * full_ref[0], axis=0, keepdims=True)
        norm = norm_ref[0]
        total = 0.0 if first == 0 else partial[...]
        for step, source in enumerate(path):
            key = qkv[source, HEAD_DIM : 2 * HEAD_DIM, :]
            value = qkv[source, 2 * HEAD_DIM : 3 * HEAD_DIM, :]
            probs = jnp.exp(dot_tn(key, query) - norm)
            if first + step == 0:
                probs = jnp.where(causal_mask((seg_len, seg_len)), probs, 0.0)
            score_grad = (probs * (dot_tn(value, grad) - delta)).astype(BF16)
            total = total + dot_nn(key, score_grad)
            grad_key[source] += dot_nt(query, score_grad)
            grad_value[source] += dot_nt(grad, probs.astype(BF16))
        partial[...] = total

    path, length = path_of(table, seg, path_len)
    pl.when(length == 1)(functools.partial(run, path[:1], 0))
    pl.when(length >= 2)(functools.partial(run, path[:2], 0))
    for first in range(2, path_len):
        pl.when(length > first)(functools.partial(run, path[first : first + 1], first))
    grad_query[seg] = (partial[...] * scale).astype(BF16)

    @pl.when(seg == segs - 1)
    def _():
        first = 0
        for out in outs:

            @pl.loop(0, out.shape[0])
            def _(at, out=out, first=first):
                out[at, 0:HEAD_DIM, :] = grad_query[first + at]
                out[at, HEAD_DIM : 2 * HEAD_DIM, :] = grad_key[first + at].astype(BF16)
                out[at, 2 * HEAD_DIM : 3 * HEAD_DIM, :] = grad_value[first + at].astype(BF16)

            first += out.shape[0]


def attention_backward(table, parts, grad, full, norm, path_len, scale):
    rows, seg_len = parts[0].shape[1:]
    segs = sum(p.shape[0] for p in parts)
    placed = pl.BlockSpec((1, HEAD_DIM, seg_len), lambda s, t: (s, 0, 0))
    tile = pl.BlockSpec((1, HEAD_DIM, seg_len), lambda s, t: (s, 0, 0))
    line = pl.BlockSpec((1, 1, seg_len), lambda s, t: (s, 0, 0))
    scratch = [
        pltpu.VMEM((segs, HEAD_DIM, seg_len), BF16),
        pltpu.VMEM((segs, HEAD_DIM, seg_len), F32),
        pltpu.VMEM((segs, HEAD_DIM, seg_len), F32),
        pltpu.VMEM((HEAD_DIM, seg_len), F32),
    ]
    if len(parts) > 1:
        scratch.append(pltpu.VMEM((segs, rows, seg_len), BF16))
    return pl.pallas_call(
        functools.partial(backward_kernel, path_len, scale, len(parts)),
        out_shape=[jax.ShapeDtypeStruct(p.shape, BF16) for p in parts],
        grid_spec=pltpu.PrefetchScalarGridSpec(
            num_scalar_prefetch=1,
            grid=(segs,),
            in_specs=[*part_specs(parts), placed, tile, line],
            out_specs=part_specs(parts),
            scratch_shapes=scratch,
        ),
        compiler_params=pltpu.CompilerParams(vmem_limit_bytes=28 << 20 if segs <= 8 else None),
        name="tree_attention_backward",
    )(table, *parts, grad, full, norm)


def rotary_tables(token_pos):
    half = HEAD_DIM // 2
    frequency = 10000.0 ** (-jnp.arange(half, dtype=F32) * 2.0 / HEAD_DIM)
    angles = frequency[:, None] * token_pos.astype(F32)[None, :]
    return jnp.cos(angles), jnp.sin(angles)


def rotate(tensor, cosine, sine):
    half = HEAD_DIM // 2
    first, second = tensor[..., :half, :], tensor[..., half:, :]
    return jnp.concatenate([first * cosine - second * sine, first * sine + second * cosine], axis=-2)


def rotate_back(tensor, cosine, sine):
    half = HEAD_DIM // 2
    first, second = tensor[..., :half, :], tensor[..., half:, :]
    return jnp.concatenate([first * cosine + second * sine, second * cosine - first * sine], axis=-2)


def whole_call(kernel, where, operands, outs, scratch, name):
    def spec(shape):
        return pl.BlockSpec(shape, lambda at, where: (0,) * len(shape), pipeline_mode=pl.Buffered(1))

    return pl.pallas_call(
        kernel,
        out_shape=[jax.ShapeDtypeStruct(shape, kind) for shape, kind in outs],
        grid_spec=pltpu.PrefetchScalarGridSpec(
            num_scalar_prefetch=1,
            grid=(1,),
            in_specs=[spec(operand.shape) for operand in operands],
            out_specs=[spec(shape) for shape, _ in outs],
            scratch_shapes=scratch,
        ),
        name=name,
    )(where, *operands)


def pack_kernel(where, query, key, value, gate, up, down, out, gain_one, gain_two, mine, spread):
    mine[...] = jnp.concatenate([query[...], key[...], value[...]], axis=1)
    width, heads = gate.shape[1], out.shape[0]
    spare = jnp.zeros((out.shape[1], spread.shape[2] - 3 * width - heads - 2), BF16)
    gains = [ref[...].astype(F32).T.astype(BF16) for ref in (gain_one, gain_two)]
    last = jnp.concatenate([out[...].T, *gains, spare], axis=1)
    turned = down[...].T

    @pl.loop(0, spread.shape[0])
    def _(at):
        spread[at, :, 0:width] = gate[...]
        spread[at, :, width : 2 * width] = up[...]
        spread[at, :, 2 * width : 3 * width] = turned
        spread[at, :, 3 * width :] = last


def merge_kernel(where, own, got, *outs):
    half = own.shape[0] // 2
    side = where[0] % 2
    rows = [pl.ds(pl.multiple_of(half * which, half), half) for which in (side, 1 - side)]
    start = 0
    for keep, leave in zip(outs[0::2], outs[1::2]):
        columns = slice(start, start + keep.shape[2])
        for out, at in zip((keep, leave), rows):
            out[0] = (own[at, columns].astype(F32) + got[at, columns].astype(F32)).astype(BF16)
        start += keep.shape[2]


def merge_terms(where, own, got, groups):
    rows, columns = own.shape
    half = lax.axis_size("dp") // 2
    tile = rows // half
    block = pl.BlockSpec((tile, columns), lambda at, where: (at, 0))
    shapes = [(half, tile // 2, width) for width in groups for _ in range(2)]
    return pl.pallas_call(
        merge_kernel,
        out_shape=[jax.ShapeDtypeStruct(shape, BF16) for shape in shapes],
        grid_spec=pltpu.PrefetchScalarGridSpec(
            num_scalar_prefetch=1,
            grid=(half,),
            in_specs=[block, block],
            out_specs=[pl.BlockSpec((1, *shape[1:]), lambda at, where: (at, 0, 0)) for shape in shapes],
        ),
        compiler_params=pltpu.CompilerParams(vmem_limit_bytes=16 << 20),
        name="merge_terms",
    )(where, own, got)


def tail_kernel(heads, where, blocks, tokens, weights, cosine, sine, resid, keep, leave, own, other, grads, terms):
    core, chip = where[1], where[2]
    terms[...] = jnp.zeros_like(terms)

    @pl.loop(0, MICRO)
    def _(batch):
        for head in range(heads):
            block = blocks[FIRST_SLOT + batch * heads + head]
            query = rotate_back(block[0:HEAD_DIM].astype(F32), cosine[batch], sine[batch])
            key = rotate_back(block[HEAD_DIM : 2 * HEAD_DIM].astype(F32), cosine[batch], sine[batch])
            for kind, part in enumerate((query.astype(BF16), key.astype(BF16), block[2 * HEAD_DIM :])):
                start = (kind * heads + head) * HEAD_DIM
                grads[batch, start : start + HEAD_DIM] = part
        terms[...] += dot_nt(tokens[batch].T, grads[batch])

    half, rows, _ = keep.shape
    side = where[0] % 2
    for at in range(half):
        for out, which in ((keep, side), (leave, 1 - side)):
            out[at] = terms[pl.ds(pl.multiple_of((2 * at + which) * rows, rows), rows), :].astype(BF16)
    own[...] = dot_nt(grads[core].T, weights[...]) + jnp.where(core == chip, 1.0, 0.0) * resid[...]
    other[...] = dot_nt(grads[1 - core].T, weights[...]).astype(BF16)


def swap(value, bit):
    count = lax.axis_size("tensor")
    return lax.ppermute(value, "tensor", [(at, at ^ bit) for at in range(count)])


def send(value, bits):
    return lax.ppermute(value, "dp", [(at, at ^ bits) for at in range(lax.axis_size("dp"))])


def exchange(blocks):
    return lax.all_to_all(blocks, "dp", 0, 0, tiled=True)


def exchange_far(blocks):
    size = lax.axis_size("dp")
    groups = [list(range(side, size, 2)) for side in range(2)]
    return lax.all_to_all(blocks, "dp", 0, 0, axis_index_groups=groups, tiled=True)


def rounded(value):
    return lax.reduce_precision(value, 8, 7)


def pick(stack, at):
    return lax.dynamic_index_in_dim(stack, at, 0, keepdims=False)


def small_group():
    return lax.axis_size("dp") in (4, 8)


def gather_far_sides(shard):
    return jnp.stack([shard] + [send(shard, bits) for bits in range(2, lax.axis_size("dp"), 2)])


def assemble_kernel(where, near, far, out):
    place, side = where[0] // 2, where[0] % 2
    for at in range(near.shape[0]):
        out[place ^ at, side] = near[at]
        out[place ^ at, 1 - side] = far[at]


def assemble(near, far):
    half, rows, columns = near.shape
    where = lax.axis_index("dp").astype(jnp.int32).reshape(1)
    (full,) = whole_call(
        assemble_kernel, where, [near, far], [((half, 2, rows, columns), near.dtype)], [], "assemble"
    )
    return full.reshape(half * 2 * rows, columns)


def after(values, *others):
    return lax.optimization_barrier((values, others))[0]


def gather_near(shard):
    half = lax.axis_size("dp") // 2
    return exchange_far(jnp.broadcast_to(shard[None], (half, *shard.shape)))


def merge_sides(near, far):
    side = lax.axis_index("dp") % 2
    half, rows, columns = near.shape
    at = lax.broadcasted_iota(jnp.int32, (half, 2, rows, columns), 1)
    return jnp.where(at == side, near[:, None], far[:, None]).reshape(half * 2 * rows, columns)


def split_terms(terms):
    size, side = lax.axis_size("dp"), lax.axis_index("dp") % 2
    *groups, rows, columns = terms.shape
    sides = terms.reshape(*groups, size // 2, 2, rows // size, columns)
    axis = len(groups)
    parts = []
    for which in (side, 1 - side):
        part = lax.dynamic_index_in_dim(sides, which, axis + 1, keepdims=False)
        parts.append(jnp.moveaxis(part, axis, 0))
    return parts


def sum_far_sides(half):
    place = lax.axis_index("dp") // 2
    total = pick(half, place).astype(F32)
    for at in range(1, half.shape[0]):
        total = total + send(pick(half, place ^ at), 2 * at).astype(F32)
    return total


def sum_sides(keep, leave):
    return (keep.astype(F32) + send(leave, 1).astype(F32)).astype(BF16)


def to_units(parts):
    size, units, shape = lax.axis_size("dp"), parts.shape[0], parts.shape[1:]
    before = jnp.zeros((FIRST_SLOT, *shape), BF16)
    after = jnp.zeros((size - FIRST_SLOT - units, *shape), BF16)
    return exchange(jnp.concatenate([before, parts, after], axis=0))


def from_units(parts, units):
    return exchange(parts)[FIRST_SLOT : FIRST_SLOT + units]


def rms_backward(grad_out, normed, inverse, gain):
    scaled = grad_out * gain
    return inverse * (scaled - normed * jnp.mean(scaled * normed, axis=-1, keepdims=True))


def body(
    inputs, seg_parent, positions, w_query, w_key, w_value, w_out, w_gate, w_up, w_down, gain_attn, gain_mlp, out_grad
):
    seg_count = lax.axis_size("dp")
    my_seg = lax.axis_index("dp")
    core = lax.axis_index("tensor") % 2
    chip = lax.axis_index("tensor") // 2
    where = jnp.stack([my_seg, core, chip]).astype(jnp.int32)
    tree_segs = min(16, seg_count)
    branch_count = tree_segs // 4
    path_len = tree_segs - 3 * branch_count + 2
    seg_len, width = inputs.shape[1:]
    scale = HEAD_DIM ** (-0.5)
    part_rows = w_query.shape[0]
    local_heads = w_query.shape[1] // HEAD_DIM
    hidden_units = w_gate.shape[1]
    head_width = local_heads * HEAD_DIM
    units = MICRO * local_heads
    last_width = 256

    small = small_group()
    columns = 3 * hidden_units + last_width
    spread_count = seg_count // 2 if small else 1
    mine_qkv, spread = whole_call(
        pack_kernel,
        where,
        [w_query, w_key, w_value, w_gate, w_up, w_down, w_out, gain_attn[None], gain_mlp[None]],
        [((part_rows, 3 * head_width), BF16), ((spread_count, part_rows, columns), BF16)],
        [],
        "pack",
    )
    if small:
        near_qkv = gather_far_sides(mine_qkv)
        far_qkv = send(near_qkv, 1)
        near = exchange_far(spread)
        full_qkv = assemble(near_qkv, far_qkv)
    else:
        full_qkv = lax.all_gather(mine_qkv, "dp", axis=0, tiled=True)
        packed = spread[0]

    tables = [rotary_tables(positions[b]) for b in range(MICRO)]
    cosines, sines = (jnp.stack([pair[at] for pair in tables]) for at in range(2))
    blocks = []
    for b in range(MICRO):
        cosine, sine = tables[b]
        heads = dot(full_qkv, inputs[b], ((0,), (1,))).reshape(3, local_heads, HEAD_DIM, seg_len)
        query = rotate(heads[0], cosine, sine).astype(BF16) * jnp.asarray(scale, BF16)
        key = rotate(heads[1], cosine, sine).astype(BF16)
        blocks.append(jnp.concatenate([query, key, heads[2].astype(BF16)], axis=1))
    blocks = jnp.concatenate(blocks, axis=0)
    unit_qkv = to_units(blocks)
    if small:
        near = after(near, blocks)
        cut = 2 * hidden_units
        far_one = send(near[:, :, cut:], 1)
        far_two = send(after(near[:, :, :cut], far_one), 1)
        near_other = swap(near, 2)
        unit_qkv, far_one, near_other = lax.optimization_barrier((unit_qkv, far_one, near_other))
        far_one_other = swap(far_one, 2)
    unit_micro = (my_seg - FIRST_SLOT) // local_heads >= 1
    chain = jnp.concatenate([jnp.where(unit_micro, seg_count, 0).reshape(1), seg_parent.reshape(-1)])
    chain = chain.astype(jnp.int32)
    unit_low, unit_full, unit_norm = attention_forward(chain, [unit_qkv], path_len)
    if small:
        unit_low, far_two, far_one_other = lax.optimization_barrier((unit_low, far_two, far_one_other))
        far_two_other = swap(far_two, 2)
        far = jnp.concatenate([far_two, far_one], axis=2)
        weights_own = merge_sides(near, far)
    attended = from_units(unit_low, units).reshape(MICRO, head_width, seg_len)

    if small:
        weights_other = merge_sides(near_other, jnp.concatenate([far_two_other, far_one_other], axis=2))
    else:
        weights_own = lax.all_gather(packed, "dp", axis=0, tiled=True)
        weights_other = swap(weights_own, 2)
    heads_own = pick(attended, chip)
    heads_other = swap(pick(attended, 1 - chip), 2)
    tokens = pick(inputs, chip).astype(F32)
    both_weights = (weights_own, weights_other)
    gates = [w[:, :hidden_units] for w in both_weights]
    ups = [w[:, hidden_units : 2 * hidden_units] for w in both_weights]
    downs = [w[:, 2 * hidden_units : 3 * hidden_units] for w in both_weights]
    lasts = [w[:, 3 * hidden_units :] for w in both_weights]
    outs = [w[:, :head_width] for w in lasts]
    gains = lasts[0][:, head_width : head_width + 2].astype(F32).T
    gain_first, gain_second = gains[0:1], gains[1:2]

    def core_sum(part):
        part = rounded(part)
        return part + swap(part.astype(BF16), 1).astype(F32)

    attn_out = core_sum(dot(heads_own, outs[0], ((0,), (1,))) + dot(heads_other, outs[1], ((0,), (1,))))
    resid_one = tokens + attn_out
    inverse_one = lax.rsqrt(jnp.mean(resid_one * resid_one, axis=-1, keepdims=True) + EPSILON)
    normed_one = resid_one * inverse_one
    hidden = normed_one * gain_first
    hidden_low = hidden.astype(BF16)
    gate = [dot_nn(hidden_low, w) for w in gates]
    up = [dot_nn(hidden_low, w) for w in ups]
    sigmoid = [jax.nn.sigmoid(g) for g in gate]
    silu = [g * s for g, s in zip(gate, sigmoid)]
    activation = [(s * u).astype(BF16) for s, u in zip(silu, up)]
    mlp = core_sum(dot_nt(activation[0], downs[0]) + dot_nt(activation[1], downs[1]))
    resid_two = hidden + mlp
    inverse_two = lax.rsqrt(jnp.mean(resid_two * resid_two, axis=-1, keepdims=True) + EPSILON)
    normed_two = resid_two * inverse_two
    result = (normed_two * gain_second).astype(BF16)

    grad_result = pick(out_grad, chip).astype(F32)
    gain_two_term = jnp.sum(grad_result * normed_two, axis=0)
    grad_resid_two = rms_backward(grad_result, normed_two, inverse_two, gain_second)
    grad_mlp_low = grad_resid_two.astype(BF16)
    grad_act = [dot_nn(grad_mlp_low, w) for w in downs]
    grad_gate_low = [
        (a * u * s * (1.0 + g * (1.0 - s))).astype(BF16) for a, u, s, g in zip(grad_act, up, sigmoid, gate)
    ]
    grad_up_low = [(a * s).astype(BF16) for a, s in zip(grad_act, silu)]
    hidden_part = (
        dot_nt(grad_gate_low[0], gates[0])
        + dot_nt(grad_up_low[0], ups[0])
        + dot_nt(grad_gate_low[1], gates[1])
        + dot_nt(grad_up_low[1], ups[1])
    )
    grad_hidden = grad_resid_two + core_sum(hidden_part)
    gain_one_term = jnp.sum(grad_hidden * normed_one, axis=0)
    grad_resid_one = rms_backward(grad_hidden, normed_one, inverse_one, gain_first)
    grad_attn_low = grad_resid_one.astype(BF16)

    grad_own = dot(outs[0], grad_attn_low, ((0,), (1,))).astype(BF16)
    grad_other = swap(dot(outs[1], grad_attn_low, ((0,), (1,))).astype(BF16), 2)
    first_chip = chip == 0
    grad_pair = jnp.stack(
        [jnp.where(first_chip, grad_own, grad_other), jnp.where(first_chip, grad_other, grad_own)]
    )
    unit_grad = to_units(grad_pair.reshape(units, HEAD_DIM, seg_len))

    down = [dot_tn(grad_mlp_low, a) for a in activation]
    wide = [
        jnp.concatenate([dot_tn(hidden_low, g).astype(BF16), dot_tn(hidden_low, u).astype(BF16)], axis=1)
        for g, u in zip(grad_gate_low, grad_up_low)
    ]
    heads_pad = [jnp.pad(rows, ((0, last_width - head_width), (0, 0))) for rows in (heads_own, heads_other)]
    term_last = []
    for rows in heads_pad:
        term = dot(grad_attn_low, rows, ((0,), (1,)))
        column = lax.broadcasted_iota(jnp.int32, term.shape, 1)
        term = jnp.where(column == head_width, gain_one_term[:, None], term)
        term_last.append(jnp.where(column == head_width + 1, gain_two_term[:, None], term).astype(BF16))
    leave_terms = jnp.concatenate([wide[1], down[1].astype(BF16), term_last[1]], axis=1)
    keep_terms = jnp.concatenate([wide[0], down[0].astype(BF16), term_last[0]], axis=1)
    got_terms = swap(after(leave_terms, grad_other), 2)

    unit_grad = after(unit_grad, leave_terms, result)
    (unit_back,) = attention_backward(chain, [unit_qkv], unit_grad, unit_full, unit_norm, path_len, scale)
    back = exchange(unit_back)
    if small:
        half_terms = sum_sides(*merge_terms(where, keep_terms, after(got_terms, unit_back), [columns]))
    else:
        sum_terms = (keep_terms.astype(F32) + got_terms.astype(F32)).astype(BF16)
        shard = lax.psum_scatter(sum_terms, "dp", scatter_dimension=0, tiled=True).astype(F32)
    if small:
        side = ((seg_count // 2, part_rows, 3 * head_width), BF16)
        keep, leave, part, part_other = whole_call(
            functools.partial(tail_kernel, local_heads),
            where,
            [back, inputs, full_qkv, cosines, sines, grad_resid_one],
            [side, side, ((seg_len, width), F32), ((seg_len, width), BF16)],
            [pltpu.VMEM((MICRO, 3 * head_width, seg_len), BF16), pltpu.VMEM((width, 3 * head_width), F32)],
            "tail",
        )
        half_terms, keep, leave = lax.optimization_barrier((half_terms, keep, leave))
        shard = sum_far_sides(half_terms)
        shard_qkv = sum_far_sides(sum_sides(keep, leave))
        part = part + swap(part_other, 1).astype(F32)
    else:
        back = back[FIRST_SLOT : FIRST_SLOT + units].astype(F32).reshape(MICRO, local_heads, 3, HEAD_DIM, seg_len)
        grads = []
        for b in range(MICRO):
            query = rotate_back(back[b, :, 0], cosines[b], sines[b])
            key = rotate_back(back[b, :, 1], cosines[b], sines[b])
            grads.append(
                jnp.concatenate([query, key, back[b, :, 2]], axis=0).reshape(3 * head_width, seg_len).astype(BF16)
            )
        stack = jnp.stack(grads)
        term_qkv = sum(dot(inputs[b], grads[b], ((0,), (1,))) for b in range(MICRO)).astype(BF16)
        shard_qkv = lax.psum_scatter(term_qkv, "dp", scatter_dimension=0, tiled=True).astype(F32)
        part_own = dot(pick(stack, core), full_qkv, ((0,), (1,)))
        part_other = dot(pick(stack, 1 - core), full_qkv, ((0,), (1,)))
        part = part_own + swap(part_other.astype(BF16), 1).astype(F32) + jnp.where(core == chip, grad_resid_one, 0.0)
    part = rounded(part)
    input_mine = part + swap(part.astype(BF16), 2).astype(F32)
    shard_last = shard[:, 3 * hidden_units :]
    gain_terms = shard_last[:, head_width : head_width + 2].T

    def by_micro(own, other, first):
        micro = lax.broadcasted_iota(jnp.int32, (MICRO, *own.shape), 0)
        return jnp.where(micro == jnp.where(first, 0, 1), own[None], other[None])

    half = seg_len // 2
    result_half = swap(pick(result.reshape(2, half, width), core), 2)
    result_other = by_micro(result_half, swap(result_half, 1), core == 0).reshape(seg_len, width)
    return (
        by_micro(result, result_other, first_chip),
        by_micro(input_mine, swap(input_mine, 1), core == 0),
        shard_qkv[:, : head_width],
        shard_qkv[:, head_width : 2 * head_width],
        shard_qkv[:, 2 * head_width :],
        shard_last[:, :head_width].T,
        shard[:, :hidden_units],
        shard[:, hidden_units : 2 * hidden_units],
        shard[:, 2 * hidden_units : 3 * hidden_units].T,
        gain_terms[0],
        gain_terms[1],
    )


def solution(mesh):
    weight, turned = P("dp", "tensor"), P("tensor", "dp")
    rows, gain = P(None, "dp", None), P("dp")
    return jax.shard_map(
        body,
        mesh=mesh,
        in_specs=(
            rows, P(), P(None, "dp"), weight, weight, weight, turned, weight, weight, turned, gain, gain, rows,
        ),
        out_specs=(rows, rows, weight, weight, weight, turned, weight, weight, turned, gain, gain),
        check_vma=False,
    )
```
